32 devices in a mesh: rep: 4 (over y, x), shard: 4 (over z), seq: 2 (over core).
Axes of the slice: x: 2, y: 2, z: 4, core: 2. Of those that a mesh axis runs over, the one named last changes fastest.
Arguments:
- inputs: bfloat16 [16, 1024, 1024], P(('rep', 'shard'), 'seq'), may hold values from -6 to 6
- documents: int32 [16, 1024], P(('rep', 'shard')), may hold values from 0 to 3, never falling along the last dimension, each value on 1 to 512 neighbouring positions
- norm_attn_one: float32 [1024], P(('shard', 'seq')), may hold values from 0.25 to 1.75
- query_one: float32 [1024, 1024], P(('shard', 'seq')), may hold values from -0.1875 to 0.1875
- key_one: float32 [1024, 1024], P(('shard', 'seq')), may hold values from -0.1875 to 0.1875
- value_one: float32 [1024, 1024], P(('shard', 'seq')), may hold values from -0.1875 to 0.1875
- proj_one: float32 [1024, 1024], P(('shard', 'seq')), may hold values from -0.75 to 0.75
- norm_ffn_one: float32 [1024], P(('shard', 'seq')), may hold values from 0.25 to 1.75
- gate_one: float32 [1024, 2816], P(('shard', 'seq')), may hold values from -0.1875 to 0.1875
- upward_one: float32 [1024, 2816], P(('shard', 'seq')), may hold values from -0.1875 to 0.1875
- down_one: float32 [2816, 1024], P(('shard', 'seq')), may hold values from -0.109375 to 0.109375
- norm_attn_two: float32 [1024], P(('shard', 'seq')), may hold values from 0.25 to 1.75
- query_two: float32 [1024, 1024], P(('shard', 'seq')), may hold values from -0.1875 to 0.1875
- key_two: float32 [1024, 1024], P(('shard', 'seq')), may hold values from -0.1875 to 0.1875
- value_two: float32 [1024, 1024], P(('shard', 'seq')), may hold values from -0.1875 to 0.1875
- proj_two: float32 [1024, 1024], P(('shard', 'seq')), may hold values from -0.75 to 0.75
- norm_ffn_two: float32 [1024], P(('shard', 'seq')), may hold values from 0.25 to 1.75
- gate_two: float32 [1024, 2816], P(('shard', 'seq')), may hold values from -0.1875 to 0.1875
- upward_two: float32 [1024, 2816], P(('shard', 'seq')), may hold values from -0.1875 to 0.1875
- down_two: float32 [2816, 1024], P(('shard', 'seq')), may hold values from -0.109375 to 0.109375
- cotangent: bfloat16 [16, 1024, 1024], P(('rep', 'shard'), 'seq'), may hold values from -6 to 6
Outputs:
- outputs: bfloat16 [16, 1024, 1024], P(('rep', 'shard'), 'seq')
- grad_input: float32 [16, 1024, 1024], P(('rep', 'shard'), 'seq')
- grad_norm_attn_one: float32 [1024], P(('shard', 'seq'))
- grad_query_one: float32 [1024, 1024], P(('shard', 'seq'))
- grad_key_one: float32 [1024, 1024], P(('shard', 'seq'))
- grad_value_one: float32 [1024, 1024], P(('shard', 'seq'))
- grad_proj_one: float32 [1024, 1024], P(('shard', 'seq'))
- grad_norm_ffn_one: float32 [1024], P(('shard', 'seq'))
- grad_gate_one: float32 [1024, 2816], P(('shard', 'seq'))
- grad_upward_one: float32 [1024, 2816], P(('shard', 'seq'))
- grad_down_one: float32 [2816, 1024], P(('shard', 'seq'))
- grad_norm_attn_two: float32 [1024], P(('shard', 'seq'))
- grad_query_two: float32 [1024, 1024], P(('shard', 'seq'))
- grad_key_two: float32 [1024, 1024], P(('shard', 'seq'))
- grad_value_two: float32 [1024, 1024], P(('shard', 'seq'))
- grad_proj_two: float32 [1024, 1024], P(('shard', 'seq'))
- grad_norm_ffn_two: float32 [1024], P(('shard', 'seq'))
- grad_gate_two: float32 [1024, 2816], P(('shard', 'seq'))
- grad_upward_two: float32 [1024, 2816], P(('shard', 'seq'))
- grad_down_two: float32 [2816, 1024], P(('shard', 'seq'))
The draws below stay inside these ranges and needn't reach their ends.
Inputs may be any that keep to these rules, and one draw needn't show every extreme that they name: `documents`: ids never fall along a sequence; a document holds 1 to 512 tokens.
All inputs are finite; a program needn't handle non-finite values.
Results may differ from the reference program's by a relative error of at most 0.033.
Values may be sent and summed in bfloat16 or wider, within the bound.
No kernel may reach another device: no remote copies, remote signals or barrier semaphores. Data moves between devices by JAX's collectives and lax.ppermute only.
A program may use at most 200 MiB of HBM per device.

```python
import math
import jax
import jax.numpy as jnp
import numpy as np
from jax import lax

D = 1024
HEADS = 16
HD = 64
FF = 2816
LENGTH = 1024
BLOCK = 256
DOCS = 4
SEQS = 16


def level_of(stream_key, dims, shards, low, high):
    def one(dim, blocks):
        heights = jax.random.uniform(jax.random.fold_in(jax.random.fold_in(stream_key, 6), dim), (blocks,), jnp.float32, low / len(shards), high / len(shards))
        return jnp.repeat(jnp.exp(heights), dims[dim] // blocks).reshape((-1,) + (1,) * (len(dims) - dim - 1))

    factor_of = one(*shards[0])
    for cut in shards[1:]:
        factor_of = factor_of * one(*cut)
    return factor_of


def profile(number_of, total, most, lean):
    loads = [(1 << 20) // math.isqrt(grade ** lean) + 1 for grade in range(2, number_of + 1)]
    spare, counts = total - most - (number_of - 1), [1] * (number_of - 1)
    while spare > 0:
        free = [i for i in range(number_of - 1) if counts[i] < most]
        mass, budget = sum([loads[i] for i in free]), spare
        for i in free:
            more = min(most - counts[i], max(1, budget * loads[i] // mass), spare)
            counts[i] = counts[i] + more
            spare = spare - more
    return np.array([most] + counts)


def ragged_sizes(own_key, amount, total, limit, slope):
    if amount == 2:
        one = jax.random.randint(own_key, (), max(1, total - limit), min(limit, total - 1) + 1)
        return jnp.stack([one, total - one])
    sizes = jnp.asarray(profile(amount, total, limit, slope), jnp.int32)
    couples = (amount - 1) // 2
    source_of, sink = sizes[1:1 + 2 * couples:2], sizes[2:2 + 2 * couples:2]
    room = jnp.minimum(source_of - 1, limit - sink)
    passed = jax.random.randint(jax.random.fold_in(own_key, 1), (couples,), 0, 1 << 20) % (room + 1)
    sizes = sizes.at[1:1 + 2 * couples:2].set(source_of - passed).at[2:2 + 2 * couples:2].set(sink + passed)
    return sizes[jax.random.permutation(jax.random.fold_in(own_key, 2), amount)]


def normal_values(rng, extent, width, bound, cuts=(), kind=jnp.bfloat16):
    values = width * jax.random.normal(rng, extent, jnp.float32)
    if cuts:
        values = values * level_of(rng, extent, cuts, -0.22, 0.18)
    return jnp.clip(values, -bound, bound).astype(kind)


def setup_inputs(seed: int = 0) -> dict:
    key_list = jax.random.split(jax.random.key(seed), 22)
    inputs = normal_values(key_list[0], (SEQS, LENGTH, D), 1.0, 6.0, ((0, 16), (1, 2)))
    documents = jax.vmap(lambda own: jnp.searchsorted(jnp.cumsum(ragged_sizes(own, DOCS, LENGTH, LENGTH // 2, 0)), jnp.arange(LENGTH), side="right"))(jax.random.split(key_list[1], SEQS)).reshape((SEQS, LENGTH)).astype(jnp.int32)
    norm_attn_one = jnp.clip(1.0 + 0.15 * jax.random.normal(key_list[2], (D,), jnp.float32), 0.25, 1.75)
    query_one = normal_values(key_list[3], (D, D), D ** -0.5, 0.1875, ((0, 8),), jnp.float32)
    key_one = normal_values(key_list[4], (D, D), D ** -0.5, 0.1875, ((0, 8),), jnp.float32)
    value_one = normal_values(key_list[5], (D, D), D ** -0.5, 0.1875, ((0, 8),), jnp.float32)
    proj_one = normal_values(key_list[6], (D, D), (D // 16) ** -0.5, 0.75, ((0, 8),), jnp.float32)
    norm_ffn_one = jnp.clip(1.0 + 0.15 * jax.random.normal(key_list[7], (D,), jnp.float32), 0.25, 1.75)
    gate_one = normal_values(key_list[8], (D, FF), D ** -0.5, 0.1875, ((0, 8),), jnp.float32)
    upward_one = normal_values(key_list[9], (D, FF), D ** -0.5, 0.1875, ((0, 8),), jnp.float32)
    down_one = normal_values(key_list[10], (FF, D), FF ** -0.5, 0.109375, ((0, 8),), jnp.float32)
    norm_attn_two = jnp.clip(1.0 + 0.15 * jax.random.normal(key_list[11], (D,), jnp.float32), 0.25, 1.75)
    query_two = normal_values(key_list[12], (D, D), D ** -0.5, 0.1875, ((0, 8),), jnp.float32)
    key_two = normal_values(key_list[13], (D, D), D ** -0.5, 0.1875, ((0, 8),), jnp.float32)
    value_two = normal_values(key_list[14], (D, D), D ** -0.5, 0.1875, ((0, 8),), jnp.float32)
    proj_two = normal_values(key_list[15], (D, D), (D // 16) ** -0.5, 0.75, ((0, 8),), jnp.float32)
    norm_ffn_two = jnp.clip(1.0 + 0.15 * jax.random.normal(key_list[16], (D,), jnp.float32), 0.25, 1.75)
    gate_two = normal_values(key_list[17], (D, FF), D ** -0.5, 0.1875, ((0, 8),), jnp.float32)
    upward_two = normal_values(key_list[18], (D, FF), D ** -0.5, 0.1875, ((0, 8),), jnp.float32)
    down_two = normal_values(key_list[19], (FF, D), FF ** -0.5, 0.109375, ((0, 8),), jnp.float32)
    cotangent = normal_values(key_list[20], (SEQS, LENGTH, D), 1.0, 6.0, ((0, 16), (1, 2)))
    return dict(inputs=inputs, documents=documents, norm_attn_one=norm_attn_one, query_one=query_one, key_one=key_one, value_one=value_one, proj_one=proj_one, norm_ffn_one=norm_ffn_one, gate_one=gate_one, upward_one=upward_one, down_one=down_one, norm_attn_two=norm_attn_two, query_two=query_two, key_two=key_two, value_two=value_two, proj_two=proj_two, norm_ffn_two=norm_ffn_two, gate_two=gate_two, upward_two=upward_two, down_two=down_two, cotangent=cotangent)


@jax.custom_vjp
def low(v):
    return lax.optimization_barrier(v.astype(jnp.bfloat16)).astype(jnp.float32)

@jax.custom_vjp
def low_back(v):
    return v

def low_keep(v):
    return (low(v), None)

def low_pass(kept, grad):
    return (grad,)

def back_keep(v):
    return (v, None)

def back_low(kept, grad):
    return (low(grad),)
low.defvjp(low_keep, low_pass)
low_back.defvjp(back_keep, back_low)
eps_norm = 1e-05
rope_base = 10000.0
mask_fill = -1000000000.0

def rms_norm(values, gain_row):
    return values * lax.rsqrt(lax.optimization_barrier(jnp.mean(values * values, axis=-1, keepdims=True)) + eps_norm) * gain_row

def rotate_pairs(values, cosine_table, sine_table):
    half_size = values.shape[-1] // 2
    first_half = values[..., :half_size]
    second_half = values[..., half_size:]
    return jnp.concatenate([first_half * cosine_table - second_half * sine_table, second_half * cosine_table + first_half * sine_table], axis=-1)

def attend_sequence(packed):
    query_rows, key_rows, value_rows, doc_row = packed
    scores = low_back(jnp.einsum('qhd,khd->hqk', query_rows, key_rows, precision=lax.Precision.HIGHEST)) * HD ** (-0.5)
    blocks = jnp.arange(LENGTH, dtype=jnp.int32) // BLOCK
    allowed = (blocks[None, :] <= blocks[:, None]) & (doc_row[None, :] == doc_row[:, None])
    scores = jnp.where(allowed[None], scores, mask_fill)
    attn_weights = low(jax.nn.softmax(scores, axis=-1))
    return jnp.einsum('hqk,khd->qhd', attn_weights, value_rows, precision=lax.Precision.HIGHEST)

def layer_forward(stream, weights, value_first, documents, cosine_table, sine_table):
    gain_attn, w_query, w_key, w_value, w_proj, gain_ffn, w_gate, w_upward, w_down = [low(weight) for weight in weights]
    seq_count = stream.shape[0]
    flat = stream.reshape(seq_count * LENGTH, D)
    normed = low(rms_norm(flat, gain_attn))
    query_raw = low_back(jnp.dot(normed, w_query, precision=lax.Precision.HIGHEST))
    key_raw = low_back(jnp.dot(normed, w_key, precision=lax.Precision.HIGHEST))
    projected = low_back(jnp.dot(normed, w_value, precision=lax.Precision.HIGHEST))
    query_rows = low(rotate_pairs(query_raw.reshape(seq_count, LENGTH, HEADS, HD), cosine_table, sine_table))
    key_rows = low(rotate_pairs(key_raw.reshape(seq_count, LENGTH, HEADS, HD), cosine_table, sine_table))
    if value_first is None:
        value_mix = low(projected)
    else:
        value_mix = low(0.5 * projected + 0.5 * value_first)
    value_rows = value_mix.reshape(seq_count, LENGTH, HEADS, HD)
    attended = lax.map(jax.checkpoint(attend_sequence), (query_rows, key_rows, value_rows, documents))
    attended = low(low_back(attended.reshape(seq_count * LENGTH, D)))
    middle = flat + low_back(jnp.dot(attended, w_proj, precision=lax.Precision.HIGHEST))
    normed_ffn = low(rms_norm(middle, gain_ffn))
    gate_pre = low_back(jnp.dot(normed_ffn, w_gate, precision=lax.Precision.HIGHEST))
    upward_pre = low_back(jnp.dot(normed_ffn, w_upward, precision=lax.Precision.HIGHEST))
    inner = low(jax.nn.silu(gate_pre) * upward_pre)
    result = middle + low_back(jnp.dot(inner, w_down, precision=lax.Precision.HIGHEST))
    return (result.reshape(seq_count, LENGTH, D), value_mix)

def reference(inputs, documents, norm_attn_one, query_one, key_one, value_one, proj_one, norm_ffn_one, gate_one, upward_one, down_one, norm_attn_two, query_two, key_two, value_two, proj_two, norm_ffn_two, gate_two, upward_two, down_two, cotangent):
    half_size = HD // 2
    frequencies = rope_base ** (-(jnp.arange(half_size, dtype=jnp.float32) * 2.0 / HD))
    angles = jnp.arange(LENGTH, dtype=jnp.float32)[:, None] * frequencies[None, :]
    cosine_table = jnp.cos(angles)[None, :, None, :]
    sine_table = jnp.sin(angles)[None, :, None, :]
    masters_one = (norm_attn_one, query_one, key_one, value_one, proj_one, norm_ffn_one, gate_one, upward_one, down_one)
    masters_two = (norm_attn_two, query_two, key_two, value_two, proj_two, norm_ffn_two, gate_two, upward_two, down_two)

    def forward(weights_one, weights_two, start):
        middle, value_first = layer_forward(start, weights_one, None, documents, cosine_table, sine_table)
        result, unused = layer_forward(middle, weights_two, value_first, documents, cosine_table, sine_table)
        return result
    result, pullback = jax.vjp(forward, masters_one, masters_two, inputs.astype(jnp.float32))
    grads_one, grads_two, grad_start = pullback(cotangent.astype(jnp.float32))
    return (result.astype(jnp.bfloat16), grad_start, grads_one[0], grads_one[1], grads_one[2], grads_one[3], grads_one[4], grads_one[5], grads_one[6], grads_one[7], grads_one[8], grads_two[0], grads_two[1], grads_two[2], grads_two[3], grads_two[4], grads_two[5], grads_two[6], grads_two[7], grads_two[8])
```

```python
import functools
import jax
import jax.numpy as jnp
from jax import lax
from jax.experimental import pallas as pl
from jax.experimental.pallas import tpu as pltpu
from jax.sharding import PartitionSpec as P

HD = 64
BLOCK = 256
LANES = 128
FLAT = 512
eps_norm = 1e-05
rope_base = 10000.0
mask_fill = -1000000000.0


def window(block):
    return max(0, block - 2)


def swap_halves(x):
    lane = lax.broadcasted_iota(jnp.int32, x.shape, 1)
    ahead = pltpu.roll(x, LANES - HD // 2, axis=1)
    behind = pltpu.roll(x, HD // 2, axis=1)
    return jnp.where(lane % HD < HD // 2, ahead, behind)


def fill_bias(bias, docs_column, docs_row, blocks):
    at = 0
    for i in range(blocks):
        first = window(i)
        rows = (i + 1 - first) * BLOCK
        same = (
            docs_column[pl.ds(first * BLOCK, rows), 0:1]
            == docs_row[0:1, pl.ds(i * BLOCK, BLOCK)]
        )
        bias[pl.ds(at, rows), :] = jnp.where(same, 0.0, mask_fill)
        at += rows


def ahead_kernel(blocks, mixed, half_ref, tokens_ref, weight_ref, *rest):
    if mixed:
        first_ref, rest = rest[0], rest[1:]
    cos_ref, sin_ref, column_ref, row_ref, kept_ref, out_ref, lse_ref, bias = rest
    spin = half_ref[0] * (blocks // 2)

    @pl.when(pl.program_id(0) == 0)
    def _():
        fill_bias(bias, column_ref, row_ref, blocks)

    def place(b):
        return pl.multiple_of(lax.rem(b + spin, blocks) * BLOCK, BLOCK)

    for b in range(blocks):
        rows = pl.ds(b * BLOCK, BLOCK)
        cosine, sine = cos_ref[rows, :], sin_ref[rows, :]
        raw = jnp.dot(
            tokens_ref[pl.ds(place(b), BLOCK), :], weight_ref[...], preferred_element_type=jnp.float32
        )
        for part in range(2):
            one = raw[:, part * LANES : (part + 1) * LANES]
            turned = one * cosine + swap_halves(one) * sine
            kept_ref[rows, part * LANES : (part + 1) * LANES] = turned.astype(jnp.bfloat16)
        value = raw[:, 2 * LANES :]
        if mixed:
            value = 0.5 * value + 0.5 * first_ref[rows, 2 * LANES :].astype(jnp.float32)
        kept_ref[rows, 2 * LANES :] = value.astype(jnp.bfloat16)

    value_turned = kept_ref[:, 2 * LANES :].T
    head_lane = lax.broadcasted_iota(jnp.int32, (BLOCK, LANES), 1) // HD
    at = 0
    for i in range(blocks):
        first = window(i)
        count = (i + 1 - first) * BLOCK
        rows = pl.ds(i * BLOCK, BLOCK)
        query = kept_ref[rows, 0:LANES] * jnp.bfloat16(HD**-0.5)
        keys = kept_ref[pl.ds(first * BLOCK, count), LANES : 2 * LANES]
        fill = bias[pl.ds(at, count), :]
        at += count
        outs = []
        for head in range(LANES // HD):
            one = jnp.where(head_lane == head, query, jnp.bfloat16(0))
            scores = (
                lax.dot_general(keys, one, (((1,), (1,)), ((), ())), preferred_element_type=jnp.float32)
                + fill
            )
            top = jnp.max(scores, axis=0, keepdims=True)
            powers = jnp.exp(scores - top)
            total = jnp.sum(powers, axis=0, keepdims=True)
            weights = (powers * (1.0 / total)).astype(jnp.bfloat16)
            outs.append(
                jnp.dot(
                    value_turned[head * HD : (head + 1) * HD, first * BLOCK : first * BLOCK + count],
                    weights,
                    preferred_element_type=jnp.float32,
                )
            )
            lse_ref[0, head : head + 1, rows] = top + jnp.log(total)
        merged = jnp.concatenate(outs, axis=0)
        out_ref[pl.ds(place(i), BLOCK), :] = merged.T.astype(jnp.bfloat16)


def back_kernel(blocks, mixed, half_ref, kept_ref, grad_ref, lse_ref, *rest):
    if not mixed:
        extra_ref, rest = rest[0], rest[1:]
    cos_ref, sin_ref, column_ref, row_ref, out_ref, *rest = rest
    if mixed:
        passed_ref, rest = rest[0], rest[1:]
    bias, key_sum, value_sum = rest
    spin = half_ref[0] * (blocks // 2)

    @pl.when(pl.program_id(0) == 0)
    def _():
        fill_bias(bias, column_ref, row_ref, blocks)

    def place(b):
        return pl.multiple_of(lax.rem(b + spin, blocks) * BLOCK, BLOCK)

    def unrotate(x, rows):
        return x * cos_ref[rows, :] - swap_halves(x) * sin_ref[rows, :]

    keys_turned = kept_ref[:, LANES : 2 * LANES].T
    head_lane = lax.broadcasted_iota(jnp.int32, (BLOCK, LANES), 1) // HD
    at = 0
    for i in range(blocks):
        first = window(i)
        count = (i + 1 - first) * BLOCK
        rows = pl.ds(i * BLOCK, BLOCK)
        span = pl.ds(first * BLOCK, count)
        query = kept_ref[rows, 0:LANES] * jnp.bfloat16(HD**-0.5)
        grad = grad_ref[pl.ds(place(i), BLOCK), :]
        keys = kept_ref[span, LANES : 2 * LANES]
        values = kept_ref[span, 2 * LANES :]
        fill = bias[pl.ds(at, count), :]
        at += count
        outs = []
        key_add, value_add = [], []
        for head in range(LANES // HD):
            pick = head_lane == head
            one = jnp.where(pick, query, jnp.bfloat16(0))
            grad_one = jnp.where(pick, grad, jnp.bfloat16(0))
            scores = (
                lax.dot_general(keys, one, (((1,), (1,)), ((), ())), preferred_element_type=jnp.float32)
                + fill
            )
            weights = jnp.exp(scores - lse_ref[0, head : head + 1, rows])
            grad_weights = lax.dot_general(
                values, grad_one, (((1,), (1,)), ((), ())), preferred_element_type=jnp.float32
            )
            delta = jnp.sum(weights * grad_weights, axis=0, keepdims=True)
            grad_scores = (weights * (grad_weights - delta)).astype(jnp.bfloat16)
            value_add.append(
                jnp.dot(weights.astype(jnp.bfloat16), grad_one, preferred_element_type=jnp.float32)
            )
            key_add.append(jnp.dot(grad_scores, one, preferred_element_type=jnp.float32))
            outs.append(
                jnp.dot(
                    keys_turned[head * HD : (head + 1) * HD, first * BLOCK : first * BLOCK + count],
                    grad_scores,
                    preferred_element_type=jnp.float32,
                )
            )
        key_add, value_add = sum(key_add[1:], key_add[0]), sum(value_add[1:], value_add[0])
        old = count - BLOCK
        if old:
            key_sum[pl.ds(first * BLOCK, old), :] += key_add[:old]
            value_sum[pl.ds(first * BLOCK, old), :] += value_add[:old]
        key_sum[rows, :] = key_add[old:]
        value_sum[rows, :] = value_add[old:]
        grad_query = jnp.concatenate(outs, axis=0).T * HD**-0.5
        out_ref[pl.ds(place(i), BLOCK), 0:LANES] = unrotate(grad_query, rows).astype(jnp.bfloat16)
    for b in range(blocks):
        rows = pl.ds(b * BLOCK, BLOCK)
        there = pl.ds(place(b), BLOCK)
        out_ref[there, LANES : 2 * LANES] = unrotate(key_sum[rows, :], rows).astype(jnp.bfloat16)
        value_grad = value_sum[rows, :]
        if mixed:
            value_grad = 0.5 * value_grad
            passed_ref[rows, :] = value_grad
        else:
            value_grad = value_grad + extra_ref[rows, :]
        out_ref[there, 2 * LANES :] = value_grad.astype(jnp.bfloat16)


def bias_rows(blocks):
    return sum(i + 1 - window(i) for i in range(blocks)) * BLOCK


def whole(shape):
    return pl.BlockSpec(shape, lambda h, s: (0,) * len(shape))


def attend_ahead(tokens, weight, first_kept, tables, half):
    cosine, sine, column, row = tables
    length, width = tokens.shape[0], weight.shape[1]
    pairs, blocks = width // (3 * LANES), length // BLOCK
    mixed = first_kept is not None
    wide = pl.BlockSpec((length, 3 * LANES), lambda h, s: (0, h))
    slim = pl.BlockSpec((length, LANES), lambda h, s: (0, h))
    return pl.pallas_call(
        functools.partial(ahead_kernel, blocks, mixed),
        out_shape=(
            jax.ShapeDtypeStruct((length, width), jnp.bfloat16),
            jax.ShapeDtypeStruct((length, pairs * LANES), jnp.bfloat16),
            jax.ShapeDtypeStruct((pairs, LANES // HD, length), jnp.float32),
        ),
        grid_spec=pltpu.PrefetchScalarGridSpec(
            num_scalar_prefetch=1,
            grid=(pairs,),
            in_specs=[whole(tokens.shape), pl.BlockSpec((weight.shape[0], 3 * LANES), lambda h, s: (0, h))]
            + ([wide] if mixed else [])
            + [whole(cosine.shape), whole(sine.shape), whole(column.shape), whole(row.shape)],
            out_specs=(wide, slim, pl.BlockSpec((1, LANES // HD, length), lambda h, s: (h, 0, 0))),
            scratch_shapes=[pltpu.VMEM((bias_rows(blocks), BLOCK), jnp.float32)],
        ),
        compiler_params=pltpu.CompilerParams(dimension_semantics=("arbitrary",), vmem_limit_bytes=48 << 20),
        cost_estimate=pl.CostEstimate(flops=0, transcendentals=0, bytes_accessed=0),
        name="attend_ahead",
    )(half, tokens, weight, *((first_kept,) if mixed else ()), cosine, sine, column, row)


def attend_back(kept, grad, lse, extra, tables, half):
    cosine, sine, column, row = tables
    length, width = kept.shape
    pairs, blocks = width // (3 * LANES), length // BLOCK
    mixed = extra is None
    wide = pl.BlockSpec((length, 3 * LANES), lambda h, s: (0, h))
    slim = pl.BlockSpec((length, LANES), lambda h, s: (0, h))
    outs = [jax.ShapeDtypeStruct((length, width), jnp.bfloat16)]
    out_specs = [wide]
    if mixed:
        outs.append(jax.ShapeDtypeStruct((length, pairs * LANES), jnp.float32))
        out_specs.append(slim)
    result = pl.pallas_call(
        functools.partial(back_kernel, blocks, mixed),
        out_shape=tuple(outs),
        grid_spec=pltpu.PrefetchScalarGridSpec(
            num_scalar_prefetch=1,
            grid=(pairs,),
            in_specs=[wide, slim, pl.BlockSpec((1, LANES // HD, length), lambda h, s: (h, 0, 0))]
            + ([] if mixed else [slim])
            + [whole(cosine.shape), whole(sine.shape), whole(column.shape), whole(row.shape)],
            out_specs=tuple(out_specs),
            scratch_shapes=[
                pltpu.VMEM((bias_rows(blocks), BLOCK), jnp.float32),
                pltpu.VMEM((length, LANES), jnp.float32),
                pltpu.VMEM((length, LANES), jnp.float32),
            ],
        ),
        compiler_params=pltpu.CompilerParams(dimension_semantics=("arbitrary",), vmem_limit_bytes=48 << 20),
        cost_estimate=pl.CostEstimate(flops=0, transcendentals=0, bytes_accessed=0),
        name="attend_back",
    )(half, kept, grad, lse, *(() if mixed else (extra,)), cosine, sine, column, row)
    return result if mixed else (result[0], None)


def swap_cores(x):
    return lax.ppermute(x, "seq", [(0, 1), (1, 0)])


def exchange(x, mask):
    count = lax.axis_size("rep")
    return lax.ppermute(x, "rep", [(i, i ^ mask) for i in range(count)])


def unflat(read, rows, columns, write):
    at = 0
    for i in range(columns // FLAT):
        write(0, i * FLAT, read(at, rows, 0, FLAT))
        at += rows
    left = columns % FLAT
    if left:
        step = rows * left // FLAT
        for i in range(FLAT // left):
            write(i * step, columns - left, read(at, step, i * left, left))
        at += step
    return at


def join_kernel(masks, parts, cores, slot_ref, *refs):
    pieces, outs = refs[: len(masks)], refs[-sum(len(w) if k == "columns" else 1 for k, _, w in parts) :]
    for mask, piece in zip(masks, pieces):
        slot = lax.bitwise_xor(slot_ref[0], mask)
        base, at = 0, 0
        for kind, rows, widths in parts:
            columns = sum(widths)

            def read(row, count, column, width, base=base):
                return piece[0, base + row : base + row + count, column : column + width]

            def write(row, column, values, kind=kind, rows=rows, widths=widths, at=at):
                if kind == "columns":
                    one = rows // cores
                    left, which = column, 0
                    while left >= widths[which]:
                        left, which = left - widths[which], which + 1
                    took, offset = 0, column
                    while took < values.shape[1]:
                        size = min(widths[which] - left, values.shape[1] - took)
                        count = values.shape[0]
                        for done in range(0, count, min(one, count)):
                            core, inside = divmod(row + done, one)
                            size_rows = min(one, count)
                            outs[at + which][0, core, slot, inside : inside + size_rows, left : left + size] = (
                                values[done : done + size_rows, took : took + size]
                            )
                        took, left, which = took + size, 0, which + 1
                else:
                    there = pl.ds(pl.multiple_of(slot * columns, columns) + column, values.shape[1])
                    outs[at][0, row : row + values.shape[0], there] = values

            base += unflat(read, rows, columns, write)
            at += len(widths) if kind == "columns" else 1


def join(pieces, masks, slot, sizes, parts, start=None, after=()):
    groups, cores = sizes
    count, rows = len(masks), pieces[0].shape[0] // groups
    read = rows if start is None else sum(h * sum(w) for _, h, w in parts) // FLAT
    at = 0 if start is None else start // read
    shapes = []
    for kind, height, widths in parts:
        if kind == "columns":
            shapes += [(groups, cores, count, height // cores, w) for w in widths]
        else:
            shapes.append((groups, height, count * widths[0]))
    outs = pl.pallas_call(
        functools.partial(join_kernel, masks, parts, cores),
        out_shape=[jax.ShapeDtypeStruct(s, jnp.bfloat16) for s in shapes],
        grid_spec=pltpu.PrefetchScalarGridSpec(
            num_scalar_prefetch=1,
            grid=(groups,),
            in_specs=[pl.BlockSpec((1, read, FLAT), lambda g, s: (g, at, 0))] * count
            + [pl.BlockSpec(memory_space=pl.ANY)] * len(after),
            out_specs=[
                pl.BlockSpec((1, *s[1:]), lambda g, t, n=len(s): (g,) + (0,) * (n - 1)) for s in shapes
            ],
        ),
        cost_estimate=pl.CostEstimate(flops=0, transcendentals=0, bytes_accessed=0),
        name="join",
    )(slot, *[p.reshape(groups, rows, FLAT) for p in pieces], *after)
    return [o.reshape(-1, o.shape[-1]) for o in outs]


def core_columns(rows, sizes, core):
    shards, cores = sizes
    width = rows.shape[1] // (shards * cores)
    even, odd = (
        jnp.concatenate(
            [rows[:, (s * cores + c) * width : (s * cores + c + 1) * width] for s in range(shards)],
            axis=1,
        )
        for c in range(cores)
    )
    return jnp.where(core == 0, even, odd), jnp.where(core == 0, odd, even)


def head_major(parts):
    pairs = parts[0].shape[1] // LANES
    return jnp.concatenate(
        [p[:, i * LANES : (i + 1) * LANES] for i in range(pairs) for p in parts], axis=1
    )


def head_minor(joined):
    pairs = joined.shape[1] // (3 * LANES)
    return [
        jnp.concatenate(
            [
                joined[:, (3 * i + j) * LANES : (3 * i + j + 1) * LANES]
                for i in range(pairs)
            ],
            axis=1,
        )
        for j in range(3)
    ]


def chip_rows(rows_of, sizes, core):
    mine, theirs = rows_of
    other = swap_cores(theirs)
    return jnp.concatenate(
        [jnp.where(core == 0, mine, other), jnp.where(core == 0, other, mine)], axis=0
    )


def gather_shard(x):
    return lax.all_gather(x, "shard", axis=0, tiled=True)


def column_parts(weights, sizes, core, interleave):
    mine, theirs = zip(*[core_columns(w.astype(jnp.bfloat16), sizes, core) for w in weights])
    if interleave:
        return head_major(mine), head_major(theirs)
    return jnp.concatenate(mine, axis=1), jnp.concatenate(theirs, axis=1)


def gather_plain(masters, sizes, core):
    _, w_query, w_key, w_value, w_proj, _, w_gate, w_upward, w_down = masters
    w_qkv = gather_shard(chip_rows(column_parts((w_query, w_key, w_value), sizes, core, True), sizes, core))
    w_wide = gather_shard(chip_rows(column_parts((w_gate, w_upward), sizes, core, False), sizes, core))
    w_proj, w_down = (gather_shard(w.astype(jnp.bfloat16)) for w in (w_proj, w_down))
    width = w_wide.shape[1] // 2
    return w_qkv, w_proj, w_wide[:, :width], w_wide[:, width:], w_down


def call(kernel, outs, grid, in_specs, out_specs, name, scratch=(), scalars=1):
    return pl.pallas_call(
        kernel,
        out_shape=outs,
        grid_spec=pltpu.PrefetchScalarGridSpec(
            num_scalar_prefetch=scalars,
            grid=grid,
            in_specs=in_specs,
            out_specs=out_specs,
            scratch_shapes=scratch,
        ),
        compiler_params=pltpu.CompilerParams(
            dimension_semantics=("arbitrary",) * len(grid), vmem_limit_bytes=56 << 20
        ),
        cost_estimate=pl.CostEstimate(flops=0, transcendentals=0, bytes_accessed=0),
        name=name,
    )


def fixed(shape):
    return pl.BlockSpec(shape, lambda *ids: (0,) * len(shape))


def low(values):
    return values.astype(jnp.bfloat16)


def near_split_kernel(shards, place_ref, *refs):
    weights, gains, (mine, theirs) = refs[:3], refs[3:-2], refs[-2:]
    core = place_ref[1]
    for out, which in ((mine, core), (theirs, 1 - core)):
        for s in range(shards):
            there = pl.ds(pl.multiple_of((2 * s + which) * LANES, LANES), LANES)
            for j, weight in enumerate(weights):
                out[:, (3 * s + j) * LANES : (3 * s + j + 1) * LANES] = low(weight[:, there])
        if gains:
            rows = jnp.concatenate([g[...] for g in gains] + [jnp.zeros((16 - len(gains), LANES), jnp.float32)], axis=0)
            out[0:16, 3 * shards * LANES :] = low(rows)


def near_merge_kernel(place_ref, mine, theirs, proj, out):
    core = place_ref[1]
    rows = mine.shape[0]
    for j in range(3):
        for part, which in ((mine, core), (theirs, 1 - core)):
            there = pl.ds(pl.multiple_of((2 * j + which) * rows, rows), rows)
            out[there, :] = part[:, j * FLAT : (j + 1) * FLAT]
    half = proj.shape[0] // 2
    start = 6 * rows
    out[start : start + half, 0 : FLAT // 2] = low(proj[0:half, :])
    out[start : start + half, FLAT // 2 :] = low(proj[half:, :])
    if out.shape[0] > start + half:
        out[start + half :, :] = jnp.zeros((16, FLAT), jnp.bfloat16)
        for part, which in ((mine, core), (theirs, 1 - core)):
            there = pl.ds(pl.multiple_of(which * LANES, LANES), LANES)
            out[start + half :, there] = part[0:16, 3 * FLAT : 3 * FLAT + LANES]


def far_split_kernel(shards, place_ref, gate, upward, mine, theirs):
    core = place_ref[1]
    width = gate.shape[1] // (2 * shards)
    for at, weight in enumerate((gate, upward)):
        even, odd = (
            low(jnp.concatenate([weight[:, (2 * s + c) * width : (2 * s + c + 1) * width] for s in range(shards)], axis=1))
            for c in range(2)
        )
        there = slice(at * shards * width, (at + 1) * shards * width)
        mine[:, there] = jnp.where(core == 0, even, odd)
        theirs[:, there] = jnp.where(core == 0, odd, even)


def far_merge_kernel(place_ref, mine, theirs, down, out):
    core = place_ref[1]
    rows, columns = mine.shape
    blocks = columns // FLAT
    for part, which in ((mine, core), (theirs, 1 - core)):
        for j in range(blocks):
            there = pl.ds(pl.multiple_of((2 * j + which) * rows, rows), rows)
            out[there, :] = part[:, j * FLAT : (j + 1) * FLAT]
        there = pl.ds(pl.multiple_of(which * (FLAT // 2), FLAT // 2), FLAT // 2)
        out[2 * blocks * rows : (2 * blocks + 1) * rows, there] = part[:, blocks * FLAT :]
    half, start = down.shape[0] // 2, (2 * blocks + 1) * rows
    out[start:, 0 : FLAT // 2] = low(down[0:half, :])
    out[start:, FLAT // 2 :] = low(down[half:, :])


def shape_of(*shape, dtype=jnp.bfloat16):
    return jax.ShapeDtypeStruct(shape, dtype)


def quarter_of_rows(weight):
    return pl.BlockSpec((weight.shape[0] // 4, weight.shape[1]), lambda i, s: (s[0], 0))


def quarter_of_columns(weight):
    return pl.BlockSpec((weight.shape[0], weight.shape[1] // 4), lambda i, s: (0, s[0]))


def gather_near(weights, proj, gains, shards, place):
    rows = weights[0].shape[0] // 4
    width = 3 * shards * LANES + (LANES if gains else 0)
    gains = [g.reshape(1, LANES) for g in gains]
    mine, theirs = call(
        functools.partial(near_split_kernel, shards),
        [shape_of(rows, width)] * 2,
        (1,),
        [quarter_of_rows(w) for w in weights] + [fixed((1, LANES))] * len(gains),
        [fixed((rows, width))] * 2,
        "near_split",
    )(place, *weights, *gains)
    total = 6 * rows + proj.shape[0] // 2 + (16 if gains else 0)
    merged = call(
        near_merge_kernel,
        shape_of(total, FLAT),
        (1,),
        [fixed((rows, width))] * 2 + [quarter_of_columns(proj)],
        fixed((total, FLAT)),
        "near_merge",
    )(place, mine, swap_cores(theirs), proj)
    return gather_shard(merged)


def gather_far(weights, down, shards, place):
    rows, width = weights[0].shape[0] // 4, weights[0].shape[1]
    mine, theirs = call(
        functools.partial(far_split_kernel, shards),
        [shape_of(rows, width)] * 2,
        (1,),
        [quarter_of_rows(w) for w in weights],
        [fixed((rows, width))] * 2,
        "far_split",
    )(place, *weights)
    total = rows * width // (FLAT // 2) + down.shape[0] // 2
    merged = call(
        far_merge_kernel,
        shape_of(total, FLAT),
        (1,),
        [fixed((rows, width))] * 2 + [quarter_of_columns(down)],
        fixed((total, FLAT)),
        "far_merge",
    )(place, mine, swap_cores(theirs), down)
    return gather_shard(merged)


def gated_kernel(none_ref, tokens, gate, upward, gate_out, upward_out, inner_out):
    one = jnp.dot(tokens[...], gate[...], preferred_element_type=jnp.float32)
    two = jnp.dot(tokens[...], upward[...], preferred_element_type=jnp.float32)
    inner_out[...] = low(one * jax.nn.sigmoid(one) * two)
    gate_out[...] = low(one)
    upward_out[...] = low(two)


def gated(tokens, gate, upward, place):
    length, width, tile = tokens.shape[0], gate.shape[1], 256
    rows = pl.BlockSpec((tile, width), lambda i, s: (i, 0))
    return call(
        gated_kernel,
        [shape_of(length, width)] * 3,
        (length // tile,),
        [pl.BlockSpec((tile, tokens.shape[1]), lambda i, s: (i, 0)), fixed(gate.shape), fixed(upward.shape)],
        [rows] * 3,
        "gated",
    )(place, tokens, gate, upward)


def bit_of(rep, mask):
    return (rep // mask) % 2


def halve_rows(grad, groups, bit, mask):
    shaped = grad.reshape(groups, 2, -1, grad.shape[1])
    sent = lax.dynamic_index_in_dim(shaped, 1 - bit, 1, keepdims=False)
    kept = lax.dynamic_index_in_dim(shaped, bit, 1, keepdims=False)
    got = exchange(sent, mask)
    total = kept.astype(jnp.float32) + got.astype(jnp.float32)
    return total.astype(jnp.bfloat16).reshape(-1, grad.shape[1])


def halve_columns(grad, bit, mask):
    width = grad.shape[1] // 2
    sent = lax.dynamic_slice_in_dim(grad, (1 - bit) * width, width, 1)
    kept = lax.dynamic_slice_in_dim(grad, bit * width, width, 1)
    got = exchange(sent, mask)
    return (kept.astype(jnp.float32) + got.astype(jnp.float32)).astype(jnp.bfloat16)


def scatter_shard(x):
    return lax.psum_scatter(x, "shard", scatter_dimension=0, tiled=True)


def columns_back(grad, sizes, rep, plan):
    if plan is None:
        return lax.psum(scatter_shard(grad), "rep")
    first, second = plan
    groups = sizes[0] * sizes[1]
    half = halve_rows(grad, groups, bit_of(rep, first), first)
    return scatter_shard(halve_rows(half, groups, bit_of(rep, second), second))


def rows_back(grad, rep, plan):
    if plan is None:
        return lax.psum(scatter_shard(grad), "rep")
    first, second = plan
    half = halve_columns(grad, bit_of(rep, first), first)
    return scatter_shard(halve_columns(half, bit_of(rep, second), second))


def in_order(pieces, slot_high, slot_low):
    p0, p1, p2, p3 = pieces
    low = slot_low == 1
    q0, q1 = jnp.where(low, p1, p0), jnp.where(low, p0, p1)
    q2, q3 = jnp.where(low, p3, p2), jnp.where(low, p2, p3)
    high = slot_high == 1
    return [
        jnp.where(high, q2, q0),
        jnp.where(high, q3, q1),
        jnp.where(high, q0, q2),
        jnp.where(high, q1, q3),
    ]


def share_slots(piece, plan):
    first, second = plan
    return [piece, exchange(piece, second), exchange(piece, first), exchange(piece, first ^ second)]


def spread_columns(even, odd, sizes):
    shards, cores = sizes
    width = even.shape[1] // shards
    return jnp.concatenate(
        [p[:, s * width : (s + 1) * width] for s in range(shards) for p in (even, odd)], axis=1
    )


def finish_columns(reduced, sizes, core, rep, plan):
    rows = reduced.shape[0] // 2
    shaped = reduced.reshape(2, rows, reduced.shape[1])
    mine = lax.dynamic_index_in_dim(shaped, core, 0, keepdims=False)
    other = swap_cores(lax.dynamic_index_in_dim(shaped, 1 - core, 0, keepdims=False))
    even, odd = jnp.where(core == 0, mine, other), jnp.where(core == 0, other, mine)
    if plan is None:
        return even.astype(jnp.float32), odd.astype(jnp.float32)
    both = jnp.concatenate([even, odd], axis=1)
    first, second = plan
    ordered = in_order(share_slots(both, plan), bit_of(rep, first), bit_of(rep, second))
    full = jnp.concatenate(ordered, axis=0).astype(jnp.float32)
    return full[:, : even.shape[1]], full[:, even.shape[1] :]


def finish_rows(reduced, rep, plan):
    if plan is None:
        return reduced.astype(jnp.float32)
    first, second = plan
    ordered = in_order(share_slots(reduced, plan), bit_of(rep, first), bit_of(rep, second))
    return jnp.concatenate(ordered, axis=1).astype(jnp.float32)


def norm_ahead(values, gain_row):
    factor = lax.rsqrt(jnp.mean(values * values, axis=-1, keepdims=True) + eps_norm)
    return ((values * factor * gain_row).astype(jnp.bfloat16), factor)


def norm_back(values, factor, gain_row, upstream):
    scaled = upstream * gain_row
    gain_grad = jnp.sum(upstream * values * factor, axis=0)
    inner_mean = jnp.mean(scaled * values, axis=-1, keepdims=True)
    return (factor * scaled - values * (factor * factor * factor) * inner_mean, gain_grad)


def both_halves(mine):
    return jnp.concatenate([mine, swap_cores(mine)], axis=0)


def dot(a, b):
    return jnp.dot(a, b, preferred_element_type=jnp.float32)


def dot_nt(a, b):
    return lax.dot_general(a, b, (((1,), (1,)), ((), ())), preferred_element_type=jnp.float32)


def dot_tn(a, b):
    return lax.dot_general(a, b, (((0,), (0,)), ((), ())), preferred_element_type=jnp.float32)


def sum_halves(product, rows):
    theirs = swap_cores(product(slice(rows, 2 * rows)).astype(jnp.bfloat16))
    return product(slice(0, rows)) + theirs.astype(jnp.float32)


def tie(value, *others):
    return lax.optimization_barrier((value, *others))[0]


def layer_ahead(flat, gains, weights, first_kept, tables, place):
    gain_attn, gain_ffn = gains
    rows = flat.shape[0]
    normed, factor_attn = norm_ahead(flat, gain_attn)
    normed_all = both_halves(normed)
    w_qkv, w_proj = weights.near()
    kept, attended, lse = attend_ahead(normed_all, w_qkv, first_kept, tables, place[1:])
    attended = weights.after_attention(attended)
    theirs = dot(attended[rows:], w_proj).astype(jnp.bfloat16)
    middle = flat + dot(attended[:rows], w_proj) + swap_cores(theirs).astype(jnp.float32)
    normed_ffn, factor_ffn = norm_ahead(middle, gain_ffn)
    ffn_all = both_halves(normed_ffn)
    w_gate, w_upward = weights.wide()
    ffn_all = weights.before_wide(ffn_all)
    gate_pre, upward_pre, inner = gated(ffn_all, w_gate, w_upward, place)
    inner = weights.after_wide(inner)
    (w_down,) = weights.down(inner)
    theirs = dot(inner[rows:], w_down).astype(jnp.bfloat16)
    result = middle + dot(inner[:rows], w_down) + swap_cores(theirs).astype(jnp.float32)
    result = weights.at_end(result)
    saved = (
        flat,
        factor_attn,
        normed_all,
        kept,
        lse,
        attended,
        middle,
        factor_ffn,
        ffn_all,
        gate_pre,
        upward_pre,
        inner,
    )
    return result, kept, saved, (w_qkv, w_proj, w_gate, w_upward, w_down)


class Plain:
    def __init__(self, weights):
        self.weights = weights

    def near(self):
        return self.weights[:2]

    def wide(self):
        return self.weights[2:4]

    def down(self, inner):
        return self.weights[4:]

    def same(self, value):
        return value

    after_attention = before_wide = after_wide = at_end = same


class Quarters:
    def __init__(self, place, piece, first, second, before_first=(), before_second=()):
        self.slot, self.starts = place[:1], {}
        self.masks = (0, first, second, first ^ second)
        self.one = exchange(tie(piece, *before_first), first)
        self.two = exchange(tie(piece, *before_second), second)
        self.three = exchange(tie(self.one, *before_second), second)
        self.pieces = [piece, self.one, self.two, self.three]


class Tuned(Plain):
    def __init__(self, shapes, sizes, place):
        (qkv_rows, qkv_width), proj_rows, (wide_rows, wide_width), down_rows = shapes
        self.cut, self.shards = wide_rows * wide_width // FLAT, sizes[0]
        self.near_parts = (("columns", qkv_rows, (qkv_width,)), ("rows", proj_rows, (FLAT // 2,)))
        self.wide_parts = (("columns", wide_rows, (wide_width // 2,) * 2),)
        self.down_parts = (("rows", down_rows, (FLAT // 2,)),)
        self.join = lambda q, parts, after=(): join(
            q.pieces, q.masks, q.slot, sizes, parts, q.starts.get(parts[0][0]), after
        )

    def split(self, far):
        far = far.reshape(self.shards, -1, FLAT)
        return (f.reshape(-1, FLAT) for f in (far[:, : self.cut], far[:, self.cut :]))

    def near(self):
        return self.join(self.near_way, self.near_parts)

    def wide(self):
        return self.join(self.wide_way, self.wide_parts)

    def down(self, inner):
        return self.join(self.down_way, self.down_parts, (inner,))


class Halves:
    def __init__(self, place, pieces, before):
        self.slot, self.starts = 2 * half_of(place[:1]), {}
        self.masks = (0, 1, 2, 3)
        self.one, self.two = exchange(tie(pieces[0], *before), 1), exchange(pieces[1], 2)
        self.pieces = [*pieces, self.one, self.two]


def half_of(rep):
    return lax.bitwise_xor(rep, rep // 2) % 2


def first_ways(layer, near, far, place):
    near = Quarters(place, near, 1, 2)
    wide, down = layer.split(tie(far, near.one, near.two, near.three))
    return near, Quarters(place, wide, 2, 1), Quarters(place, down, 1, 2)


def second_ways(layer, near, far, wide_one, down_one, place):
    near = Quarters(place, near, 2, 1, (down_one.two,), (wide_one.one,))
    wide, down = zip(*[layer.split(f) for f in far])
    wide = Halves(place, wide, (near.two, near.three))
    return near, wide, Halves(place, down, (near.two, near.three))


def layer_back(upstream, gains, weights, saved, extra, tables, half, send):
    gain_attn, gain_ffn = gains
    w_qkv, w_proj, w_gate, w_upward, w_down = weights
    (
        flat,
        factor_attn,
        normed_all,
        kept,
        lse,
        attended,
        middle,
        factor_ffn,
        ffn_all,
        gate_pre,
        upward_pre,
        inner,
    ) = saved
    rows = flat.shape[0]
    grad_down_all = both_halves(upstream.astype(jnp.bfloat16))
    grad_inner = dot_nt(grad_down_all, w_down)
    gate_pre, upward_pre = gate_pre.astype(jnp.float32), upward_pre.astype(jnp.float32)
    sigmoid_gate = jax.nn.sigmoid(gate_pre)
    grad_gate = (
        grad_inner * upward_pre * sigmoid_gate * (1.0 + gate_pre * (1.0 - sigmoid_gate))
    ).astype(jnp.bfloat16)
    grad_upward = (grad_inner * gate_pre * sigmoid_gate).astype(jnp.bfloat16)
    sent_down = send.down(dot_tn(inner, grad_down_all).astype(jnp.bfloat16))
    sent_gate = send.gate(
        jnp.concatenate(
            [
                dot_tn(ffn_all, grad_gate).astype(jnp.bfloat16),
                dot_tn(ffn_all, grad_upward).astype(jnp.bfloat16),
            ],
            axis=1,
        )
    )
    grad_normed_ffn = sum_halves(
        lambda part: dot_nt(grad_gate[part], w_gate) + dot_nt(grad_upward[part], w_upward), rows
    )
    grad_part_ffn, grad_gain_ffn = norm_back(middle, factor_ffn, gain_ffn, grad_normed_ffn)
    grad_middle = upstream + grad_part_ffn
    grad_branch_all = both_halves(grad_middle.astype(jnp.bfloat16))
    grad_attended = dot_nt(grad_branch_all, w_proj).astype(jnp.bfloat16)
    sent_proj = send.proj(dot_tn(attended, grad_branch_all).astype(jnp.bfloat16))
    grad_qkv, passed = attend_back(kept, grad_attended, lse, extra, tables, half)
    sent_qkv = send.qkv(dot_tn(normed_all, grad_qkv).astype(jnp.bfloat16))
    grad_normed = sum_halves(lambda part: dot_nt(grad_qkv[part], w_qkv), rows)
    grad_part_attn, grad_gain_attn = norm_back(flat, factor_attn, gain_attn, grad_normed)
    grad_flat = grad_middle + grad_part_attn
    grads = send.finish(sent_qkv, sent_proj, sent_gate, sent_down)
    return grad_flat, (grad_gain_attn, grad_gain_ffn), grads, passed


class Sender:
    def __init__(self, sizes, core, rep, tuned):
        self.sizes, self.core, self.rep = sizes, core, rep
        self.near = (1, 2) if tuned else None
        self.far = (2, 1) if tuned else None

    def down(self, grad):
        return rows_back(grad, self.rep, self.near)

    def proj(self, grad):
        return rows_back(grad, self.rep, self.near)

    def gate(self, grad):
        return columns_back(grad, self.sizes, self.rep, self.far)

    def qkv(self, grad):
        return columns_back(grad, self.sizes, self.rep, self.near)

    def finish(self, qkv, proj, gate, down):
        q_even, q_odd = finish_columns(qkv, self.sizes, self.core, self.rep, self.near)
        g_even, g_odd = finish_columns(gate, self.sizes, self.core, self.rep, self.far)
        grad_qkv = [
            spread_columns(e, o, self.sizes) for e, o in zip(head_minor(q_even), head_minor(q_odd))
        ]
        width = g_even.shape[1] // 2
        grad_gate = spread_columns(g_even[:, :width], g_odd[:, :width], self.sizes)
        grad_upward = spread_columns(g_even[:, width:], g_odd[:, width:], self.sizes)
        joined = finish_rows(jnp.concatenate([proj, down], axis=0), self.rep, self.near)
        return (*grad_qkv, joined[: proj.shape[0]], grad_gate, grad_upward, joined[proj.shape[0] :])


def shards(inputs, documents, *rest):
    masters_one, masters_two, cotangent = rest[:9], rest[9:18], rest[18]
    batch, rows, features = inputs.shape
    reps, sizes = lax.axis_size("rep"), (lax.axis_size("shard"), lax.axis_size("seq"))
    assert batch == 1 and sizes[1] == 2
    core, rep = lax.axis_index("seq"), lax.axis_index("rep")
    rows_owned = masters_one[1].shape[0]
    tuned = reps == 4 and rows_owned == LANES
    length = sizes[1] * rows
    half = core.astype(jnp.int32).reshape(1)
    frequencies = rope_base ** (-(jnp.arange(HD // 2, dtype=jnp.float32) * 2.0 / HD))
    angles = jnp.arange(length, dtype=jnp.float32)[:, None] * frequencies[None, :]
    cosine, sine = jnp.cos(angles), jnp.sin(angles)
    tables = (
        jnp.tile(cosine, (1, LANES * 2 // HD)),
        jnp.tile(jnp.concatenate([-sine, sine], axis=1), (1, LANES // HD)),
        documents.reshape(length, 1),
        documents.reshape(1, length),
    )
    gain_rows = jnp.stack([masters_one[0], masters_one[5], masters_two[0], masters_two[5]]).astype(
        jnp.bfloat16
    )
    flat = inputs.reshape(rows, features).astype(jnp.float32)
    place = jnp.stack([rep, core]).astype(jnp.int32)
    if tuned:
        gain_list = [masters_one[0], masters_one[5], masters_two[0], masters_two[5]]
        near_one = gather_near(masters_one[1:4], masters_one[4], gain_list, sizes[0], place)
        far_one = gather_far(masters_one[6:8], masters_one[8], sizes[0], place)
        near_two = gather_near(masters_two[1:4], masters_two[4], [], sizes[0], place)
        quarter_of = 2 * half_of(rep)
        far_two = [
            gather_far(
                masters_two[6:8], masters_two[8], sizes[0], jnp.stack([quarter_of + u, core]).astype(jnp.int32)
            )
            for u in range(2)
        ]
        gains = near_one.reshape(sizes[0], -1, FLAT)[:, -16:-12, : 2 * LANES]
        gains = gains.transpose(1, 0, 2).reshape(4, features).astype(jnp.float32)
        quarter, columns = rows_owned // 4 * 2, sizes[0] * LANES
        shapes = (
            (quarter, 3 * columns),
            rows_owned,
            (quarter, 2 * sizes[0] * masters_one[8].shape[0]),
            masters_one[8].shape[0],
        )
        first, second = Tuned(shapes, sizes, place), Tuned(shapes, sizes, place)
        near, wide, down = ways_one = first_ways(first, near_one, far_one, place)
        first.near_way, first.wide_way, first.down_way = ways_one
        ways = second_ways(second, near_two, far_two, wide, down, place)
        second.near_way, second.wide_way, second.down_way = ways
        first.after_attention = lambda value: tie(value, near_two, wide.one, wide.two, down.one, down.two)
        first.before_wide = lambda value: tie(value, far_two[0])
        first.after_wide = lambda value: tie(value, far_two[1], ways[0].one, ways[0].two)
        first.at_end = lambda value: tie(value, ways[0].three)
        second.after_attention = lambda value: tie(value, ways[1].one, ways[1].two)
    else:
        gains = lax.all_gather(gain_rows, ("shard", "seq"), axis=1, tiled=True).astype(jnp.float32)
        first, second = (Plain(gather_plain(m, sizes, core)) for m in (masters_one, masters_two))
    middle_one, first_kept, saved_one, weights_one = layer_ahead(
        flat, (gains[0:1], gains[1:2]), first, None, tables, place
    )
    final, _, saved_two, weights_two = layer_ahead(
        middle_one, (gains[2:3], gains[3:4]), second, first_kept, tables, place
    )
    outputs = final.astype(jnp.bfloat16).reshape(batch, rows, features)
    upstream = cotangent.reshape(rows, features).astype(jnp.float32)
    send = Sender(sizes, core, rep, tuned)
    grad_middle, gains_two, grads_two, extra = layer_back(
        upstream, (gains[2:3], gains[3:4]), weights_two, saved_two, None, tables, half, send
    )
    grad_flat, gains_one, grads_one, _ = layer_back(
        grad_middle, (gains[0:1], gains[1:2]), weights_one, saved_one, extra, tables, half, send
    )
    grad_input = grad_flat.reshape(batch, rows, features)
    gain_total = lax.psum(jnp.stack([*gains_one, *gains_two]), ("rep", "shard", "seq"))
    block = features // (sizes[0] * sizes[1])
    mine = lax.axis_index("shard") * sizes[1] + core
    own = lax.dynamic_slice_in_dim(gain_total, mine * block, block, 1)

    def ordered(gain_attn, gain_ffn, grads):
        query, key, value, proj, gate, upward, down = grads
        return (gain_attn, query, key, value, proj, gain_ffn, gate, upward, down)

    return (
        (outputs, grad_input)
        + ordered(own[0], own[1], grads_one)
        + ordered(own[2], own[3], grads_two)
    )


def solution(mesh):
    tokens = P(("rep", "shard"), "seq", None)
    vector, matrix = P(("shard", "seq")), P(("shard", "seq"), None)
    layer = (vector, matrix, matrix, matrix, matrix, vector, matrix, matrix, matrix)
    return jax.shard_map(
        shards,
        mesh=mesh,
        in_specs=(tokens, P(("rep", "shard"), None), *layer, *layer, tokens),
        out_specs=(tokens, tokens, *layer, *layer),
        check_vma=False,
    )
```

```python
import functools
import jax
import jax.numpy as jnp
from jax import lax
from jax.experimental import pallas as pl
from jax.experimental.pallas import tpu as pltpu
from jax.sharding import PartitionSpec as P

HD = 64
BLOCK = 256
LANES = 128
FLAT = 512
eps_norm = 1e-05
rope_base = 10000.0
mask_fill = -1000000000.0


def window(block):
    return max(0, block - 2)


def swap_halves(x):
    lane = lax.broadcasted_iota(jnp.int32, x.shape, 1)
    ahead = pltpu.roll(x, LANES - HD // 2, axis=1)
    behind = pltpu.roll(x, HD // 2, axis=1)
    return jnp.where(lane % HD < HD // 2, ahead, behind)


def fill_bias(bias, docs_column, docs_row, blocks):
    at = 0
    for i in range(blocks):
        first = window(i)
        rows = (i + 1 - first) * BLOCK
        same = (
            docs_column[pl.ds(first * BLOCK, rows), 0:1]
            == docs_row[0:1, pl.ds(i * BLOCK, BLOCK)]
        )
        bias[pl.ds(at, rows), :] = jnp.where(same, 0.0, mask_fill)
        at += rows


def block_of(mine_ref, other_ref, block, blocks, half):
    own, rows = block // (blocks // 2), pl.ds(block % (blocks // 2) * BLOCK, BLOCK)
    return jnp.where(half == own, mine_ref[rows, :], other_ref[rows, :])


def ahead_kernel(blocks, mixed, half_ref, mine_ref, other_ref, weight_ref, *rest):
    if mixed:
        first_ref, rest = rest[0], rest[1:]
    cos_ref, sin_ref, column_ref, row_ref, kept_ref, out_ref, lse_ref, bias = rest
    spin = half_ref[0] * (blocks // 2)

    @pl.when(pl.program_id(0) == 0)
    def _():
        fill_bias(bias, column_ref, row_ref, blocks)

    def place(b):
        return pl.multiple_of(lax.rem(b + spin, blocks) * BLOCK, BLOCK)

    for b in range(blocks):
        rows = pl.ds(b * BLOCK, BLOCK)
        cosine, sine = cos_ref[rows, :], sin_ref[rows, :]
        tokens = block_of(mine_ref, other_ref, b, blocks, half_ref[0])
        raw = jnp.dot(tokens, weight_ref[...], preferred_element_type=jnp.float32)
        for part in range(2):
            one = raw[:, part * LANES : (part + 1) * LANES]
            turned = one * cosine + swap_halves(one) * sine
            kept_ref[rows, part * LANES : (part + 1) * LANES] = turned.astype(jnp.bfloat16)
        value = raw[:, 2 * LANES :]
        if mixed:
            value = 0.5 * value + 0.5 * first_ref[rows, 2 * LANES :].astype(jnp.float32)
        kept_ref[rows, 2 * LANES :] = value.astype(jnp.bfloat16)

    value_turned = kept_ref[:, 2 * LANES :].T
    head_lane = lax.broadcasted_iota(jnp.int32, (BLOCK, LANES), 1) // HD
    at = 0
    for i in range(blocks):
        first = window(i)
        count = (i + 1 - first) * BLOCK
        rows = pl.ds(i * BLOCK, BLOCK)
        query = kept_ref[rows, 0:LANES] * jnp.bfloat16(HD**-0.5)
        keys = kept_ref[pl.ds(first * BLOCK, count), LANES : 2 * LANES]
        fill = bias[pl.ds(at, count), :]
        at += count
        outs = []
        for head in range(LANES // HD):
            one = jnp.where(head_lane == head, query, jnp.bfloat16(0))
            scores = (
                lax.dot_general(keys, one, (((1,), (1,)), ((), ())), preferred_element_type=jnp.float32)
                + fill
            )
            top = jnp.max(scores, axis=0, keepdims=True)
            powers = jnp.exp(scores - top)
            total = jnp.sum(powers, axis=0, keepdims=True)
            weights = (powers * (1.0 / total)).astype(jnp.bfloat16)
            outs.append(
                jnp.dot(
                    value_turned[head * HD : (head + 1) * HD, first * BLOCK : first * BLOCK + count],
                    weights,
                    preferred_element_type=jnp.float32,
                )
            )
            lse_ref[0, head : head + 1, rows] = top + jnp.log(total)
        merged = jnp.concatenate(outs, axis=0)
        out_ref[pl.ds(place(i), BLOCK), :] = merged.T.astype(jnp.bfloat16)


def back_kernel(blocks, mixed, half_ref, kept_ref, mine_ref, other_ref, lse_ref, *rest):
    if not mixed:
        extra_ref, rest = rest[0], rest[1:]
    cos_ref, sin_ref, column_ref, row_ref, out_ref, *rest = rest
    if mixed:
        passed_ref, rest = rest[0], rest[1:]
    bias, key_sum, value_sum = rest
    spin = half_ref[0] * (blocks // 2)

    @pl.when(pl.program_id(0) == 0)
    def _():
        fill_bias(bias, column_ref, row_ref, blocks)

    def place(b):
        return pl.multiple_of(lax.rem(b + spin, blocks) * BLOCK, BLOCK)

    def unrotate(x, rows):
        return x * cos_ref[rows, :] - swap_halves(x) * sin_ref[rows, :]

    keys_turned = kept_ref[:, LANES : 2 * LANES].T
    head_lane = lax.broadcasted_iota(jnp.int32, (BLOCK, LANES), 1) // HD
    at = 0
    for i in range(blocks):
        first = window(i)
        count = (i + 1 - first) * BLOCK
        rows = pl.ds(i * BLOCK, BLOCK)
        span = pl.ds(first * BLOCK, count)
        query = kept_ref[rows, 0:LANES] * jnp.bfloat16(HD**-0.5)
        grad = block_of(mine_ref, other_ref, i, blocks, half_ref[0])
        keys = kept_ref[span, LANES : 2 * LANES]
        values = kept_ref[span, 2 * LANES :]
        fill = bias[pl.ds(at, count), :]
        at += count
        outs = []
        key_add, value_add = [], []
        for head in range(LANES // HD):
            pick = head_lane == head
            one = jnp.where(pick, query, jnp.bfloat16(0))
            grad_one = jnp.where(pick, grad, jnp.bfloat16(0))
            scores = (
                lax.dot_general(keys, one, (((1,), (1,)), ((), ())), preferred_element_type=jnp.float32)
                + fill
            )
            weights = jnp.exp(scores - lse_ref[0, head : head + 1, rows])
            grad_weights = lax.dot_general(
                values, grad_one, (((1,), (1,)), ((), ())), preferred_element_type=jnp.float32
            )
            delta = jnp.sum(weights * grad_weights, axis=0, keepdims=True)
            grad_scores = (weights * (grad_weights - delta)).astype(jnp.bfloat16)
            value_add.append(
                jnp.dot(weights.astype(jnp.bfloat16), grad_one, preferred_element_type=jnp.float32)
            )
            key_add.append(jnp.dot(grad_scores, one, preferred_element_type=jnp.float32))
            outs.append(
                jnp.dot(
                    keys_turned[head * HD : (head + 1) * HD, first * BLOCK : first * BLOCK + count],
                    grad_scores,
                    preferred_element_type=jnp.float32,
                )
            )
        key_add, value_add = sum(key_add[1:], key_add[0]), sum(value_add[1:], value_add[0])
        old = count - BLOCK
        if old:
            key_sum[pl.ds(first * BLOCK, old), :] += key_add[:old]
            value_sum[pl.ds(first * BLOCK, old), :] += value_add[:old]
        key_sum[rows, :] = key_add[old:]
        value_sum[rows, :] = value_add[old:]
        grad_query = jnp.concatenate(outs, axis=0).T * HD**-0.5
        out_ref[pl.ds(place(i), BLOCK), 0:LANES] = unrotate(grad_query, rows).astype(jnp.bfloat16)
    for b in range(blocks):
        rows = pl.ds(b * BLOCK, BLOCK)
        there = pl.ds(place(b), BLOCK)
        out_ref[there, LANES : 2 * LANES] = unrotate(key_sum[rows, :], rows).astype(jnp.bfloat16)
        value_grad = value_sum[rows, :]
        if mixed:
            value_grad = 0.5 * value_grad
            passed_ref[rows, :] = value_grad
        else:
            value_grad = value_grad + extra_ref[rows, :]
        out_ref[there, 2 * LANES :] = value_grad.astype(jnp.bfloat16)


def bias_rows(blocks):
    return sum(i + 1 - window(i) for i in range(blocks)) * BLOCK


def whole(shape):
    return pl.BlockSpec(shape, lambda h, s: (0,) * len(shape))


def attend_ahead(tokens, weight, first_kept, tables, half):
    cosine, sine, column, row = tables
    length, width = 2 * tokens[0].shape[0], weight.shape[1]
    pairs, blocks = width // (3 * LANES), length // BLOCK
    mixed = first_kept is not None
    wide = pl.BlockSpec((length, 3 * LANES), lambda h, s: (0, h))
    slim = pl.BlockSpec((length, LANES), lambda h, s: (0, h))
    return pl.pallas_call(
        functools.partial(ahead_kernel, blocks, mixed),
        out_shape=(
            jax.ShapeDtypeStruct((length, width), jnp.bfloat16),
            jax.ShapeDtypeStruct((length, pairs * LANES), jnp.bfloat16),
            jax.ShapeDtypeStruct((pairs, LANES // HD, length), jnp.float32),
        ),
        grid_spec=pltpu.PrefetchScalarGridSpec(
            num_scalar_prefetch=1,
            grid=(pairs,),
            in_specs=[whole(tokens[0].shape)] * 2
            + [pl.BlockSpec((weight.shape[0], 3 * LANES), lambda h, s: (0, h))]
            + ([wide] if mixed else [])
            + [whole(cosine.shape), whole(sine.shape), whole(column.shape), whole(row.shape)],
            out_specs=(wide, slim, pl.BlockSpec((1, LANES // HD, length), lambda h, s: (h, 0, 0))),
            scratch_shapes=[pltpu.VMEM((bias_rows(blocks), BLOCK), jnp.float32)],
        ),
        compiler_params=pltpu.CompilerParams(dimension_semantics=("arbitrary",), vmem_limit_bytes=48 << 20),
        cost_estimate=pl.CostEstimate(flops=0, transcendentals=0, bytes_accessed=0),
        name="attend_ahead",
    )(half, *tokens, weight, *((first_kept,) if mixed else ()), cosine, sine, column, row)


def attend_back(kept, grad, lse, extra, tables, half):
    cosine, sine, column, row = tables
    length, width = kept.shape
    pairs, blocks = width // (3 * LANES), length // BLOCK
    mixed = extra is None
    wide = pl.BlockSpec((length, 3 * LANES), lambda h, s: (0, h))
    slim = pl.BlockSpec((length, LANES), lambda h, s: (0, h))
    outs = [jax.ShapeDtypeStruct((length, width), jnp.bfloat16)]
    out_specs = [wide]
    if mixed:
        outs.append(jax.ShapeDtypeStruct((length, pairs * LANES), jnp.float32))
        out_specs.append(slim)
    result = pl.pallas_call(
        functools.partial(back_kernel, blocks, mixed),
        out_shape=tuple(outs),
        grid_spec=pltpu.PrefetchScalarGridSpec(
            num_scalar_prefetch=1,
            grid=(pairs,),
            in_specs=[wide]
            + [pl.BlockSpec((length // 2, LANES), lambda h, s: (0, h))] * 2
            + [pl.BlockSpec((1, LANES // HD, length), lambda h, s: (h, 0, 0))]
            + ([] if mixed else [slim])
            + [whole(cosine.shape), whole(sine.shape), whole(column.shape), whole(row.shape)],
            out_specs=tuple(out_specs),
            scratch_shapes=[
                pltpu.VMEM((bias_rows(blocks), BLOCK), jnp.float32),
                pltpu.VMEM((length, LANES), jnp.float32),
                pltpu.VMEM((length, LANES), jnp.float32),
            ],
        ),
        compiler_params=pltpu.CompilerParams(dimension_semantics=("arbitrary",), vmem_limit_bytes=48 << 20),
        cost_estimate=pl.CostEstimate(flops=0, transcendentals=0, bytes_accessed=0),
        name="attend_back",
    )(half, kept, *grad, lse, *(() if mixed else (extra,)), cosine, sine, column, row)
    return result if mixed else (result[0], None)


def swap_cores(x):
    return lax.ppermute(x, "seq", [(0, 1), (1, 0)])


def exchange(x, mask):
    count = lax.axis_size("rep")
    return lax.ppermute(x, "rep", [(i, i ^ mask) for i in range(count)])


def unflat(read, rows, columns, write):
    at = 0
    for i in range(columns // FLAT):
        write(0, i * FLAT, read(at, rows, 0, FLAT))
        at += rows
    left = columns % FLAT
    if left:
        step = rows * left // FLAT
        for i in range(FLAT // left):
            write(i * step, columns - left, read(at, step, i * left, left))
        at += step
    return at


def join_kernel(masks, parts, cores, slot_ref, *refs):
    pieces, outs = refs[: len(masks)], refs[-sum(len(w) if k == "columns" else 1 for k, _, w in parts) :]
    for mask, piece in zip(masks, pieces):
        slot = lax.bitwise_xor(slot_ref[0], mask)
        base, at = 0, 0
        for kind, rows, widths in parts:
            columns = sum(widths)

            def read(row, count, column, width, base=base):
                return piece[0, base + row : base + row + count, column : column + width]

            def write(row, column, values, kind=kind, rows=rows, widths=widths, at=at):
                if kind == "columns":
                    one = rows // cores
                    left, which = column, 0
                    while left >= widths[which]:
                        left, which = left - widths[which], which + 1
                    took, offset = 0, column
                    while took < values.shape[1]:
                        size = min(widths[which] - left, values.shape[1] - took)
                        count = values.shape[0]
                        for done in range(0, count, min(one, count)):
                            core, inside = divmod(row + done, one)
                            size_rows = min(one, count)
                            outs[at + which][0, core, slot, inside : inside + size_rows, left : left + size] = (
                                values[done : done + size_rows, took : took + size]
                            )
                        took, left, which = took + size, 0, which + 1
                else:
                    there = pl.ds(pl.multiple_of(slot * columns, columns) + column, values.shape[1])
                    outs[at][0, row : row + values.shape[0], there] = values

            base += unflat(read, rows, columns, write)
            at += len(widths) if kind == "columns" else 1


def join(pieces, masks, slot, sizes, parts, start=None, after=()):
    groups, cores = sizes
    count, rows = len(masks), pieces[0].shape[0] // groups
    read = rows if start is None else sum(h * sum(w) for _, h, w in parts) // FLAT
    at = 0 if start is None else start // read
    shapes = []
    for kind, height, widths in parts:
        if kind == "columns":
            shapes += [(groups, cores, count, height // cores, w) for w in widths]
        else:
            shapes.append((groups, height, count * widths[0]))
    outs = pl.pallas_call(
        functools.partial(join_kernel, masks, parts, cores),
        out_shape=[jax.ShapeDtypeStruct(s, jnp.bfloat16) for s in shapes],
        grid_spec=pltpu.PrefetchScalarGridSpec(
            num_scalar_prefetch=1,
            grid=(groups,),
            in_specs=[pl.BlockSpec((1, read, FLAT), lambda g, s: (g, at, 0))] * count
            + [pl.BlockSpec(memory_space=pl.ANY)] * len(after),
            out_specs=[
                pl.BlockSpec((1, *s[1:]), lambda g, t, n=len(s): (g,) + (0,) * (n - 1)) for s in shapes
            ],
        ),
        cost_estimate=pl.CostEstimate(flops=0, transcendentals=0, bytes_accessed=0),
        name="join",
    )(slot, *[p.reshape(groups, rows, FLAT) for p in pieces], *after)
    return [o.reshape(-1, o.shape[-1]) for o in outs]


def core_columns(rows, sizes, core):
    shards, cores = sizes
    width = rows.shape[1] // (shards * cores)
    even, odd = (
        jnp.concatenate(
            [rows[:, (s * cores + c) * width : (s * cores + c + 1) * width] for s in range(shards)],
            axis=1,
        )
        for c in range(cores)
    )
    return jnp.where(core == 0, even, odd), jnp.where(core == 0, odd, even)


def head_major(parts):
    pairs = parts[0].shape[1] // LANES
    return jnp.concatenate(
        [p[:, i * LANES : (i + 1) * LANES] for i in range(pairs) for p in parts], axis=1
    )


def head_minor(joined):
    pairs = joined.shape[1] // (3 * LANES)
    return [
        jnp.concatenate(
            [
                joined[:, (3 * i + j) * LANES : (3 * i + j + 1) * LANES]
                for i in range(pairs)
            ],
            axis=1,
        )
        for j in range(3)
    ]


def chip_rows(rows_of, sizes, core):
    mine, theirs = rows_of
    other = swap_cores(theirs)
    return jnp.concatenate(
        [jnp.where(core == 0, mine, other), jnp.where(core == 0, other, mine)], axis=0
    )


def gather_shard(x):
    return lax.all_gather(x, "shard", axis=0, tiled=True)


def column_parts(weights, sizes, core, interleave):
    mine, theirs = zip(*[core_columns(w.astype(jnp.bfloat16), sizes, core) for w in weights])
    if interleave:
        return head_major(mine), head_major(theirs)
    return jnp.concatenate(mine, axis=1), jnp.concatenate(theirs, axis=1)


def gather_plain(masters, sizes, core):
    _, w_query, w_key, w_value, w_proj, _, w_gate, w_upward, w_down = masters
    w_qkv = gather_shard(chip_rows(column_parts((w_query, w_key, w_value), sizes, core, True), sizes, core))
    w_wide = gather_shard(chip_rows(column_parts((w_gate, w_upward), sizes, core, False), sizes, core))
    w_proj, w_down = (gather_shard(w.astype(jnp.bfloat16)) for w in (w_proj, w_down))
    return w_qkv, w_proj, w_wide, w_down


def call(kernel, outs, grid, in_specs, out_specs, name, scratch=(), scalars=1):
    return pl.pallas_call(
        kernel,
        out_shape=outs,
        grid_spec=pltpu.PrefetchScalarGridSpec(
            num_scalar_prefetch=scalars,
            grid=grid,
            in_specs=in_specs,
            out_specs=out_specs,
            scratch_shapes=scratch,
        ),
        compiler_params=pltpu.CompilerParams(
            dimension_semantics=("arbitrary",) * len(grid), vmem_limit_bytes=56 << 20
        ),
        cost_estimate=pl.CostEstimate(flops=0, transcendentals=0, bytes_accessed=0),
        name=name,
    )


def fixed(shape):
    return pl.BlockSpec(shape, lambda *ids: (0,) * len(shape))


def low(values):
    return values.astype(jnp.bfloat16)


def near_split_kernel(shards, place_ref, *refs):
    weights, gains, (mine, theirs) = refs[:3], refs[3:-2], refs[-2:]
    core = place_ref[1]
    for out, which in ((mine, core), (theirs, 1 - core)):
        for s in range(shards):
            there = pl.ds(pl.multiple_of((2 * s + which) * LANES, LANES), LANES)
            for j, weight in enumerate(weights):
                out[:, (3 * s + j) * LANES : (3 * s + j + 1) * LANES] = low(weight[:, there])
        if gains:
            rows = jnp.concatenate([g[...] for g in gains] + [jnp.zeros((16 - len(gains), LANES), jnp.float32)], axis=0)
            out[0:16, 3 * shards * LANES :] = low(rows)


def near_merge_kernel(place_ref, mine, theirs, proj, out):
    core = place_ref[1]
    rows = mine.shape[0]
    for j in range(3):
        for part, which in ((mine, core), (theirs, 1 - core)):
            there = pl.ds(pl.multiple_of((2 * j + which) * rows, rows), rows)
            out[there, :] = part[:, j * FLAT : (j + 1) * FLAT]
    half = proj.shape[0] // 2
    start = 6 * rows
    out[start : start + half, 0 : FLAT // 2] = low(proj[0:half, :])
    out[start : start + half, FLAT // 2 :] = low(proj[half:, :])
    if out.shape[0] > start + half:
        out[start + half :, :] = jnp.zeros((16, FLAT), jnp.bfloat16)
        for part, which in ((mine, core), (theirs, 1 - core)):
            there = pl.ds(pl.multiple_of(which * LANES, LANES), LANES)
            out[start + half :, there] = part[0:16, 3 * FLAT : 3 * FLAT + LANES]


def far_split_kernel(shards, place_ref, gate, upward, mine, theirs):
    core = place_ref[1]
    width = gate.shape[1] // (2 * shards)
    for at, weight in enumerate((gate, upward)):
        even, odd = (
            low(jnp.concatenate([weight[:, (2 * s + c) * width : (2 * s + c + 1) * width] for s in range(shards)], axis=1))
            for c in range(2)
        )
        there = slice(at * shards * width, (at + 1) * shards * width)
        mine[:, there] = jnp.where(core == 0, even, odd)
        theirs[:, there] = jnp.where(core == 0, odd, even)


def far_merge_kernel(place_ref, mine, theirs, down, out):
    core = place_ref[1]
    rows, columns = mine.shape
    blocks = columns // FLAT
    for part, which in ((mine, core), (theirs, 1 - core)):
        for j in range(blocks):
            there = pl.ds(pl.multiple_of((2 * j + which) * rows, rows), rows)
            out[there, :] = part[:, j * FLAT : (j + 1) * FLAT]
        there = pl.ds(pl.multiple_of(which * (FLAT // 2), FLAT // 2), FLAT // 2)
        out[2 * blocks * rows : (2 * blocks + 1) * rows, there] = part[:, blocks * FLAT :]
    half, start = down.shape[0] // 2, (2 * blocks + 1) * rows
    out[start:, 0 : FLAT // 2] = low(down[0:half, :])
    out[start:, FLAT // 2 :] = low(down[half:, :])


def shape_of(*shape, dtype=jnp.bfloat16):
    return jax.ShapeDtypeStruct(shape, dtype)


def quarter_of_rows(weight):
    return pl.BlockSpec((weight.shape[0] // 4, weight.shape[1]), lambda i, s: (s[0], 0))


def quarter_of_columns(weight):
    return pl.BlockSpec((weight.shape[0], weight.shape[1] // 4), lambda i, s: (0, s[0]))


def gather_near(weights, proj, gains, shards, place):
    rows = weights[0].shape[0] // 4
    width = 3 * shards * LANES + (LANES if gains else 0)
    gains = [g.reshape(1, LANES) for g in gains]
    mine, theirs = call(
        functools.partial(near_split_kernel, shards),
        [shape_of(rows, width)] * 2,
        (1,),
        [quarter_of_rows(w) for w in weights] + [fixed((1, LANES))] * len(gains),
        [fixed((rows, width))] * 2,
        "near_split",
    )(place, *weights, *gains)
    total = 6 * rows + proj.shape[0] // 2 + (16 if gains else 0)
    merged = call(
        near_merge_kernel,
        shape_of(total, FLAT),
        (1,),
        [fixed((rows, width))] * 2 + [quarter_of_columns(proj)],
        fixed((total, FLAT)),
        "near_merge",
    )(place, mine, swap_cores(theirs), proj)
    return merged


def gather_far(weights, down, shards, place):
    rows, width = weights[0].shape[0] // 4, weights[0].shape[1]
    mine, theirs = call(
        functools.partial(far_split_kernel, shards),
        [shape_of(rows, width)] * 2,
        (1,),
        [quarter_of_rows(w) for w in weights],
        [fixed((rows, width))] * 2,
        "far_split",
    )(place, *weights)
    total = rows * width // (FLAT // 2) + down.shape[0] // 2
    merged = call(
        far_merge_kernel,
        shape_of(total, FLAT),
        (1,),
        [fixed((rows, width))] * 2 + [quarter_of_columns(down)],
        fixed((total, FLAT)),
        "far_merge",
    )(place, mine, swap_cores(theirs), down)
    return merged


def dot_nn(a, b):
    return jnp.dot(a, b, preferred_element_type=jnp.float32)


def halves_of_rows(tile, per_half):
    return [
        lambda i, s: (jnp.minimum(i, per_half - 1), 0),
        lambda i, s: (jnp.maximum(i - per_half, 0), 0),
    ]


def gated_kernel(per_half, none_ref, mine, other, weight, gate_out, upward_out, inner_out):
    tokens = jnp.where(pl.program_id(0) < per_half, mine[...], other[...])
    width = gate_out.shape[1]
    one, two = dot_nn(tokens, weight[:, :width]), dot_nn(tokens, weight[:, width:])
    inner_out[...] = low(one * jax.nn.sigmoid(one) * two)
    gate_out[...] = low(one)
    upward_out[...] = low(two)


def gated(tokens, weight, place):
    length, width, tile = 2 * tokens[0].shape[0], weight.shape[1] // 2, 256
    rows = pl.BlockSpec((tile, width), lambda i, s: (i, 0))
    maps = halves_of_rows(tile, length // tile // 2)
    return call(
        functools.partial(gated_kernel, length // tile // 2),
        [shape_of(length, width)] * 3,
        (length // tile,),
        [pl.BlockSpec((tile, tokens[0].shape[1]), m) for m in maps] + [fixed(weight.shape)],
        [rows] * 3,
        "gated",
    )(place, *tokens, weight)


def gated_back_kernel(per_half, none_ref, mine, other, weight, gate, upward, out):
    grad = jnp.where(pl.program_id(0) < per_half, mine[...], other[...])
    width = gate.shape[1]
    inner = lax.dot_general(grad, weight[...], (((1,), (1,)), ((), ())), preferred_element_type=jnp.float32)
    one, two = gate[...].astype(jnp.float32), upward[...].astype(jnp.float32)
    part = jax.nn.sigmoid(one)
    out[:, :width] = low(inner * two * part * (1.0 + one * (1.0 - part)))
    out[:, width:] = low(inner * one * part)


def gated_back(grad, weight, gate, upward, place):
    (length, width), tile = gate.shape, 256
    rows = pl.BlockSpec((tile, width), lambda i, s: (i, 0))
    maps = halves_of_rows(tile, length // tile // 2)
    return call(
        functools.partial(gated_back_kernel, length // tile // 2),
        shape_of(length, 2 * width),
        (length // tile,),
        [pl.BlockSpec((tile, grad[0].shape[1]), m) for m in maps] + [fixed(weight.shape), rows, rows],
        pl.BlockSpec((tile, 2 * width), lambda i, s: (i, 0)),
        "gated_back",
    )(place, *grad, weight, gate, upward)


def turned(a, b):
    return lax.dot_general(a, b, (((0,), (0,)), ((), ())), preferred_element_type=jnp.float32)


def grad_rows_kernel(bits_ref, mine, other, right, *outs):
    half, parts = mine.shape[0], len(outs) // 2
    product = turned(mine[...], right[0:half, :]) + turned(other[...], right[half:, :])
    groups, rows, width = outs[0].shape
    for part in range(parts):
        sent, kept = outs[2 * part : 2 * part + 2]
        upper, columns = bits_ref[part] == 0, slice(part * width, (part + 1) * width)
        for g in range(groups):
            one, two = (low(product[(2 * g + h) * rows : (2 * g + h + 1) * rows, columns]) for h in range(2))
            kept[g] = jnp.where(upper, one, two)
            sent[g] = jnp.where(upper, two, one)


def grad_rows(left, right, groups, bits, parts=1, tile=256):
    half, features = left[0].shape
    length, width = right.shape
    per, rows = groups * tile // features, features // groups // 2
    out = pl.BlockSpec((per, rows, width // parts), lambda i, s: (i, 0, 0))
    return call(
        grad_rows_kernel,
        [shape_of(groups, rows, width // parts)] * (2 * parts),
        (features // tile,),
        [pl.BlockSpec((half, tile), lambda i, s: (0, i))] * 2 + [fixed((length, width))],
        [out] * (2 * parts),
        "grad_rows",
    )(bits, *left, right)


def grad_whole_kernel(none_ref, left, mine, other, out):
    half = mine.shape[0]
    out[...] = low(turned(left[0:half, :], mine[...]) + turned(left[half:, :], other[...]))


def grad_whole(left, right, place, steps=2):
    length, rows = left.shape
    half, width = right[0].shape
    side = pl.BlockSpec((half, width // steps), lambda i, s: (0, i))
    return call(
        grad_whole_kernel,
        shape_of(rows, width),
        (steps,),
        [fixed((length, rows)), side, side],
        pl.BlockSpec((rows, width // steps), lambda i, s: (0, i)),
        "grad_whole",
    )(place, left, *right)


def grad_columns_kernel(bits_ref, left, mine, other, sent, kept):
    half = mine.shape[0]
    product = low(turned(left[0:half, :], mine[...]) + turned(left[half:, :], other[...]))

    @pl.when(pl.program_id(0) == 0)
    def _():
        sent[...] = product

    @pl.when(pl.program_id(0) == 1)
    def _():
        kept[...] = product


def grad_columns(left, right, bits):
    length, rows = left.shape
    half, width = right[0].shape
    side = pl.BlockSpec((half, width // 2), lambda i, s: (0, jnp.where(i == 0, 1 - s[0], s[0])))
    return call(
        grad_columns_kernel,
        [shape_of(rows, width // 2)] * 2,
        (2,),
        [fixed((length, rows)), side, side],
        [fixed((rows, width // 2))] * 2,
        "grad_columns",
    )(bits, left, *right)


def add(a, b):
    return a + b


def halve_kernel(parts, bits_ref, *refs):
    ins, outs = refs[: 2 * parts], refs[2 * parts :]
    for part in range(parts):
        kept, got = ins[2 * part : 2 * part + 2]
        sent_out, kept_out = outs[2 * part : 2 * part + 2]
        total = add(kept[...], got[...])
        upper = bits_ref[1 - part] == 0
        middle = kept.shape[1] // 2
        one, two = total[:, :middle], total[:, middle:]
        kept_out[...] = jnp.where(upper, one, two)
        sent_out[...] = jnp.where(upper, two, one)


def halve(ins, bits, steps):
    shape, parts = ins[0].shape, len(ins) // 2
    block = (shape[0] // steps, *shape[1:])
    small = (*shape[:1], shape[1] // 2, *shape[2:])
    index = lambda i, s: (i,) + (0,) * (len(shape) - 1)
    return call(
        functools.partial(halve_kernel, parts),
        [shape_of(*small)] * (2 * parts),
        (steps,),
        [pl.BlockSpec(block, index)] * (2 * parts),
        [pl.BlockSpec((block[0], *small[1:]), index)] * (2 * parts),
        "halve",
    )(bits, *ins)


def flatten_kernel(parts, none_ref, *refs):
    bodies, tails, out = refs[: 2 * parts], refs[2 * parts : -1], refs[-1]
    sums = [add(bodies[2 * p][...], bodies[2 * p + 1][...]) for p in range(parts)]
    total = jnp.concatenate(sums, axis=2) if parts > 1 else sums[0]
    cores, rows, columns = total.shape
    blocks, left = columns // FLAT, columns % FLAT
    for j in range(blocks):
        for c in range(cores):
            there = slice((j * cores + c) * rows, (j * cores + c + 1) * rows)
            out[0, there, :] = total[c, :, j * FLAT : (j + 1) * FLAT]
    at = blocks * cores * rows
    if left:
        for c in range(cores):
            out[0, at : at + rows, c * left : (c + 1) * left] = total[c, :, columns - left :]
        at += rows
    if tails:
        tail = add(tails[0][...], tails[1][...])
        half = tail.shape[0] // 2
        out[0, at:, 0 : FLAT // 2] = tail[:half]
        out[0, at:, FLAT // 2 :] = tail[half:]


def flatten(bodies, tails, shards, bits):
    groups, rows, columns = bodies[0].shape
    height, width = tails[0].shape if tails else (0, 0)
    cores, parts = groups // shards, len(bodies) // 2
    total = (parts * cores * rows * columns + height // shards * width) // FLAT
    return call(
        functools.partial(flatten_kernel, parts),
        shape_of(shards, total, FLAT),
        (shards,),
        [pl.BlockSpec((cores, rows, columns), lambda i, s: (i, 0, 0))] * len(bodies)
        + [pl.BlockSpec((height // shards, width), lambda i, s: (i, 0))] * len(tails),
        pl.BlockSpec((1, total, FLAT), lambda i, s: (i, 0, 0)),
        "flatten",
    )(bits, *bodies, *tails).reshape(-1, FLAT)


def append_kernel(none_ref, *refs):
    bodies, (kept, got, out) = refs[:-3], refs[-3:]
    at = 0
    for body in bodies:
        out[at : at + body.shape[0], :] = body[...]
        at += body.shape[0]
    tail, half = add(kept[...], got[...]), kept.shape[0] // 2
    out[at:, 0 : FLAT // 2] = tail[:half]
    out[at:, FLAT // 2 :] = tail[half:]


def append(bodies, kept, got, bits):
    rows = sum(b.shape[0] for b in bodies) + kept.shape[0] // 2
    return call(
        append_kernel,
        shape_of(rows, FLAT),
        (1,),
        [fixed(x.shape) for x in (*bodies, kept, got)],
        fixed((rows, FLAT)),
        "append",
    )(bits, *bodies, kept, got)


def from_row(pieces, start):
    return [p.at[pl.ds(start, p.shape[0] - start)] for p in pieces] if start else pieces


def pick_kernel(blocks, rows, left, start, count, place_ref, *refs):
    pieces, out = from_row(refs[:count], start), refs[-1]
    which = 1 - place_ref[1]
    for k, piece in enumerate(pieces):
        for j in range(blocks):
            there = pl.ds(pl.multiple_of((2 * j + which) * rows, rows), rows)
            out[k, j * rows : (j + 1) * rows, :] = piece[there, :]
        if left:
            there = pl.ds(pl.multiple_of(which * left, left), left)
            out[k, blocks * rows :, 0:left] = piece[2 * blocks * rows : (2 * blocks + 1) * rows, there]
            out[k, blocks * rows :, left:] = jnp.zeros((rows, FLAT - left), jnp.bfloat16)


def pick(pieces, rows, columns, place, start, after):
    blocks, left = columns // FLAT, columns % FLAT
    total = (blocks + (left > 0)) * rows
    return call(
        functools.partial(pick_kernel, blocks, rows, left, start, len(pieces)),
        shape_of(len(pieces), total, FLAT),
        (1,),
        [fixed(pieces[0].shape)] * len(pieces) + [pl.BlockSpec(memory_space=pl.ANY)] * len(after),
        fixed((len(pieces), total, FLAT)),
        "pick",
    )(place, *pieces, *after)


def slots_of(bits_ref):
    places = []
    for one, two in ((0, 0), (1, 0), (0, 1), (1, 1)):
        first, second = lax.bitwise_xor(bits_ref[0], one), lax.bitwise_xor(bits_ref[1], two)
        places.append((2 * first + second, 2 * second + first))
    return places


def tail_out(piece, start, out, slot):
    half, columns = out.shape[0] // 2, FLAT // 2
    there = pl.ds(pl.multiple_of(slot * columns, columns), columns)
    out[0:half, there] = piece[start : start + half, 0:columns].astype(jnp.float32)
    out[half:, there] = piece[start : start + half, columns:].astype(jnp.float32)


def finish_near_kernel(shards, rows, start, bits_ref, place_ref, *refs):
    pieces, other, outs, tail = from_row(refs[:4], start), refs[4], refs[5:8], refs[8]
    core = place_ref[1]
    for k, slots in enumerate(slots_of(bits_ref)):
        for s in range(shards):
            there = pl.ds(pl.multiple_of(slots[2 * s // shards] * rows, rows), rows)
            for j, out in enumerate(outs):
                block, lane = divmod((3 * s + j) * LANES, FLAT)
                mine_rows = pl.ds(pl.multiple_of((2 * block + core) * rows, rows), rows)
                mine = pieces[k][mine_rows, lane : lane + LANES]
                theirs = other[k, block * rows : (block + 1) * rows, lane : lane + LANES]
                for part, which in ((mine, core), (theirs, 1 - core)):
                    lanes = pl.ds(pl.multiple_of((2 * s + which) * LANES, LANES), LANES)
                    out[there, lanes] = part.astype(jnp.float32)
        tail_out(pieces[k], 6 * rows, tail, slots[0])


def finish_far_kernel(shards, rows, start, bits_ref, place_ref, *refs):
    pieces, other, outs, tail = from_row(refs[:4], start), refs[4], refs[5:7], refs[7]
    core = place_ref[1]
    width = outs[0].shape[1] // (2 * shards)
    columns = 2 * shards * width
    blocks, left = columns // FLAT, columns % FLAT
    for k, slots in enumerate(slots_of(bits_ref)):
        mine = [
            pieces[k][pl.ds(pl.multiple_of((2 * j + core) * rows, rows), rows), :] for j in range(blocks)
        ]
        lanes = pl.ds(pl.multiple_of(core * left, left), left)
        mine.append(pieces[k][2 * blocks * rows : (2 * blocks + 1) * rows, lanes])
        theirs = [other[k, j * rows : (j + 1) * rows, :] for j in range(blocks)]
        theirs.append(other[k, blocks * rows :, 0:left])
        mine, theirs = (jnp.concatenate(p, axis=1).astype(jnp.float32) for p in (mine, theirs))
        even, odd = jnp.where(core == 0, mine, theirs), jnp.where(core == 0, theirs, mine)
        for at, out in enumerate(outs):
            there = pl.ds(pl.multiple_of(slots[at] * rows, rows), rows)
            parts = [
                p[:, (at * shards + s) * width : (at * shards + s + 1) * width]
                for s in range(shards)
                for p in (even, odd)
            ]
            out[there, :] = jnp.concatenate(parts, axis=1)
        tail_out(pieces[k], (2 * blocks + 1) * rows, tail, slots[0])


class Way:
    def __init__(self, halves, plan, bits):
        self.sent, self.kept = halves[::2], halves[1::2]
        self.plan, self.bits = plan, bits
        self.got = [exchange(x, plan[p]) for p, x in enumerate(self.sent)]

    def last(self, value):
        return [x for pair in zip(self.kept, self.got) for x in (tie(pair[0], value), pair[1])]

    def half(self, value, steps=2):
        outs = halve(self.last(value), self.bits, steps)
        self.sent, self.kept = outs[::2], outs[1::2]
        self.got = [exchange(x, self.plan[1 - p]) for p, x in enumerate(self.sent)]
        return tuple(self.sent)


class TunedSender:
    def __init__(self, sizes, place, near, far):
        self.sizes, self.place, self.near_plan, self.far_plan = sizes, place, near, far
        self.near_bits, self.far_bits = (
            jnp.stack([bit_of(place[0], m) for m in plan]).astype(jnp.int32) for plan in (near, far)
        )
        self.groups = sizes[0] * sizes[1]

    def down(self, left, right):
        grad = grad_whole(left, right, self.place)
        self.down_sum = scatter_shard(grad)
        return grad

    def down_way(self, value):
        reduced, bit = tie(self.down_sum, value), self.far_bits[0]
        width = reduced.shape[1] // 2
        halves = [lax.dynamic_slice_in_dim(reduced, b * width, width, 1) for b in (1 - bit, bit)]
        self.way_down = Way(halves, self.far_plan, self.far_bits)
        return halves[0]

    def wide(self, left, right):
        self.way_wide = Way(grad_rows(left, right, self.groups, self.far_bits, 2), self.far_plan, self.far_bits)
        return self.way_wide.sent[0]

    def proj(self, left, right):
        self.way_proj = Way(grad_columns(left, right, self.near_bits), self.near_plan, self.near_bits)
        return self.way_proj.sent[0]

    def qkv(self, left, right):
        self.way_qkv = Way(grad_rows(left, right, self.groups, self.near_bits, 2), self.near_plan, self.near_bits)
        return self.way_qkv.sent[0]

    def half(self, name, steps=2):
        return lambda value: getattr(self, name).half(value, steps)

    def got(self, name):
        return lambda value: tuple(getattr(self, name).got)

    def scatter_wide(self, value):
        self.wide_shape = self.way_wide.kept[0].shape
        flat = flatten(self.way_wide.last(value), (), self.sizes[0], self.far_bits)
        self.wide_sum = scatter_shard(flat)
        return flat

    def scatter_near(self, value):
        self.near_shape, self.proj_height = self.way_qkv.kept[0].shape, self.way_proj.kept[0].shape[0] // self.sizes[0]
        flat = flatten(self.way_qkv.last(value), self.way_proj.last(value), self.sizes[0], self.near_bits)
        self.near_sum = scatter_shard(flat)
        return flat

    def shared(self, piece, plan):
        return [piece] + [exchange(piece, m) for m in (*plan, plan[0] ^ plan[1])]

    def share_near(self, value):
        self.near_at, self.near_pieces = 0, self.shared(tie(self.near_sum, value), self.near_plan)
        return self.near_pieces[0]

    def share_far(self, value):
        piece = append([tie(self.wide_sum, value)], self.way_down.kept[0], self.way_down.got[0], self.far_bits)
        self.far_at, self.far_pieces = 0, self.shared(piece, self.far_plan)
        return piece

    def share_all(self, value):
        bodies = [tie(self.near_sum, value), self.wide_sum]
        piece = append(bodies, self.way_down.kept[0], self.way_down.got[0], self.far_bits)
        self.near_at, self.far_at = 0, self.near_sum.shape[0]
        own, one, two, both = self.near_pieces = self.shared(piece, self.near_plan)
        self.far_pieces = [own, one, two, both] if self.near_plan == self.far_plan else [own, two, one, both]
        return piece

    def far_got(self, value):
        return tuple(self.far_pieces[1:])

    def near_got(self, value):
        return tuple(self.near_pieces[1:])

    def pick_near(self, value, *after):
        _, rows, columns = self.near_shape
        pieces = [tie(self.near_pieces[0], value), *self.near_pieces[1:]]
        picked = pick(pieces, rows, 2 * columns, self.place, self.near_at, after)
        self.near_other = swap_cores(picked)
        return picked

    def pick_far(self, value, *after):
        _, rows, columns = self.wide_shape
        pieces = [tie(self.far_pieces[0], value), *self.far_pieces[1:]]
        picked = pick(pieces, rows, 2 * columns, self.place, self.far_at, after)
        self.far_other = swap_cores(picked)
        return picked

    def finish_near(self, value):
        rows, features = self.near_shape[1], self.groups * LANES
        self.near = self.finish(
            functools.partial(finish_near_kernel, self.sizes[0], rows, self.near_at),
            [(4 * rows, features)] * 3 + [(self.proj_height, 2 * FLAT)],
            (self.near_bits, tie(self.place, value), *self.near_pieces, self.near_other),
            "finish_near",
        )
        return self.near[0]

    def finish_far(self, value):
        _, rows, columns = self.wide_shape
        self.far = self.finish(
            functools.partial(finish_far_kernel, self.sizes[0], rows, self.far_at),
            [(4 * rows, 2 * columns)] * 2 + [(self.way_down.kept[0].shape[0], 2 * FLAT)],
            (self.far_bits, tie(self.place, value), *self.far_pieces, self.far_other),
            "finish_far",
        )
        return self.far[0]

    def finish(self, kernel, shapes, operands, name):
        return call(
            kernel,
            [shape_of(*s, dtype=jnp.float32) for s in shapes],
            (1,),
            [fixed(x.shape) for x in operands[2:]],
            [fixed(s) for s in shapes],
            name,
            scalars=2,
        )(*operands)


class PlainSender:
    def __init__(self, sizes, core):
        self.sizes, self.core = sizes, core

    def total(self, grad):
        return lax.psum(scatter_shard(low(grad)), "rep")

    def down(self, left, right):
        self.down_sum = self.total(dot_tn(left, jnp.concatenate(right, axis=0)))

    def proj(self, left, right):
        self.proj_sum = self.total(dot_tn(left, jnp.concatenate(right, axis=0)))

    def wide(self, left, right):
        self.wide_sum = self.total(dot_tn(jnp.concatenate(left, axis=0), right))

    def qkv(self, left, right):
        self.qkv_sum = self.total(dot_tn(jnp.concatenate(left, axis=0), right))

    def columns(self, reduced):
        shaped = reduced.reshape(2, -1, reduced.shape[1])
        mine = lax.dynamic_index_in_dim(shaped, self.core, 0, keepdims=False)
        other = swap_cores(lax.dynamic_index_in_dim(shaped, 1 - self.core, 0, keepdims=False))
        even, odd = jnp.where(self.core == 0, mine, other), jnp.where(self.core == 0, other, mine)
        return even.astype(jnp.float32), odd.astype(jnp.float32)

    def near(self):
        even, odd = self.columns(self.qkv_sum)
        parts = [spread_columns(e, o, self.sizes) for e, o in zip(head_minor(even), head_minor(odd))]
        return (*parts, self.proj_sum.astype(jnp.float32))

    def far(self):
        even, odd = self.columns(self.wide_sum)
        width = even.shape[1] // 2
        parts = [spread_columns(even[:, at], odd[:, at], self.sizes) for at in (slice(0, width), slice(width, None))]
        return (*parts, self.down_sum.astype(jnp.float32))


def bit_of(rep, mask):
    return (rep // mask) % 2


def scatter_shard(x):
    return lax.psum_scatter(x, "shard", scatter_dimension=0, tiled=True)


def spread_columns(even, odd, sizes):
    shards, cores = sizes
    width = even.shape[1] // shards
    return jnp.concatenate(
        [p[:, s * width : (s + 1) * width] for s in range(shards) for p in (even, odd)], axis=1
    )


def norm_ahead(values, gain_row):
    factor = lax.rsqrt(jnp.mean(values * values, axis=-1, keepdims=True) + eps_norm)
    return ((values * factor * gain_row).astype(jnp.bfloat16), factor)


def norm_back(values, factor, gain_row, upstream):
    scaled = upstream * gain_row
    gain_grad = jnp.sum(upstream * values * factor, axis=0)
    inner_mean = jnp.mean(scaled * values, axis=-1, keepdims=True)
    return (factor * scaled - values * (factor * factor * factor) * inner_mean, gain_grad)


def both_halves(mine):
    return mine, swap_cores(mine)


def dot(a, b):
    return jnp.dot(a, b, preferred_element_type=jnp.float32)


def dot_nt(a, b):
    return lax.dot_general(a, b, (((1,), (1,)), ((), ())), preferred_element_type=jnp.float32)


def dot_tn(a, b):
    return lax.dot_general(a, b, (((0,), (0,)), ((), ())), preferred_element_type=jnp.float32)


def sum_halves(product, rows, hook=lambda value: value):
    theirs = hook(swap_cores(product(slice(rows, 2 * rows)).astype(jnp.bfloat16)))
    return product(slice(0, rows)) + theirs.astype(jnp.float32)


def tie(value, *others):
    return lax.optimization_barrier((value, *others))[0]


def layer_ahead(flat, gains, weights, first_kept, tables, place):
    gain_attn, gain_ffn = gains
    rows = flat.shape[0]
    normed, factor_attn = norm_ahead(flat, gain_attn)
    normed = both_halves(normed)
    w_qkv, w_proj = weights.near()
    kept, attended, lse = attend_ahead(normed, w_qkv, first_kept, tables, place[1:])
    attended = weights.after_attention(attended)
    theirs = low(dot(attended[rows:], w_proj))
    middle = flat + dot(attended[:rows], w_proj) + swap_cores(theirs).astype(jnp.float32)
    normed_ffn, factor_ffn = norm_ahead(middle, gain_ffn)
    normed_ffn = both_halves(normed_ffn)
    (w_wide,) = weights.wide()
    normed_ffn = (weights.before_wide(normed_ffn[0]), normed_ffn[1])
    gate_pre, upward_pre, inner = gated(normed_ffn, w_wide, place)
    inner = weights.after_wide(inner)
    (w_down,) = weights.down(inner)
    theirs = low(dot(inner[rows:], w_down))
    result = middle + dot(inner[:rows], w_down) + swap_cores(theirs).astype(jnp.float32)
    result = weights.at_end(result)
    saved = (
        flat,
        factor_attn,
        normed,
        kept,
        lse,
        attended,
        middle,
        factor_ffn,
        normed_ffn,
        gate_pre,
        upward_pre,
        inner,
    )
    return result, kept, saved, (w_qkv, w_proj, w_wide, w_down)


class Plain:
    def __init__(self, weights):
        self.weights = weights

    def near(self):
        return self.weights[:2]

    def wide(self):
        return self.weights[2:3]

    def down(self, inner):
        return self.weights[3:]

    def same(self, value):
        return value

    after_attention = before_wide = after_wide = at_end = same


class Quarters:
    def __init__(self, place, piece, first, second, before_first=(), before_second=()):
        self.slot, self.starts = place[:1], {}
        self.masks = (0, first, second, first ^ second)
        self.one = exchange(tie(piece, *before_first), first)
        self.two = exchange(tie(piece, *before_second), second)
        self.three = exchange(tie(self.one, *before_second), second)
        self.pieces = [piece, self.one, self.two, self.three]


class Tuned(Plain):
    def __init__(self, shapes, sizes, place):
        (qkv_rows, qkv_width), proj_rows, (wide_rows, wide_width), down_rows = shapes
        self.cut, self.shards = wide_rows * wide_width // FLAT, sizes[0]
        self.near_parts = (("columns", qkv_rows, (qkv_width,)), ("rows", proj_rows, (FLAT // 2,)))
        self.wide_parts = (("columns", wide_rows, (wide_width,)),)
        self.down_parts = (("rows", down_rows, (FLAT // 2,)),)
        self.join = lambda q, parts, after=(): join(
            q.pieces, q.masks, q.slot, sizes, parts, q.starts.get(parts[0][0]), after
        )

    def split(self, far):
        far = far.reshape(self.shards, -1, FLAT)
        return (f.reshape(-1, FLAT) for f in (far[:, : self.cut], far[:, self.cut :]))

    def near(self):
        return self.join(self.near_way, self.near_parts)

    def wide(self):
        return self.join(self.wide_way, self.wide_parts)

    def down(self, inner):
        return self.join(self.down_way, self.down_parts, (inner,))


class Halves:
    def __init__(self, place, pieces, before):
        self.slot, self.starts = 2 * half_of(place[:1]), {}
        self.masks = (0, 1, 2, 3)
        self.one, self.two = exchange(tie(pieces[0], *before), 1), exchange(pieces[1], 2)
        self.pieces = [*pieces, self.one, self.two]


def half_of(rep):
    return lax.bitwise_xor(rep, rep // 2) % 2


def first_ways(layer, near, far, place):
    near = Quarters(place, near, 1, 2)
    wide, down = layer.split(tie(far, near.one, near.two, near.three))
    return near, Quarters(place, wide, 2, 1), Quarters(place, down, 1, 2)


def second_ways(layer, near, far, wide_one, down_one, place):
    near = Quarters(place, near, 2, 1, (down_one.two,), (wide_one.one,))
    wide, down = zip(*[layer.split(f) for f in far])
    wide = Halves(place, wide, (near.two, near.three))
    return near, wide, Halves(place, down, (near.two, near.three))


def layer_back(upstream, gains, weights, saved, extra, tables, place, send, hooks):
    gain_attn, gain_ffn = gains
    w_qkv, w_proj, w_wide, w_down = weights
    (
        flat,
        factor_attn,
        normed,
        kept,
        lse,
        attended,
        middle,
        factor_ffn,
        normed_ffn,
        gate_pre,
        upward_pre,
        inner,
    ) = saved
    rows = flat.shape[0]
    mine, other = both_halves(low(upstream))
    grad_down = hooks.start(mine), other
    grad_down = hooks.after_down(hooks.after(grad_down[0], send.down(inner, grad_down))), grad_down[1]
    grad_wide = hooks.before_wide(gated_back(grad_down, w_down, gate_pre, upward_pre, place))
    grad_wide = hooks.after_wide(hooks.after(grad_wide, send.wide(normed_ffn, grad_wide)))
    grad_normed_ffn = sum_halves(lambda part: dot_nt(grad_wide[part], w_wide), rows)
    grad_part_ffn, grad_gain_ffn = norm_back(middle, factor_ffn, gain_ffn, grad_normed_ffn)
    grad_middle = upstream + grad_part_ffn
    mine, other = both_halves(low(grad_middle))
    grad_branch = hooks.before_branch(mine), other
    mine, other = (low(dot_nt(g, w_proj)) for g in grad_branch)
    mine = hooks.before_attention(hooks.after(mine, send.proj(attended, grad_branch)))
    grad_qkv, passed = attend_back(kept, (mine, other), lse, extra, tables, place[1:])
    grad_qkv = hooks.before_qkv(grad_qkv)
    grad_qkv = hooks.after_qkv(hooks.after(grad_qkv, send.qkv(normed, grad_qkv)))
    grad_normed = sum_halves(lambda part: dot_nt(grad_qkv[part], w_qkv), rows, hooks.before_norm)
    grad_part_attn, grad_gain_attn = norm_back(flat, factor_attn, gain_attn, grad_normed)
    grad_flat = hooks.at_end(grad_middle + grad_part_attn)
    return grad_flat, (grad_gain_attn, grad_gain_ffn), passed


class Hooks:
    def same(self, value):
        return value

    start = before_norm = before_branch = after_down = before_wide = after_wide = before_attention = before_qkv = after_qkv = at_end = same

    def after(self, value, other):
        return value if other is None else tie(value, other)


def sum_over(x, axes):
    for axis in axes:
        count, mask = lax.axis_size(axis), 1
        while mask < count:
            x = x + lax.ppermute(x, axis, [(i, i ^ mask) for i in range(count)])
            mask *= 2
    return x


def shards(inputs, documents, *rest):
    masters_one, masters_two, cotangent = rest[:9], rest[9:18], rest[18]
    batch, rows, features = inputs.shape
    reps, sizes = lax.axis_size("rep"), (lax.axis_size("shard"), lax.axis_size("seq"))
    assert batch == 1 and sizes[1] == 2
    core, rep = lax.axis_index("seq"), lax.axis_index("rep")
    rows_owned = masters_one[1].shape[0]
    tuned = reps == 4 and rows_owned == LANES
    length = sizes[1] * rows
    frequencies = rope_base ** (-(jnp.arange(HD // 2, dtype=jnp.float32) * 2.0 / HD))
    angles = jnp.arange(length, dtype=jnp.float32)[:, None] * frequencies[None, :]
    cosine, sine = jnp.cos(angles), jnp.sin(angles)
    tables = (
        jnp.tile(cosine, (1, LANES * 2 // HD)),
        jnp.tile(jnp.concatenate([-sine, sine], axis=1), (1, LANES // HD)),
        documents.reshape(length, 1),
        documents.reshape(1, length),
    )
    gain_rows = jnp.stack([masters_one[0], masters_one[5], masters_two[0], masters_two[5]]).astype(
        jnp.bfloat16
    )
    flat = inputs.reshape(rows, features).astype(jnp.float32)
    place = jnp.stack([rep, core]).astype(jnp.int32)
    if tuned:
        gain_list = [masters_one[0], masters_one[5], masters_two[0], masters_two[5]]
        near_one = gather_near(masters_one[1:4], masters_one[4], gain_list, sizes[0], place)
        far_one = gather_far(masters_one[6:8], masters_one[8], sizes[0], place)
        near_two = gather_near(masters_two[1:4], masters_two[4], [], sizes[0], place)
        quarter_of = 2 * half_of(rep)
        far_two = [
            gather_far(
                masters_two[6:8], masters_two[8], sizes[0], jnp.stack([quarter_of + u, core]).astype(jnp.int32)
            )
            for u in range(2)
        ]
        ready = (far_one, near_two, *far_two)
        near_one, far_one, near_two = gather_shard(near_one), gather_shard(far_one), gather_shard(near_two)
        far_two = [gather_shard(f) for f in far_two]
        near_one = tie(near_one, *ready)
        gains = near_one.reshape(sizes[0], -1, FLAT)[:, -16:-12, : 2 * LANES]
        gains = gains.transpose(1, 0, 2).reshape(4, features).astype(jnp.float32)
        quarter, columns = rows_owned // 4 * 2, sizes[0] * LANES
        shapes = (
            (quarter, 3 * columns),
            rows_owned,
            (quarter, 2 * sizes[0] * masters_one[8].shape[0]),
            masters_one[8].shape[0],
        )
        first, second = Tuned(shapes, sizes, place), Tuned(shapes, sizes, place)
        near, wide, down = ways_one = first_ways(first, near_one, far_one, place)
        first.near_way, first.wide_way, first.down_way = ways_one
        ways = second_ways(second, near_two, far_two, wide, down, place)
        second.near_way, second.wide_way, second.down_way = ways
        first.after_attention = lambda value: tie(value, near_two, wide.one, wide.two, down.one, down.two)
        first.before_wide = lambda value: tie(value, far_two[0])
        first.after_wide = lambda value: tie(value, far_two[1], ways[0].one, ways[0].two)
        first.at_end = lambda value: tie(value, ways[0].three)
        second.after_attention = lambda value: tie(value, ways[1].one, ways[1].two)
    else:
        gains = lax.all_gather(gain_rows, ("shard", "seq"), axis=1, tiled=True).astype(jnp.float32)
        first, second = (Plain(gather_plain(m, sizes, core)) for m in (masters_one, masters_two))
    middle_one, first_kept, saved_one, weights_one = layer_ahead(
        flat, (gains[0:1], gains[1:2]), first, None, tables, place
    )
    final, _, saved_two, weights_two = layer_ahead(
        middle_one, (gains[2:3], gains[3:4]), second, first_kept, tables, place
    )
    outputs = final.astype(jnp.bfloat16).reshape(batch, rows, features)
    upstream = cotangent.reshape(rows, features).astype(jnp.float32)
    hooks_two, hooks_one = Hooks(), Hooks()
    if tuned:
        two, one = TunedSender(sizes, place, (1, 2), (2, 1)), TunedSender(sizes, place, (1, 2), (2, 1))

        def at(*steps):
            def hook(value):
                for step in steps:
                    done = step(value)
                    value = tie(value, *(done if isinstance(done, tuple) else (done,)))
                return value

            return hook

        hooks_two.before_attention = at(two.got("way_wide"))
        hooks_two.before_qkv = at(two.half("way_wide"), two.half("way_proj", 1))
        hooks_two.after_qkv = at(two.got("way_wide"), two.got("way_proj"))
        hooks_one.start = at(two.scatter_wide, two.down_way)
        hooks_one.after_down = at(two.half("way_qkv"), two.half("way_down", 1))
        hooks_one.before_wide = at(two.got("way_qkv"), two.got("way_down"))
        hooks_one.after_wide = at(two.scatter_near)
        hooks_one.before_attention = at(one.half("way_wide"), one.down_way)
        hooks_one.before_qkv = at(
            lambda value: two.near_sum,
            two.share_far,
            one.half("way_proj", 1),
            one.scatter_wide,
            one.half("way_down", 1),
        )
        hooks_one.after_qkv = at(two.far_got, one.got("way_down"))
        hooks_one.before_norm = at(one.half("way_qkv"))
    else:
        two, one = PlainSender(sizes, core), PlainSender(sizes, core)
    grad_middle, gains_two, extra = layer_back(
        upstream, (gains[2:3], gains[3:4]), weights_two, saved_two, None, tables, place, two, hooks_two
    )
    grad_flat, gains_one, _ = layer_back(
        grad_middle, (gains[0:1], gains[1:2]), weights_one, saved_one, extra, tables, place, one, hooks_one
    )
    gain_grads = jnp.stack([*gains_one, *gains_two])
    if tuned:
        gain_total = sum_over(gain_grads, ("shard", "seq", "rep"))
        value = at(one.got("way_qkv"), one.got("way_proj"), one.share_far, one.scatter_near)(tie(grad_flat, outputs))
        at(two.pick_far, two.finish_far, two.share_near)(value)
        one.pick_far(value, two.far[0])
        two.pick_near(value, two.far[0])
        at(one.finish_far, two.finish_near, one.share_near)(value)
        one.pick_near(value, two.near[0], one.far[0], gain_total)
        one.finish_near(value)
        near_two, far_two, near_one, far_one = two.near, two.far, one.near, one.far
    else:
        gain_total = sum_over(gain_grads, ("shard", "seq", "rep"))
        near_two, far_two, near_one, far_one = two.near(), two.far(), one.near(), one.far()
    grad_input = grad_flat.reshape(batch, rows, features)
    block = features // (sizes[0] * sizes[1])
    mine = lax.axis_index("shard") * sizes[1] + core
    own = lax.dynamic_slice_in_dim(gain_total, mine * block, block, 1)

    def ordered(gain_attn, gain_ffn, near, far):
        (query, key, value, proj), (gate, upward, down) = near, far
        return (gain_attn, query, key, value, proj, gain_ffn, gate, upward, down)

    return (
        (outputs, grad_input)
        + ordered(own[0], own[1], near_one, far_one)
        + ordered(own[2], own[3], near_two, far_two)
    )


def solution(mesh):
    tokens = P(("rep", "shard"), "seq", None)
    vector, matrix = P(("shard", "seq")), P(("shard", "seq"), None)
    layer = (vector, matrix, matrix, matrix, matrix, vector, matrix, matrix, matrix)
    return jax.shard_map(
        shards,
        mesh=mesh,
        in_specs=(tokens, P(("rep", "shard"), None), *layer, *layer, tokens),
        out_specs=(tokens, tokens, *layer, *layer),
        check_vma=False,
    )
```

```python
import functools
import jax
import jax.numpy as jnp
from jax import lax
from jax.experimental import pallas as pl
from jax.experimental.pallas import tpu as pltpu
from jax.sharding import PartitionSpec as P

HD = 64
BLOCK = 256
LANES = 128
FLAT = 512
eps_norm = 1e-05
rope_base = 10000.0
mask_fill = -1000000000.0


def window(block):
    return max(0, block - 2)


def swap_halves(x):
    lane = lax.broadcasted_iota(jnp.int32, x.shape, 1)
    ahead = pltpu.roll(x, LANES - HD // 2, axis=1)
    behind = pltpu.roll(x, HD // 2, axis=1)
    return jnp.where(lane % HD < HD // 2, ahead, behind)


def fill_bias(bias, docs_column, docs_row, blocks):
    at = 0
    for i in range(blocks):
        first = window(i)
        rows = (i + 1 - first) * BLOCK
        same = (
            docs_column[pl.ds(first * BLOCK, rows), 0:1]
            == docs_row[0:1, pl.ds(i * BLOCK, BLOCK)]
        )
        bias[pl.ds(at, rows), :] = jnp.where(same, 0.0, mask_fill)
        at += rows


def block_of(mine_ref, other_ref, block, blocks, half):
    own, rows = block // (blocks // 2), pl.ds(block % (blocks // 2) * BLOCK, BLOCK)
    return jnp.where(half == own, mine_ref[rows, :], other_ref[rows, :])


def ahead_kernel(blocks, mixed, half_ref, mine_ref, other_ref, weight_ref, *rest):
    if mixed:
        first_ref, rest = rest[0], rest[1:]
    cos_ref, sin_ref, column_ref, row_ref, kept_ref, out_ref, lse_ref, bias = rest
    spin = half_ref[0] * (blocks // 2)

    @pl.when(pl.program_id(0) == 0)
    def _():
        fill_bias(bias, column_ref, row_ref, blocks)

    def place(b):
        return pl.multiple_of(lax.rem(b + spin, blocks) * BLOCK, BLOCK)

    for b in range(blocks):
        rows = pl.ds(b * BLOCK, BLOCK)
        cosine, sine = cos_ref[rows, :], sin_ref[rows, :]
        tokens = block_of(mine_ref, other_ref, b, blocks, half_ref[0])
        raw = jnp.dot(tokens, weight_ref[...], preferred_element_type=jnp.float32)
        for part in range(2):
            one = raw[:, part * LANES : (part + 1) * LANES]
            turned = one * cosine + swap_halves(one) * sine
            kept_ref[rows, part * LANES : (part + 1) * LANES] = turned.astype(jnp.bfloat16)
        value = raw[:, 2 * LANES :]
        if mixed:
            value = 0.5 * value + 0.5 * first_ref[rows, 2 * LANES :].astype(jnp.float32)
        kept_ref[rows, 2 * LANES :] = value.astype(jnp.bfloat16)

    value_turned = kept_ref[:, 2 * LANES :].T
    head_lane = lax.broadcasted_iota(jnp.int32, (BLOCK, LANES), 1) // HD
    at = 0
    for i in range(blocks):
        first = window(i)
        count = (i + 1 - first) * BLOCK
        rows = pl.ds(i * BLOCK, BLOCK)
        query = kept_ref[rows, 0:LANES] * jnp.bfloat16(HD**-0.5)
        keys = kept_ref[pl.ds(first * BLOCK, count), LANES : 2 * LANES]
        fill = bias[pl.ds(at, count), :]
        at += count
        outs = []
        for head in range(LANES // HD):
            one = jnp.where(head_lane == head, query, jnp.bfloat16(0))
            scores = (
                lax.dot_general(keys, one, (((1,), (1,)), ((), ())), preferred_element_type=jnp.float32)
                + fill
            )
            top = jnp.max(scores, axis=0, keepdims=True)
            powers = jnp.exp(scores - top)
            total = jnp.sum(powers, axis=0, keepdims=True)
            weights = (powers * (1.0 / total)).astype(jnp.bfloat16)
            outs.append(
                jnp.dot(
                    value_turned[head * HD : (head + 1) * HD, first * BLOCK : first * BLOCK + count],
                    weights,
                    preferred_element_type=jnp.float32,
                )
            )
            lse_ref[0, head : head + 1, rows] = top + jnp.log(total)
        merged = jnp.concatenate(outs, axis=0)
        out_ref[pl.ds(place(i), BLOCK), :] = merged.T.astype(jnp.bfloat16)


def back_kernel(blocks, mixed, half_ref, kept_ref, mine_ref, other_ref, lse_ref, *rest):
    if not mixed:
        extra_ref, rest = rest[0], rest[1:]
    cos_ref, sin_ref, column_ref, row_ref, out_ref, *rest = rest
    if mixed:
        passed_ref, rest = rest[0], rest[1:]
    bias, key_sum, value_sum = rest
    spin = half_ref[0] * (blocks // 2)

    @pl.when(pl.program_id(0) == 0)
    def _():
        fill_bias(bias, column_ref, row_ref, blocks)

    def place(b):
        return pl.multiple_of(lax.rem(b + spin, blocks) * BLOCK, BLOCK)

    def unrotate(x, rows):
        return x * cos_ref[rows, :] - swap_halves(x) * sin_ref[rows, :]

    keys_turned = kept_ref[:, LANES : 2 * LANES].T
    head_lane = lax.broadcasted_iota(jnp.int32, (BLOCK, LANES), 1) // HD
    at = 0
    for i in range(blocks):
        first = window(i)
        count = (i + 1 - first) * BLOCK
        rows = pl.ds(i * BLOCK, BLOCK)
        span = pl.ds(first * BLOCK, count)
        query = kept_ref[rows, 0:LANES] * jnp.bfloat16(HD**-0.5)
        grad = block_of(mine_ref, other_ref, i, blocks, half_ref[0])
        keys = kept_ref[span, LANES : 2 * LANES]
        values = kept_ref[span, 2 * LANES :]
        fill = bias[pl.ds(at, count), :]
        at += count
        outs = []
        key_add, value_add = [], []
        for head in range(LANES // HD):
            pick = head_lane == head
            one = jnp.where(pick, query, jnp.bfloat16(0))
            grad_one = jnp.where(pick, grad, jnp.bfloat16(0))
            scores = (
                lax.dot_general(keys, one, (((1,), (1,)), ((), ())), preferred_element_type=jnp.float32)
                + fill
            )
            weights = jnp.exp(scores - lse_ref[0, head : head + 1, rows])
            grad_weights = lax.dot_general(
                values, grad_one, (((1,), (1,)), ((), ())), preferred_element_type=jnp.float32
            )
            delta = jnp.sum(weights * grad_weights, axis=0, keepdims=True)
            grad_scores = (weights * (grad_weights - delta)).astype(jnp.bfloat16)
            value_add.append(
                jnp.dot(weights.astype(jnp.bfloat16), grad_one, preferred_element_type=jnp.float32)
            )
            key_add.append(jnp.dot(grad_scores, one, preferred_element_type=jnp.float32))
            outs.append(
                jnp.dot(
                    keys_turned[head * HD : (head + 1) * HD, first * BLOCK : first * BLOCK + count],
                    grad_scores,
                    preferred_element_type=jnp.float32,
                )
            )
        key_add, value_add = sum(key_add[1:], key_add[0]), sum(value_add[1:], value_add[0])
        old = count - BLOCK
        if old:
            key_sum[pl.ds(first * BLOCK, old), :] += key_add[:old]
            value_sum[pl.ds(first * BLOCK, old), :] += value_add[:old]
        key_sum[rows, :] = key_add[old:]
        value_sum[rows, :] = value_add[old:]
        grad_query = jnp.concatenate(outs, axis=0).T * HD**-0.5
        out_ref[pl.ds(place(i), BLOCK), 0:LANES] = unrotate(grad_query, rows).astype(jnp.bfloat16)
    for b in range(blocks):
        rows = pl.ds(b * BLOCK, BLOCK)
        there = pl.ds(place(b), BLOCK)
        out_ref[there, LANES : 2 * LANES] = unrotate(key_sum[rows, :], rows).astype(jnp.bfloat16)
        value_grad = value_sum[rows, :]
        if mixed:
            value_grad = 0.5 * value_grad
            passed_ref[rows, :] = value_grad
        else:
            value_grad = value_grad + extra_ref[rows, :]
        out_ref[there, 2 * LANES :] = value_grad.astype(jnp.bfloat16)


def bias_rows(blocks):
    return sum(i + 1 - window(i) for i in range(blocks)) * BLOCK


def whole(shape):
    return pl.BlockSpec(shape, lambda h, s: (0,) * len(shape))


def attend_ahead(tokens, weight, first_kept, tables, half):
    cosine, sine, column, row = tables
    length, width = 2 * tokens[0].shape[0], weight.shape[1]
    pairs, blocks = width // (3 * LANES), length // BLOCK
    mixed = first_kept is not None
    wide = pl.BlockSpec((length, 3 * LANES), lambda h, s: (0, h))
    slim = pl.BlockSpec((length, LANES), lambda h, s: (0, h))
    return pl.pallas_call(
        functools.partial(ahead_kernel, blocks, mixed),
        out_shape=(
            jax.ShapeDtypeStruct((length, width), jnp.bfloat16),
            jax.ShapeDtypeStruct((length, pairs * LANES), jnp.bfloat16),
            jax.ShapeDtypeStruct((pairs, LANES // HD, length), jnp.float32),
        ),
        grid_spec=pltpu.PrefetchScalarGridSpec(
            num_scalar_prefetch=1,
            grid=(pairs,),
            in_specs=[whole(tokens[0].shape)] * 2
            + [pl.BlockSpec((weight.shape[0], 3 * LANES), lambda h, s: (0, h))]
            + ([wide] if mixed else [])
            + [whole(cosine.shape), whole(sine.shape), whole(column.shape), whole(row.shape)],
            out_specs=(wide, slim, pl.BlockSpec((1, LANES // HD, length), lambda h, s: (h, 0, 0))),
            scratch_shapes=[pltpu.VMEM((bias_rows(blocks), BLOCK), jnp.float32)],
        ),
        compiler_params=pltpu.CompilerParams(dimension_semantics=("arbitrary",), vmem_limit_bytes=48 << 20),
        cost_estimate=pl.CostEstimate(flops=0, transcendentals=0, bytes_accessed=0),
        name="attend_ahead",
    )(half, *tokens, weight, *((first_kept,) if mixed else ()), cosine, sine, column, row)


def attend_back(kept, grad, lse, extra, tables, half):
    cosine, sine, column, row = tables
    length, width = kept.shape
    pairs, blocks = width // (3 * LANES), length // BLOCK
    mixed = extra is None
    wide = pl.BlockSpec((length, 3 * LANES), lambda h, s: (0, h))
    slim = pl.BlockSpec((length, LANES), lambda h, s: (0, h))
    outs = [jax.ShapeDtypeStruct((length, width), jnp.bfloat16)]
    out_specs = [wide]
    if mixed:
        outs.append(jax.ShapeDtypeStruct((length, pairs * LANES), jnp.float32))
        out_specs.append(slim)
    result = pl.pallas_call(
        functools.partial(back_kernel, blocks, mixed),
        out_shape=tuple(outs),
        grid_spec=pltpu.PrefetchScalarGridSpec(
            num_scalar_prefetch=1,
            grid=(pairs,),
            in_specs=[wide]
            + [pl.BlockSpec((length // 2, LANES), lambda h, s: (0, h))] * 2
            + [pl.BlockSpec((1, LANES // HD, length), lambda h, s: (h, 0, 0))]
            + ([] if mixed else [slim])
            + [whole(cosine.shape), whole(sine.shape), whole(column.shape), whole(row.shape)],
            out_specs=tuple(out_specs),
            scratch_shapes=[
                pltpu.VMEM((bias_rows(blocks), BLOCK), jnp.float32),
                pltpu.VMEM((length, LANES), jnp.float32),
                pltpu.VMEM((length, LANES), jnp.float32),
            ],
        ),
        compiler_params=pltpu.CompilerParams(dimension_semantics=("arbitrary",), vmem_limit_bytes=48 << 20),
        cost_estimate=pl.CostEstimate(flops=0, transcendentals=0, bytes_accessed=0),
        name="attend_back",
    )(half, kept, *grad, lse, *(() if mixed else (extra,)), cosine, sine, column, row)
    return result if mixed else (result[0], None)


def swap_cores(x):
    return lax.ppermute(x, "seq", [(0, 1), (1, 0)])


def exchange(x, mask):
    count = lax.axis_size("rep")
    return lax.ppermute(x, "rep", [(i, i ^ mask) for i in range(count)])


def unflat(read, rows, columns, write):
    at = 0
    for i in range(columns // FLAT):
        write(0, i * FLAT, read(at, rows, 0, FLAT))
        at += rows
    left = columns % FLAT
    if left:
        step = rows * left // FLAT
        for i in range(FLAT // left):
            write(i * step, columns - left, read(at, step, i * left, left))
        at += step
    return at


def join_kernel(masks, parts, cores, slot_ref, *refs):
    pieces, outs = refs[: len(masks)], refs[-sum(len(w) if k == "columns" else 1 for k, _, w in parts) :]
    for mask, piece in zip(masks, pieces):
        slot = lax.bitwise_xor(slot_ref[0], mask)
        base, at = 0, 0
        for kind, rows, widths in parts:
            columns = sum(widths)

            def read(row, count, column, width, base=base):
                return piece[0, base + row : base + row + count, column : column + width]

            def write(row, column, values, kind=kind, rows=rows, widths=widths, at=at):
                if kind == "columns":
                    one = rows // cores
                    left, which = column, 0
                    while left >= widths[which]:
                        left, which = left - widths[which], which + 1
                    took, offset = 0, column
                    while took < values.shape[1]:
                        size = min(widths[which] - left, values.shape[1] - took)
                        count = values.shape[0]
                        for done in range(0, count, min(one, count)):
                            core, inside = divmod(row + done, one)
                            size_rows = min(one, count)
                            outs[at + which][0, core, slot, inside : inside + size_rows, left : left + size] = (
                                values[done : done + size_rows, took : took + size]
                            )
                        took, left, which = took + size, 0, which + 1
                else:
                    there = pl.ds(pl.multiple_of(slot * columns, columns) + column, values.shape[1])
                    outs[at][0, row : row + values.shape[0], there] = values

            base += unflat(read, rows, columns, write)
            at += len(widths) if kind == "columns" else 1


def join(pieces, masks, slot, sizes, parts, start=None, after=()):
    groups, cores = sizes
    count, rows = len(masks), pieces[0].shape[0] // groups
    read = rows if start is None else sum(h * sum(w) for _, h, w in parts) // FLAT
    at = 0 if start is None else start // read
    shapes = []
    for kind, height, widths in parts:
        if kind == "columns":
            shapes += [(groups, cores, count, height // cores, w) for w in widths]
        else:
            shapes.append((groups, height, count * widths[0]))
    outs = pl.pallas_call(
        functools.partial(join_kernel, masks, parts, cores),
        out_shape=[jax.ShapeDtypeStruct(s, jnp.bfloat16) for s in shapes],
        grid_spec=pltpu.PrefetchScalarGridSpec(
            num_scalar_prefetch=1,
            grid=(groups,),
            in_specs=[pl.BlockSpec((1, read, FLAT), lambda g, s: (g, at, 0))] * count
            + [pl.BlockSpec(memory_space=pl.ANY)] * len(after),
            out_specs=[
                pl.BlockSpec((1, *s[1:]), lambda g, t, n=len(s): (g,) + (0,) * (n - 1)) for s in shapes
            ],
        ),
        cost_estimate=pl.CostEstimate(flops=0, transcendentals=0, bytes_accessed=0),
        name="join",
    )(slot, *[p.reshape(groups, rows, FLAT) for p in pieces], *after)
    return [o.reshape(-1, o.shape[-1]) for o in outs]


def core_columns(rows, sizes, core):
    shards, cores = sizes
    width = rows.shape[1] // (shards * cores)
    even, odd = (
        jnp.concatenate(
            [rows[:, (s * cores + c) * width : (s * cores + c + 1) * width] for s in range(shards)],
            axis=1,
        )
        for c in range(cores)
    )
    return jnp.where(core == 0, even, odd), jnp.where(core == 0, odd, even)


def head_major(parts):
    pairs = parts[0].shape[1] // LANES
    return jnp.concatenate(
        [p[:, i * LANES : (i + 1) * LANES] for i in range(pairs) for p in parts], axis=1
    )


def head_minor(joined):
    pairs = joined.shape[1] // (3 * LANES)
    return [
        jnp.concatenate(
            [
                joined[:, (3 * i + j) * LANES : (3 * i + j + 1) * LANES]
                for i in range(pairs)
            ],
            axis=1,
        )
        for j in range(3)
    ]


def chip_rows(rows_of, sizes, core):
    mine, theirs = rows_of
    other = swap_cores(theirs)
    return jnp.concatenate(
        [jnp.where(core == 0, mine, other), jnp.where(core == 0, other, mine)], axis=0
    )


def gather_shard(x):
    return lax.all_gather(x, "shard", axis=0, tiled=True)


def column_parts(weights, sizes, core, interleave):
    mine, theirs = zip(*[core_columns(w.astype(jnp.bfloat16), sizes, core) for w in weights])
    if interleave:
        return head_major(mine), head_major(theirs)
    return jnp.concatenate(mine, axis=1), jnp.concatenate(theirs, axis=1)


def gather_plain(masters, sizes, core):
    _, w_query, w_key, w_value, w_proj, _, w_gate, w_upward, w_down = masters
    w_qkv = gather_shard(chip_rows(column_parts((w_query, w_key, w_value), sizes, core, True), sizes, core))
    w_wide = gather_shard(chip_rows(column_parts((w_gate, w_upward), sizes, core, False), sizes, core))
    w_proj, w_down = (gather_shard(w.astype(jnp.bfloat16)) for w in (w_proj, w_down))
    return w_qkv, w_proj, w_wide, w_down


def call(kernel, outs, grid, in_specs, out_specs, name, scratch=(), scalars=1):
    return pl.pallas_call(
        kernel,
        out_shape=outs,
        grid_spec=pltpu.PrefetchScalarGridSpec(
            num_scalar_prefetch=scalars,
            grid=grid,
            in_specs=in_specs,
            out_specs=out_specs,
            scratch_shapes=scratch,
        ),
        compiler_params=pltpu.CompilerParams(
            dimension_semantics=("arbitrary",) * len(grid), vmem_limit_bytes=56 << 20
        ),
        cost_estimate=pl.CostEstimate(flops=0, transcendentals=0, bytes_accessed=0),
        name=name,
    )


def fixed(shape):
    return pl.BlockSpec(shape, lambda *ids: (0,) * len(shape))


def low(values):
    return values.astype(jnp.bfloat16)


def near_split_kernel(shards, place_ref, *refs):
    weights, gains, (mine, theirs) = refs[:3], refs[3:-2], refs[-2:]
    core = place_ref[1]
    for out, which in ((mine, core), (theirs, 1 - core)):
        for s in range(shards):
            there = pl.ds(pl.multiple_of((2 * s + which) * LANES, LANES), LANES)
            for j, weight in enumerate(weights):
                out[:, (3 * s + j) * LANES : (3 * s + j + 1) * LANES] = low(weight[:, there])
        if gains:
            rows = jnp.concatenate([g[...] for g in gains] + [jnp.zeros((16 - len(gains), LANES), jnp.float32)], axis=0)
            out[0:16, 3 * shards * LANES :] = low(rows)


def near_merge_kernel(place_ref, mine, theirs, proj, out):
    core = place_ref[1]
    rows = mine.shape[0]
    for j in range(3):
        for part, which in ((mine, core), (theirs, 1 - core)):
            there = pl.ds(pl.multiple_of((2 * j + which) * rows, rows), rows)
            out[there, :] = part[:, j * FLAT : (j + 1) * FLAT]
    half = proj.shape[0] // 2
    start = 6 * rows
    out[start : start + half, 0 : FLAT // 2] = low(proj[0:half, :])
    out[start : start + half, FLAT // 2 :] = low(proj[half:, :])
    if out.shape[0] > start + half:
        out[start + half :, :] = jnp.zeros((16, FLAT), jnp.bfloat16)
        for part, which in ((mine, core), (theirs, 1 - core)):
            there = pl.ds(pl.multiple_of(which * LANES, LANES), LANES)
            out[start + half :, there] = part[0:16, 3 * FLAT : 3 * FLAT + LANES]


def far_split_kernel(shards, place_ref, gate, upward, mine, theirs):
    core = place_ref[1]
    width = gate.shape[1] // (2 * shards)
    for at, weight in enumerate((gate, upward)):
        even, odd = (
            low(jnp.concatenate([weight[:, (2 * s + c) * width : (2 * s + c + 1) * width] for s in range(shards)], axis=1))
            for c in range(2)
        )
        there = slice(at * shards * width, (at + 1) * shards * width)
        mine[:, there] = jnp.where(core == 0, even, odd)
        theirs[:, there] = jnp.where(core == 0, odd, even)


def far_merge_kernel(place_ref, mine, theirs, down, out):
    core = place_ref[1]
    rows, columns = mine.shape
    blocks = columns // FLAT
    for part, which in ((mine, core), (theirs, 1 - core)):
        for j in range(blocks):
            there = pl.ds(pl.multiple_of((2 * j + which) * rows, rows), rows)
            out[there, :] = part[:, j * FLAT : (j + 1) * FLAT]
        there = pl.ds(pl.multiple_of(which * (FLAT // 2), FLAT // 2), FLAT // 2)
        out[2 * blocks * rows : (2 * blocks + 1) * rows, there] = part[:, blocks * FLAT :]
    half, start = down.shape[0] // 2, (2 * blocks + 1) * rows
    out[start:, 0 : FLAT // 2] = low(down[0:half, :])
    out[start:, FLAT // 2 :] = low(down[half:, :])


def shape_of(*shape, dtype=jnp.bfloat16):
    return jax.ShapeDtypeStruct(shape, dtype)


def quarter_of_rows(weight):
    return pl.BlockSpec((weight.shape[0] // 4, weight.shape[1]), lambda i, s: (s[0], 0))


def quarter_of_columns(weight):
    return pl.BlockSpec((weight.shape[0], weight.shape[1] // 4), lambda i, s: (0, s[0]))


def gather_near(weights, proj, gains, shards, place):
    rows = weights[0].shape[0] // 4
    width = 3 * shards * LANES + (LANES if gains else 0)
    gains = [g.reshape(1, LANES) for g in gains]
    mine, theirs = call(
        functools.partial(near_split_kernel, shards),
        [shape_of(rows, width)] * 2,
        (1,),
        [quarter_of_rows(w) for w in weights] + [fixed((1, LANES))] * len(gains),
        [fixed((rows, width))] * 2,
        "near_split",
    )(place, *weights, *gains)
    total = 6 * rows + proj.shape[0] // 2 + (16 if gains else 0)
    merged = call(
        near_merge_kernel,
        shape_of(total, FLAT),
        (1,),
        [fixed((rows, width))] * 2 + [quarter_of_columns(proj)],
        fixed((total, FLAT)),
        "near_merge",
    )(place, mine, swap_cores(theirs), proj)
    return merged


def gather_far(weights, down, shards, place):
    rows, width = weights[0].shape[0] // 4, weights[0].shape[1]
    mine, theirs = call(
        functools.partial(far_split_kernel, shards),
        [shape_of(rows, width)] * 2,
        (1,),
        [quarter_of_rows(w) for w in weights],
        [fixed((rows, width))] * 2,
        "far_split",
    )(place, *weights)
    total = rows * width // (FLAT // 2) + down.shape[0] // 2
    merged = call(
        far_merge_kernel,
        shape_of(total, FLAT),
        (1,),
        [fixed((rows, width))] * 2 + [quarter_of_columns(down)],
        fixed((total, FLAT)),
        "far_merge",
    )(place, mine, swap_cores(theirs), down)
    return merged


def dot_nn(a, b):
    return jnp.dot(a, b, preferred_element_type=jnp.float32)


def halves_of_rows(tile, per_half):
    return [
        lambda i, s: (jnp.minimum(i, per_half - 1), 0),
        lambda i, s: (jnp.maximum(i - per_half, 0), 0),
    ]


def gated_kernel(per_half, none_ref, mine, other, weight, gate_out, upward_out, inner_out):
    tokens = jnp.where(pl.program_id(0) < per_half, mine[...], other[...])
    width = gate_out.shape[1]
    one, two = dot_nn(tokens, weight[:, :width]), dot_nn(tokens, weight[:, width:])
    inner_out[...] = low(one * jax.nn.sigmoid(one) * two)
    gate_out[...] = low(one)
    upward_out[...] = low(two)


def gated(tokens, weight, place):
    length, width, tile = 2 * tokens[0].shape[0], weight.shape[1] // 2, 256
    rows = pl.BlockSpec((tile, width), lambda i, s: (i, 0))
    maps = halves_of_rows(tile, length // tile // 2)
    return call(
        functools.partial(gated_kernel, length // tile // 2),
        [shape_of(length, width)] * 3,
        (length // tile,),
        [pl.BlockSpec((tile, tokens[0].shape[1]), m) for m in maps] + [fixed(weight.shape)],
        [rows] * 3,
        "gated",
    )(place, *tokens, weight)


def gated_back_kernel(per_half, none_ref, mine, other, weight, gate, upward, out):
    grad = jnp.where(pl.program_id(0) < per_half, mine[...], other[...])
    width = gate.shape[1]
    inner = lax.dot_general(grad, weight[...], (((1,), (1,)), ((), ())), preferred_element_type=jnp.float32)
    one, two = gate[...].astype(jnp.float32), upward[...].astype(jnp.float32)
    part = jax.nn.sigmoid(one)
    out[:, :width] = low(inner * two * part * (1.0 + one * (1.0 - part)))
    out[:, width:] = low(inner * one * part)


def gated_back(grad, weight, gate, upward, place):
    (length, width), tile = gate.shape, 256
    rows = pl.BlockSpec((tile, width), lambda i, s: (i, 0))
    maps = halves_of_rows(tile, length // tile // 2)
    return call(
        functools.partial(gated_back_kernel, length // tile // 2),
        shape_of(length, 2 * width),
        (length // tile,),
        [pl.BlockSpec((tile, grad[0].shape[1]), m) for m in maps] + [fixed(weight.shape), rows, rows],
        pl.BlockSpec((tile, 2 * width), lambda i, s: (i, 0)),
        "gated_back",
    )(place, *grad, weight, gate, upward)


def turned(a, b):
    return lax.dot_general(a, b, (((0,), (0,)), ((), ())), preferred_element_type=jnp.float32)


def grad_rows_kernel(bits_ref, mine, other, right, *outs):
    half, parts = mine.shape[0], len(outs) // 2
    product = turned(mine[...], right[0:half, :]) + turned(other[...], right[half:, :])
    groups, rows, width = outs[0].shape
    for part in range(parts):
        sent, kept = outs[2 * part : 2 * part + 2]
        upper, columns = bits_ref[part] == 0, slice(part * width, (part + 1) * width)
        for g in range(groups):
            one, two = (low(product[(2 * g + h) * rows : (2 * g + h + 1) * rows, columns]) for h in range(2))
            kept[g] = jnp.where(upper, one, two)
            sent[g] = jnp.where(upper, two, one)


def grad_rows(left, right, groups, bits, parts=1, tile=256):
    half, features = left[0].shape
    length, width = right.shape
    per, rows = groups * tile // features, features // groups // 2
    out = pl.BlockSpec((per, rows, width // parts), lambda i, s: (i, 0, 0))
    return call(
        grad_rows_kernel,
        [shape_of(groups, rows, width // parts)] * (2 * parts),
        (features // tile,),
        [pl.BlockSpec((half, tile), lambda i, s: (0, i))] * 2 + [fixed((length, width))],
        [out] * (2 * parts),
        "grad_rows",
    )(bits, *left, right)


def grad_whole_kernel(none_ref, left, mine, other, out):
    half = mine.shape[0]
    out[...] = low(turned(left[0:half, :], mine[...]) + turned(left[half:, :], other[...]))


def grad_whole(left, right, place, steps=2):
    length, rows = left.shape
    half, width = right[0].shape
    side = pl.BlockSpec((half, width // steps), lambda i, s: (0, i))
    return call(
        grad_whole_kernel,
        shape_of(rows, width),
        (steps,),
        [fixed((length, rows)), side, side],
        pl.BlockSpec((rows, width // steps), lambda i, s: (0, i)),
        "grad_whole",
    )(place, left, *right)


def grad_columns_kernel(bits_ref, left, mine, other, sent, kept):
    half = mine.shape[0]
    product = low(turned(left[0:half, :], mine[...]) + turned(left[half:, :], other[...]))

    @pl.when(pl.program_id(0) == 0)
    def _():
        sent[...] = product

    @pl.when(pl.program_id(0) == 1)
    def _():
        kept[...] = product


def grad_columns(left, right, bits):
    length, rows = left.shape
    half, width = right[0].shape
    side = pl.BlockSpec((half, width // 2), lambda i, s: (0, jnp.where(i == 0, 1 - s[0], s[0])))
    return call(
        grad_columns_kernel,
        [shape_of(rows, width // 2)] * 2,
        (2,),
        [fixed((length, rows)), side, side],
        [fixed((rows, width // 2))] * 2,
        "grad_columns",
    )(bits, left, *right)


def add(a, b):
    return a + b


def halve_kernel(parts, bits_ref, *refs):
    ins, outs = refs[: 2 * parts], refs[2 * parts :]
    for part in range(parts):
        kept, got = ins[2 * part : 2 * part + 2]
        sent_out, kept_out = outs[2 * part : 2 * part + 2]
        total = add(kept[...], got[...])
        upper = bits_ref[1 - part] == 0
        middle = kept.shape[1] // 2
        one, two = total[:, :middle], total[:, middle:]
        kept_out[...] = jnp.where(upper, one, two)
        sent_out[...] = jnp.where(upper, two, one)


def halve(ins, bits, steps):
    shape, parts = ins[0].shape, len(ins) // 2
    block = (shape[0] // steps, *shape[1:])
    small = (*shape[:1], shape[1] // 2, *shape[2:])
    index = lambda i, s: (i,) + (0,) * (len(shape) - 1)
    return call(
        functools.partial(halve_kernel, parts),
        [shape_of(*small)] * (2 * parts),
        (steps,),
        [pl.BlockSpec(block, index)] * (2 * parts),
        [pl.BlockSpec((block[0], *small[1:]), index)] * (2 * parts),
        "halve",
    )(bits, *ins)


def flatten_kernel(parts, none_ref, *refs):
    bodies, tails, out = refs[: 2 * parts], refs[2 * parts : -1], refs[-1]
    sums = [add(bodies[2 * p][...], bodies[2 * p + 1][...]) for p in range(parts)]
    total = jnp.concatenate(sums, axis=2) if parts > 1 else sums[0]
    cores, rows, columns = total.shape
    blocks, left = columns // FLAT, columns % FLAT
    for j in range(blocks):
        for c in range(cores):
            there = slice((j * cores + c) * rows, (j * cores + c + 1) * rows)
            out[0, there, :] = total[c, :, j * FLAT : (j + 1) * FLAT]
    at = blocks * cores * rows
    if left:
        for c in range(cores):
            out[0, at : at + rows, c * left : (c + 1) * left] = total[c, :, columns - left :]
        at += rows
    if tails:
        tail = add(tails[0][...], tails[1][...])
        half = tail.shape[0] // 2
        out[0, at:, 0 : FLAT // 2] = tail[:half]
        out[0, at:, FLAT // 2 :] = tail[half:]


def flatten(bodies, tails, shards, bits):
    groups, rows, columns = bodies[0].shape
    height, width = tails[0].shape if tails else (0, 0)
    cores, parts = groups // shards, len(bodies) // 2
    total = (parts * cores * rows * columns + height // shards * width) // FLAT
    return call(
        functools.partial(flatten_kernel, parts),
        shape_of(shards, total, FLAT),
        (shards,),
        [pl.BlockSpec((cores, rows, columns), lambda i, s: (i, 0, 0))] * len(bodies)
        + [pl.BlockSpec((height // shards, width), lambda i, s: (i, 0))] * len(tails),
        pl.BlockSpec((1, total, FLAT), lambda i, s: (i, 0, 0)),
        "flatten",
    )(bits, *bodies, *tails).reshape(-1, FLAT)


def append_kernel(none_ref, *refs):
    bodies, (kept, got, out) = refs[:-3], refs[-3:]
    at = 0
    for body in bodies:
        out[at : at + body.shape[0], :] = body[...]
        at += body.shape[0]
    tail, half = add(kept[...], got[...]), kept.shape[0] // 2
    out[at:, 0 : FLAT // 2] = tail[:half]
    out[at:, FLAT // 2 :] = tail[half:]


def append(bodies, kept, got, bits):
    rows = sum(b.shape[0] for b in bodies) + kept.shape[0] // 2
    return call(
        append_kernel,
        shape_of(rows, FLAT),
        (1,),
        [fixed(x.shape) for x in (*bodies, kept, got)],
        fixed((rows, FLAT)),
        "append",
    )(bits, *bodies, kept, got)


def from_row(pieces, start):
    return [p.at[pl.ds(start, p.shape[0] - start)] for p in pieces] if start else pieces


def pick_kernel(blocks, rows, left, start, count, place_ref, *refs):
    pieces, out = from_row(refs[:count], start), refs[-1]
    which = 1 - place_ref[1]
    for k, piece in enumerate(pieces):
        for j in range(blocks):
            there = pl.ds(pl.multiple_of((2 * j + which) * rows, rows), rows)
            out[k, j * rows : (j + 1) * rows, :] = piece[there, :]
        if left:
            there = pl.ds(pl.multiple_of(which * left, left), left)
            out[k, blocks * rows :, 0:left] = piece[2 * blocks * rows : (2 * blocks + 1) * rows, there]
            out[k, blocks * rows :, left:] = jnp.zeros((rows, FLAT - left), jnp.bfloat16)


def pick(pieces, rows, columns, place, start, after):
    blocks, left = columns // FLAT, columns % FLAT
    total = (blocks + (left > 0)) * rows
    return call(
        functools.partial(pick_kernel, blocks, rows, left, start, len(pieces)),
        shape_of(len(pieces), total, FLAT),
        (1,),
        [fixed(pieces[0].shape)] * len(pieces) + [pl.BlockSpec(memory_space=pl.ANY)] * len(after),
        fixed((len(pieces), total, FLAT)),
        "pick",
    )(place, *pieces, *after)


def slots_of(bits_ref):
    places = []
    for one, two in ((0, 0), (1, 0), (0, 1), (1, 1)):
        first, second = lax.bitwise_xor(bits_ref[0], one), lax.bitwise_xor(bits_ref[1], two)
        places.append((2 * first + second, 2 * second + first))
    return places


def tail_out(piece, start, out, slot):
    half, columns = out.shape[0] // 2, FLAT // 2
    there = pl.ds(pl.multiple_of(slot * columns, columns), columns)
    out[0:half, there] = piece[start : start + half, 0:columns].astype(jnp.float32)
    out[half:, there] = piece[start : start + half, columns:].astype(jnp.float32)


def finish_near_kernel(shards, rows, start, bits_ref, place_ref, *refs):
    pieces, other, outs, tail = from_row(refs[:4], start), refs[4], refs[5:8], refs[8]
    core = place_ref[1]
    for k, slots in enumerate(slots_of(bits_ref)):
        for s in range(shards):
            there = pl.ds(pl.multiple_of(slots[2 * s // shards] * rows, rows), rows)
            for j, out in enumerate(outs):
                block, lane = divmod((3 * s + j) * LANES, FLAT)
                mine_rows = pl.ds(pl.multiple_of((2 * block + core) * rows, rows), rows)
                mine = pieces[k][mine_rows, lane : lane + LANES]
                theirs = other[k, block * rows : (block + 1) * rows, lane : lane + LANES]
                for part, which in ((mine, core), (theirs, 1 - core)):
                    lanes = pl.ds(pl.multiple_of((2 * s + which) * LANES, LANES), LANES)
                    out[there, lanes] = part.astype(jnp.float32)
        tail_out(pieces[k], 6 * rows, tail, slots[0])


def finish_far_kernel(shards, rows, start, bits_ref, place_ref, *refs):
    pieces, other, outs, tail = from_row(refs[:4], start), refs[4], refs[5:7], refs[7]
    core = place_ref[1]
    width = outs[0].shape[1] // (2 * shards)
    columns = 2 * shards * width
    blocks, left = columns // FLAT, columns % FLAT
    for k, slots in enumerate(slots_of(bits_ref)):
        mine = [
            pieces[k][pl.ds(pl.multiple_of((2 * j + core) * rows, rows), rows), :] for j in range(blocks)
        ]
        lanes = pl.ds(pl.multiple_of(core * left, left), left)
        mine.append(pieces[k][2 * blocks * rows : (2 * blocks + 1) * rows, lanes])
        theirs = [other[k, j * rows : (j + 1) * rows, :] for j in range(blocks)]
        theirs.append(other[k, blocks * rows :, 0:left])
        mine, theirs = (jnp.concatenate(p, axis=1).astype(jnp.float32) for p in (mine, theirs))
        even, odd = jnp.where(core == 0, mine, theirs), jnp.where(core == 0, theirs, mine)
        for at, out in enumerate(outs):
            there = pl.ds(pl.multiple_of(slots[at] * rows, rows), rows)
            parts = [
                p[:, (at * shards + s) * width : (at * shards + s + 1) * width]
                for s in range(shards)
                for p in (even, odd)
            ]
            out[there, :] = jnp.concatenate(parts, axis=1)
        tail_out(pieces[k], (2 * blocks + 1) * rows, tail, slots[0])


class Way:
    def __init__(self, halves, plan, bits):
        self.sent, self.kept = halves[::2], halves[1::2]
        self.plan, self.bits = plan, bits
        self.got = [exchange(x, plan[p]) for p, x in enumerate(self.sent)]

    def last(self, value):
        return [x for pair in zip(self.kept, self.got) for x in (tie(pair[0], value), pair[1])]

    def half(self, value, steps=2):
        outs = halve(self.last(value), self.bits, steps)
        self.sent, self.kept = outs[::2], outs[1::2]
        self.got = [exchange(x, self.plan[1 - p]) for p, x in enumerate(self.sent)]
        return tuple(self.sent)


class TunedSender:
    def __init__(self, sizes, place, near, far):
        self.sizes, self.place, self.near_plan, self.far_plan = sizes, place, near, far
        self.near_bits, self.far_bits = (
            jnp.stack([bit_of(place[0], m) for m in plan]).astype(jnp.int32) for plan in (near, far)
        )
        self.groups = sizes[0] * sizes[1]

    def down(self, left, right):
        grad = grad_whole(left, right, self.place)
        self.down_sum = scatter_shard(grad)
        return grad

    def down_way(self, value):
        reduced, bit = tie(self.down_sum, value), self.far_bits[0]
        width = reduced.shape[1] // 2
        halves = [lax.dynamic_slice_in_dim(reduced, b * width, width, 1) for b in (1 - bit, bit)]
        self.way_down = Way(halves, self.far_plan, self.far_bits)
        return halves[0]

    def wide(self, left, right):
        self.way_wide = Way(grad_rows(left, right, self.groups, self.far_bits, 2), self.far_plan, self.far_bits)
        return self.way_wide.sent[0]

    def proj(self, left, right):
        self.proj_halves = grad_columns(left, right, self.near_bits)
        return self.proj_halves[0]

    def proj_way(self, value):
        sent, kept = self.proj_halves
        self.way_proj = Way([tie(sent, value), kept], self.near_plan, self.near_bits)
        return ()

    def qkv(self, left, right):
        self.way_qkv = Way(grad_rows(left, right, self.groups, self.near_bits, 2), self.near_plan, self.near_bits)
        return self.way_qkv.sent[0]

    def half(self, name, steps=2):
        return lambda value: getattr(self, name).half(value, steps)

    def got(self, name):
        return lambda value: tuple(getattr(self, name).got)

    def scatter_wide(self, value):
        self.wide_shape = self.way_wide.kept[0].shape
        flat = flatten(self.way_wide.last(value), (), self.sizes[0], self.far_bits)
        self.wide_sum = scatter_shard(flat)
        return flat

    def scatter_near(self, value):
        self.near_shape, self.proj_height = self.way_qkv.kept[0].shape, self.way_proj.kept[0].shape[0] // self.sizes[0]
        flat = flatten(self.way_qkv.last(value), self.way_proj.last(value), self.sizes[0], self.near_bits)
        self.near_sum = scatter_shard(flat)
        return flat

    def shared(self, piece, plan):
        return [piece] + [exchange(piece, m) for m in (*plan, plan[0] ^ plan[1])]

    def share_near(self, value):
        self.near_at, self.near_pieces = 0, self.shared(tie(self.near_sum, value), self.near_plan)
        return self.near_pieces[0]

    def share_far(self, value):
        piece = append([tie(self.wide_sum, value)], self.way_down.kept[0], self.way_down.got[0], self.far_bits)
        self.far_at, self.far_pieces = 0, self.shared(piece, self.far_plan)
        return piece

    def share_all(self, value):
        bodies = [tie(self.near_sum, value), self.wide_sum]
        piece = append(bodies, self.way_down.kept[0], self.way_down.got[0], self.far_bits)
        self.near_at, self.far_at = 0, self.near_sum.shape[0]
        own, one, two, both = self.near_pieces = self.shared(piece, self.near_plan)
        self.far_pieces = [own, one, two, both] if self.near_plan == self.far_plan else [own, two, one, both]
        return piece

    def far_got(self, value):
        return tuple(self.far_pieces[1:])

    def near_got(self, value):
        return tuple(self.near_pieces[1:])

    def pick_near(self, value, *after):
        _, rows, columns = self.near_shape
        pieces = [tie(self.near_pieces[0], value), *self.near_pieces[1:]]
        picked = pick(pieces, rows, 2 * columns, self.place, self.near_at, after)
        self.near_other = swap_cores(picked)
        return picked

    def pick_far(self, value, *after):
        _, rows, columns = self.wide_shape
        pieces = [tie(self.far_pieces[0], value), *self.far_pieces[1:]]
        picked = pick(pieces, rows, 2 * columns, self.place, self.far_at, after)
        self.far_other = swap_cores(picked)
        return picked

    def finish_near(self, value):
        rows, features = self.near_shape[1], self.groups * LANES
        self.near = self.finish(
            functools.partial(finish_near_kernel, self.sizes[0], rows, self.near_at),
            [(4 * rows, features)] * 3 + [(self.proj_height, 2 * FLAT)],
            (self.near_bits, tie(self.place, value), *self.near_pieces, self.near_other),
            "finish_near",
        )
        return self.near[0]

    def finish_far(self, value):
        _, rows, columns = self.wide_shape
        self.far = self.finish(
            functools.partial(finish_far_kernel, self.sizes[0], rows, self.far_at),
            [(4 * rows, 2 * columns)] * 2 + [(self.way_down.kept[0].shape[0], 2 * FLAT)],
            (self.far_bits, tie(self.place, value), *self.far_pieces, self.far_other),
            "finish_far",
        )
        return self.far[0]

    def finish(self, kernel, shapes, operands, name):
        return call(
            kernel,
            [shape_of(*s, dtype=jnp.float32) for s in shapes],
            (1,),
            [fixed(x.shape) for x in operands[2:]],
            [fixed(s) for s in shapes],
            name,
            scalars=2,
        )(*operands)


class PlainSender:
    def __init__(self, sizes, core):
        self.sizes, self.core = sizes, core

    def total(self, grad):
        return lax.psum(scatter_shard(low(grad)), "rep")

    def down(self, left, right):
        self.down_sum = self.total(dot_tn(left, jnp.concatenate(right, axis=0)))

    def proj(self, left, right):
        self.proj_sum = self.total(dot_tn(left, jnp.concatenate(right, axis=0)))

    def wide(self, left, right):
        self.wide_sum = self.total(dot_tn(jnp.concatenate(left, axis=0), right))

    def qkv(self, left, right):
        self.qkv_sum = self.total(dot_tn(jnp.concatenate(left, axis=0), right))

    def columns(self, reduced):
        shaped = reduced.reshape(2, -1, reduced.shape[1])
        mine = lax.dynamic_index_in_dim(shaped, self.core, 0, keepdims=False)
        other = swap_cores(lax.dynamic_index_in_dim(shaped, 1 - self.core, 0, keepdims=False))
        even, odd = jnp.where(self.core == 0, mine, other), jnp.where(self.core == 0, other, mine)
        return even.astype(jnp.float32), odd.astype(jnp.float32)

    def near(self):
        even, odd = self.columns(self.qkv_sum)
        parts = [spread_columns(e, o, self.sizes) for e, o in zip(head_minor(even), head_minor(odd))]
        return (*parts, self.proj_sum.astype(jnp.float32))

    def far(self):
        even, odd = self.columns(self.wide_sum)
        width = even.shape[1] // 2
        parts = [spread_columns(even[:, at], odd[:, at], self.sizes) for at in (slice(0, width), slice(width, None))]
        return (*parts, self.down_sum.astype(jnp.float32))


def bit_of(rep, mask):
    return (rep // mask) % 2


def scatter_shard(x):
    return lax.psum_scatter(x, "shard", scatter_dimension=0, tiled=True)


def spread_columns(even, odd, sizes):
    shards, cores = sizes
    width = even.shape[1] // shards
    return jnp.concatenate(
        [p[:, s * width : (s + 1) * width] for s in range(shards) for p in (even, odd)], axis=1
    )


def norm_ahead(values, gain_row):
    factor = lax.rsqrt(jnp.mean(values * values, axis=-1, keepdims=True) + eps_norm)
    return ((values * factor * gain_row).astype(jnp.bfloat16), factor)


def norm_back(values, factor, gain_row, upstream):
    scaled = upstream * gain_row
    gain_grad = jnp.sum(upstream * values * factor, axis=0)
    inner_mean = jnp.mean(scaled * values, axis=-1, keepdims=True)
    return (factor * scaled - values * (factor * factor * factor) * inner_mean, gain_grad)


def both_halves(mine):
    return mine, swap_cores(mine)


def dot(a, b):
    return jnp.dot(a, b, preferred_element_type=jnp.float32)


def dot_nt(a, b):
    return lax.dot_general(a, b, (((1,), (1,)), ((), ())), preferred_element_type=jnp.float32)


def dot_tn(a, b):
    return lax.dot_general(a, b, (((0,), (0,)), ((), ())), preferred_element_type=jnp.float32)


def sum_halves(product, rows, hook=lambda value: value):
    theirs = hook(swap_cores(product(slice(rows, 2 * rows)).astype(jnp.bfloat16)))
    return product(slice(0, rows)) + theirs.astype(jnp.float32)


def tie(value, *others):
    return lax.optimization_barrier((value, *others))[0]


def layer_ahead(flat, gains, weights, first_kept, tables, place):
    gain_attn, gain_ffn = gains
    rows = flat.shape[0]
    normed, factor_attn = norm_ahead(flat, gain_attn)
    normed = both_halves(normed)
    w_qkv, w_proj = weights.near()
    kept, attended, lse = attend_ahead(normed, w_qkv, first_kept, tables, place[1:])
    attended = weights.after_attention(attended)
    theirs = low(dot(attended[rows:], w_proj))
    middle = flat + dot(attended[:rows], w_proj) + swap_cores(theirs).astype(jnp.float32)
    normed_ffn, factor_ffn = norm_ahead(middle, gain_ffn)
    normed_ffn = both_halves(normed_ffn)
    (w_wide,) = weights.wide()
    normed_ffn = (weights.before_wide(normed_ffn[0]), normed_ffn[1])
    gate_pre, upward_pre, inner = gated(normed_ffn, w_wide, place)
    inner = weights.after_wide(inner)
    (w_down,) = weights.down(inner)
    theirs = low(dot(inner[rows:], w_down))
    result = middle + dot(inner[:rows], w_down) + swap_cores(theirs).astype(jnp.float32)
    result = weights.at_end(result)
    saved = (
        flat,
        factor_attn,
        normed,
        kept,
        lse,
        attended,
        middle,
        factor_ffn,
        normed_ffn,
        gate_pre,
        upward_pre,
        inner,
    )
    return result, kept, saved, (w_qkv, w_proj, w_wide, w_down)


class Plain:
    def __init__(self, weights):
        self.weights = weights

    def near(self):
        return self.weights[:2]

    def wide(self):
        return self.weights[2:3]

    def down(self, inner):
        return self.weights[3:]

    def same(self, value):
        return value

    after_attention = before_wide = after_wide = at_end = same


class Quarters:
    def __init__(self, place, piece, first, second, before_first=(), before_second=()):
        self.slot, self.starts = place[:1], {}
        self.masks = (0, first, second, first ^ second)
        self.one = exchange(tie(piece, *before_first), first)
        self.two = exchange(tie(piece, *before_second), second)
        self.three = exchange(tie(self.one, *before_second), second)
        self.pieces = [piece, self.one, self.two, self.three]


class Tuned(Plain):
    def __init__(self, shapes, sizes, place):
        (qkv_rows, qkv_width), proj_rows, (wide_rows, wide_width), down_rows = shapes
        self.cut, self.shards = wide_rows * wide_width // FLAT, sizes[0]
        self.near_parts = (("columns", qkv_rows, (qkv_width,)), ("rows", proj_rows, (FLAT // 2,)))
        self.wide_parts = (("columns", wide_rows, (wide_width,)),)
        self.down_parts = (("rows", down_rows, (FLAT // 2,)),)
        self.join = lambda q, parts, after=(): join(
            q.pieces, q.masks, q.slot, sizes, parts, q.starts.get(parts[0][0]), after
        )

    def split(self, far):
        far = far.reshape(self.shards, -1, FLAT)
        return (f.reshape(-1, FLAT) for f in (far[:, : self.cut], far[:, self.cut :]))

    def near(self):
        return self.join(self.near_way, self.near_parts)

    def wide(self):
        return self.join(self.wide_way, self.wide_parts)

    def down(self, inner):
        return self.join(self.down_way, self.down_parts, (inner,))


class Halves:
    def __init__(self, place, pieces, before):
        self.slot, self.starts = 2 * half_of(place[:1]), {}
        self.masks = (0, 1, 2, 3)
        self.one, self.two = exchange(tie(pieces[0], *before), 1), exchange(pieces[1], 2)
        self.pieces = [*pieces, self.one, self.two]


def half_of(rep):
    return lax.bitwise_xor(rep, rep // 2) % 2


def first_ways(layer, near, far, place):
    near = Quarters(place, near, 1, 2)
    wide, down = layer.split(tie(far, near.one, near.two, near.three))
    return near, Quarters(place, wide, 2, 1), Quarters(place, down, 1, 2)


def second_ways(layer, near, far, wide_one, down_one, place):
    near = Quarters(place, near, 2, 1, (down_one.two,), (wide_one.one,))
    wide, down = zip(*[layer.split(f) for f in far])
    wide = Halves(place, wide, (near.two, near.three))
    return near, wide, Halves(place, down, (near.two, near.three))


def layer_back(upstream, gains, weights, saved, extra, tables, place, send, hooks):
    gain_attn, gain_ffn = gains
    w_qkv, w_proj, w_wide, w_down = weights
    (
        flat,
        factor_attn,
        normed,
        kept,
        lse,
        attended,
        middle,
        factor_ffn,
        normed_ffn,
        gate_pre,
        upward_pre,
        inner,
    ) = saved
    rows = flat.shape[0]
    mine, other = both_halves(low(upstream))
    grad_down = hooks.start(mine), other
    grad_down = hooks.after_down(hooks.after(grad_down[0], send.down(inner, grad_down))), grad_down[1]
    grad_wide = hooks.before_wide(gated_back(grad_down, w_down, gate_pre, upward_pre, place))
    grad_wide = hooks.after_wide(hooks.after(grad_wide, send.wide(normed_ffn, grad_wide)))
    grad_normed_ffn = sum_halves(lambda part: dot_nt(grad_wide[part], w_wide), rows)
    grad_part_ffn, grad_gain_ffn = norm_back(middle, factor_ffn, gain_ffn, grad_normed_ffn)
    grad_middle = upstream + grad_part_ffn
    mine, other = both_halves(low(grad_middle))
    grad_branch = hooks.before_branch(mine), other
    mine, other = (low(dot_nt(g, w_proj)) for g in grad_branch)
    mine = hooks.before_attention(hooks.after(mine, send.proj(attended, grad_branch)))
    grad_qkv, passed = attend_back(kept, (mine, other), lse, extra, tables, place[1:])
    grad_qkv = hooks.before_qkv(grad_qkv)
    grad_qkv = hooks.after_qkv(hooks.after(grad_qkv, send.qkv(normed, grad_qkv)))
    grad_normed = sum_halves(lambda part: dot_nt(grad_qkv[part], w_qkv), rows, hooks.before_norm)
    grad_part_attn, grad_gain_attn = norm_back(flat, factor_attn, gain_attn, grad_normed)
    grad_flat = hooks.at_end(grad_middle + grad_part_attn)
    return grad_flat, (grad_gain_attn, grad_gain_ffn), passed


class Hooks:
    def same(self, value):
        return value

    start = before_norm = before_branch = after_down = before_wide = after_wide = before_attention = before_qkv = after_qkv = at_end = same

    def after(self, value, other):
        return value if other is None else tie(value, other)


def sum_over(x, axes):
    for axis in axes:
        count, mask = lax.axis_size(axis), 1
        while mask < count:
            x = x + lax.ppermute(x, axis, [(i, i ^ mask) for i in range(count)])
            mask *= 2
    return x


def shards(inputs, documents, *rest):
    masters_one, masters_two, cotangent = rest[:9], rest[9:18], rest[18]
    batch, rows, features = inputs.shape
    reps, sizes = lax.axis_size("rep"), (lax.axis_size("shard"), lax.axis_size("seq"))
    assert batch == 1 and sizes[1] == 2
    core, rep = lax.axis_index("seq"), lax.axis_index("rep")
    rows_owned = masters_one[1].shape[0]
    tuned = reps == 4 and rows_owned == LANES
    length = sizes[1] * rows
    frequencies = rope_base ** (-(jnp.arange(HD // 2, dtype=jnp.float32) * 2.0 / HD))
    angles = jnp.arange(length, dtype=jnp.float32)[:, None] * frequencies[None, :]
    cosine, sine = jnp.cos(angles), jnp.sin(angles)
    tables = (
        jnp.tile(cosine, (1, LANES * 2 // HD)),
        jnp.tile(jnp.concatenate([-sine, sine], axis=1), (1, LANES // HD)),
        documents.reshape(length, 1),
        documents.reshape(1, length),
    )
    gain_rows = jnp.stack([masters_one[0], masters_one[5], masters_two[0], masters_two[5]]).astype(
        jnp.bfloat16
    )
    flat = inputs.reshape(rows, features).astype(jnp.float32)
    place = jnp.stack([rep, core]).astype(jnp.int32)
    if tuned:
        gain_list = [masters_one[0], masters_one[5], masters_two[0], masters_two[5]]
        near_one = gather_near(masters_one[1:4], masters_one[4], gain_list, sizes[0], place)
        far_one = gather_far(masters_one[6:8], masters_one[8], sizes[0], place)
        near_two = gather_near(masters_two[1:4], masters_two[4], [], sizes[0], place)
        quarter_of = 2 * half_of(rep)
        far_two = [
            gather_far(
                masters_two[6:8], masters_two[8], sizes[0], jnp.stack([quarter_of + u, core]).astype(jnp.int32)
            )
            for u in range(2)
        ]
        ready = (far_one, near_two, *far_two)
        near_one, far_one, near_two = gather_shard(near_one), gather_shard(far_one), gather_shard(near_two)
        far_two = [gather_shard(f) for f in far_two]
        near_one = tie(near_one, *ready)
        gains = near_one.reshape(sizes[0], -1, FLAT)[:, -16:-12, : 2 * LANES]
        gains = gains.transpose(1, 0, 2).reshape(4, features).astype(jnp.float32)
        quarter, columns = rows_owned // 4 * 2, sizes[0] * LANES
        shapes = (
            (quarter, 3 * columns),
            rows_owned,
            (quarter, 2 * sizes[0] * masters_one[8].shape[0]),
            masters_one[8].shape[0],
        )
        first, second = Tuned(shapes, sizes, place), Tuned(shapes, sizes, place)
        near, wide, down = ways_one = first_ways(first, near_one, far_one, place)
        first.near_way, first.wide_way, first.down_way = ways_one
        ways = second_ways(second, near_two, far_two, wide, down, place)
        second.near_way, second.wide_way, second.down_way = ways
        first.after_attention = lambda value: tie(value, near_two, wide.one, wide.two, down.one, down.two)
        first.before_wide = lambda value: tie(value, far_two[0])
        first.after_wide = lambda value: tie(value, far_two[1], ways[0].one, ways[0].two)
        first.at_end = lambda value: tie(value, ways[0].three)
        second.after_attention = lambda value: tie(value, ways[1].one, ways[1].two)
    else:
        gains = lax.all_gather(gain_rows, ("shard", "seq"), axis=1, tiled=True).astype(jnp.float32)
        first, second = (Plain(gather_plain(m, sizes, core)) for m in (masters_one, masters_two))
    middle_one, first_kept, saved_one, weights_one = layer_ahead(
        flat, (gains[0:1], gains[1:2]), first, None, tables, place
    )
    final, _, saved_two, weights_two = layer_ahead(
        middle_one, (gains[2:3], gains[3:4]), second, first_kept, tables, place
    )
    outputs = final.astype(jnp.bfloat16).reshape(batch, rows, features)
    upstream = cotangent.reshape(rows, features).astype(jnp.float32)
    hooks_two, hooks_one = Hooks(), Hooks()
    if tuned:
        two, one = TunedSender(sizes, place, (1, 2), (2, 1)), TunedSender(sizes, place, (1, 2), (2, 1))

        def at(*steps):
            def hook(value):
                for step in steps:
                    done = step(value)
                    value = tie(value, *(done if isinstance(done, tuple) else (done,)))
                return value

            return hook

        hooks_two.before_attention = at(two.proj_way)
        hooks_two.before_qkv = at(two.half("way_wide"), two.half("way_proj", 1))
        hooks_one.start = at(two.down_way)
        hooks_one.after_down = at(two.scatter_wide)
        hooks_one.before_wide = at(two.half("way_qkv"))
        hooks_one.after_wide = at(
            lambda value: two.wide_sum, two.half("way_down", 1), two.scatter_near, two.got("way_down")
        )
        hooks_one.before_attention = at(one.proj_way, one.half("way_wide"), one.down_way)
        hooks_one.before_qkv = at(
            lambda value: two.near_sum,
            two.share_far,
            one.half("way_proj", 1),
            one.scatter_wide,
            one.half("way_down", 1),
        )
        hooks_one.after_qkv = at(two.far_got, one.got("way_down"))
        hooks_one.before_norm = at(one.half("way_qkv"))
    else:
        two, one = PlainSender(sizes, core), PlainSender(sizes, core)
    grad_middle, gains_two, extra = layer_back(
        upstream, (gains[2:3], gains[3:4]), weights_two, saved_two, None, tables, place, two, hooks_two
    )
    grad_flat, gains_one, _ = layer_back(
        grad_middle, (gains[0:1], gains[1:2]), weights_one, saved_one, extra, tables, place, one, hooks_one
    )
    gain_grads = jnp.stack([*gains_one, *gains_two])
    if tuned:
        gain_total = sum_over(gain_grads, ("shard", "seq", "rep"))
        value = at(one.got("way_qkv"), one.got("way_proj"), one.share_far, one.scatter_near)(tie(grad_flat, outputs))
        at(two.pick_far, two.finish_far, two.share_near)(value)
        one.pick_far(value, two.far[0])
        two.pick_near(value, two.far[0])
        at(one.finish_far, two.finish_near, one.share_near)(value)
        one.pick_near(value, two.near[0], one.far[0], gain_total)
        one.finish_near(value)
        near_two, far_two, near_one, far_one = two.near, two.far, one.near, one.far
    else:
        gain_total = sum_over(gain_grads, ("shard", "seq", "rep"))
        near_two, far_two, near_one, far_one = two.near(), two.far(), one.near(), one.far()
    grad_input = grad_flat.reshape(batch, rows, features)
    block = features // (sizes[0] * sizes[1])
    mine = lax.axis_index("shard") * sizes[1] + core
    own = lax.dynamic_slice_in_dim(gain_total, mine * block, block, 1)

    def ordered(gain_attn, gain_ffn, near, far):
        (query, key, value, proj), (gate, upward, down) = near, far
        return (gain_attn, query, key, value, proj, gain_ffn, gate, upward, down)

    return (
        (outputs, grad_input)
        + ordered(own[0], own[1], near_one, far_one)
        + ordered(own[2], own[3], near_two, far_two)
    )


def solution(mesh):
    tokens = P(("rep", "shard"), "seq", None)
    vector, matrix = P(("shard", "seq")), P(("shard", "seq"), None)
    layer = (vector, matrix, matrix, matrix, matrix, vector, matrix, matrix, matrix)
    return jax.shard_map(
        shards,
        mesh=mesh,
        in_specs=(tokens, P(("rep", "shard"), None), *layer, *layer, tokens),
        out_specs=(tokens, tokens, *layer, *layer),
        check_vma=False,
    )
```

```python
import functools
import jax
import jax.numpy as jnp
from jax import lax
from jax.experimental import pallas as pl
from jax.experimental.pallas import tpu as pltpu
from jax.sharding import PartitionSpec as P

HD = 64
BLOCK = 256
LANES = 128
FLAT = 512
eps_norm = 1e-05
rope_base = 10000.0
mask_fill = -1000000000.0


def window(block):
    return max(0, block - 2)


def swap_halves(x):
    lane = lax.broadcasted_iota(jnp.int32, x.shape, 1)
    ahead = pltpu.roll(x, LANES - HD // 2, axis=1)
    behind = pltpu.roll(x, HD // 2, axis=1)
    return jnp.where(lane % HD < HD // 2, ahead, behind)


def fill_bias(bias, docs_column, docs_row, blocks):
    at = 0
    for i in range(blocks):
        first = window(i)
        rows = (i + 1 - first) * BLOCK
        same = (
            docs_column[pl.ds(first * BLOCK, rows), 0:1]
            == docs_row[0:1, pl.ds(i * BLOCK, BLOCK)]
        )
        bias[pl.ds(at, rows), :] = jnp.where(same, 0.0, mask_fill)
        at += rows


def block_of(mine_ref, other_ref, block, blocks, half):
    own, rows = block // (blocks // 2), pl.ds(block % (blocks // 2) * BLOCK, BLOCK)
    return jnp.where(half == own, mine_ref[rows, :], other_ref[rows, :])


def ahead_kernel(blocks, mixed, half_ref, mine_ref, other_ref, weight_ref, *rest):
    if mixed:
        first_ref, rest = rest[0], rest[1:]
    cos_ref, sin_ref, column_ref, row_ref, kept_ref, out_ref, lse_ref, bias = rest
    spin = half_ref[0] * (blocks // 2)

    @pl.when(pl.program_id(0) == 0)
    def _():
        fill_bias(bias, column_ref, row_ref, blocks)

    def place(b):
        return pl.multiple_of(lax.rem(b + spin, blocks) * BLOCK, BLOCK)

    for b in range(blocks):
        rows = pl.ds(b * BLOCK, BLOCK)
        cosine, sine = cos_ref[rows, :], sin_ref[rows, :]
        tokens = block_of(mine_ref, other_ref, b, blocks, half_ref[0])
        raw = jnp.dot(tokens, weight_ref[...], preferred_element_type=jnp.float32)
        for part in range(2):
            one = raw[:, part * LANES : (part + 1) * LANES]
            turned = one * cosine + swap_halves(one) * sine
            kept_ref[rows, part * LANES : (part + 1) * LANES] = turned.astype(jnp.bfloat16)
        value = raw[:, 2 * LANES :]
        if mixed:
            value = 0.5 * value + 0.5 * first_ref[rows, 2 * LANES :].astype(jnp.float32)
        kept_ref[rows, 2 * LANES :] = value.astype(jnp.bfloat16)

    value_turned = kept_ref[:, 2 * LANES :].T
    head_lane = lax.broadcasted_iota(jnp.int32, (BLOCK, LANES), 1) // HD
    at = 0
    for i in range(blocks):
        first = window(i)
        count = (i + 1 - first) * BLOCK
        rows = pl.ds(i * BLOCK, BLOCK)
        query = kept_ref[rows, 0:LANES] * jnp.bfloat16(HD**-0.5)
        keys = kept_ref[pl.ds(first * BLOCK, count), LANES : 2 * LANES]
        fill = bias[pl.ds(at, count), :]
        at += count
        outs = []
        for head in range(LANES // HD):
            one = jnp.where(head_lane == head, query, jnp.bfloat16(0))
            scores = (
                lax.dot_general(keys, one, (((1,), (1,)), ((), ())), preferred_element_type=jnp.float32)
                + fill
            )
            top = jnp.max(scores, axis=0, keepdims=True)
            powers = jnp.exp(scores - top)
            total = jnp.sum(powers, axis=0, keepdims=True)
            weights = (powers * (1.0 / total)).astype(jnp.bfloat16)
            outs.append(
                jnp.dot(
                    value_turned[head * HD : (head + 1) * HD, first * BLOCK : first * BLOCK + count],
                    weights,
                    preferred_element_type=jnp.float32,
                )
            )
            lse_ref[0, head : head + 1, rows] = top + jnp.log(total)
        merged = jnp.concatenate(outs, axis=0)
        out_ref[pl.ds(place(i), BLOCK), :] = merged.T.astype(jnp.bfloat16)


def back_kernel(blocks, mixed, half_ref, kept_ref, mine_ref, other_ref, lse_ref, *rest):
    if not mixed:
        extra_ref, rest = rest[0], rest[1:]
    cos_ref, sin_ref, column_ref, row_ref, out_ref, *rest = rest
    if mixed:
        passed_ref, rest = rest[0], rest[1:]
    bias, key_sum, value_sum = rest
    spin = half_ref[0] * (blocks // 2)

    @pl.when(pl.program_id(0) == 0)
    def _():
        fill_bias(bias, column_ref, row_ref, blocks)

    def place(b):
        return pl.multiple_of(lax.rem(b + spin, blocks) * BLOCK, BLOCK)

    def unrotate(x, rows):
        return x * cos_ref[rows, :] - swap_halves(x) * sin_ref[rows, :]

    keys_turned = kept_ref[:, LANES : 2 * LANES].T
    head_lane = lax.broadcasted_iota(jnp.int32, (BLOCK, LANES), 1) // HD
    at = 0
    for i in range(blocks):
        first = window(i)
        count = (i + 1 - first) * BLOCK
        rows = pl.ds(i * BLOCK, BLOCK)
        span = pl.ds(first * BLOCK, count)
        query = kept_ref[rows, 0:LANES] * jnp.bfloat16(HD**-0.5)
        grad = block_of(mine_ref, other_ref, i, blocks, half_ref[0])
        keys = kept_ref[span, LANES : 2 * LANES]
        values = kept_ref[span, 2 * LANES :]
        fill = bias[pl.ds(at, count), :]
        at += count
        outs = []
        key_add, value_add = [], []
        for head in range(LANES // HD):
            pick = head_lane == head
            one = jnp.where(pick, query, jnp.bfloat16(0))
            grad_one = jnp.where(pick, grad, jnp.bfloat16(0))
            scores = (
                lax.dot_general(keys, one, (((1,), (1,)), ((), ())), preferred_element_type=jnp.float32)
                + fill
            )
            weights = jnp.exp(scores - lse_ref[0, head : head + 1, rows])
            grad_weights = lax.dot_general(
                values, grad_one, (((1,), (1,)), ((), ())), preferred_element_type=jnp.float32
            )
            delta = jnp.sum(weights * grad_weights, axis=0, keepdims=True)
            grad_scores = (weights * (grad_weights - delta)).astype(jnp.bfloat16)
            value_add.append(
                jnp.dot(weights.astype(jnp.bfloat16), grad_one, preferred_element_type=jnp.float32)
            )
            key_add.append(jnp.dot(grad_scores, one, preferred_element_type=jnp.float32))
            outs.append(
                jnp.dot(
                    keys_turned[head * HD : (head + 1) * HD, first * BLOCK : first * BLOCK + count],
                    grad_scores,
                    preferred_element_type=jnp.float32,
                )
            )
        key_add, value_add = sum(key_add[1:], key_add[0]), sum(value_add[1:], value_add[0])
        old = count - BLOCK
        if old:
            key_sum[pl.ds(first * BLOCK, old), :] += key_add[:old]
            value_sum[pl.ds(first * BLOCK, old), :] += value_add[:old]
        key_sum[rows, :] = key_add[old:]
        value_sum[rows, :] = value_add[old:]
        grad_query = jnp.concatenate(outs, axis=0).T * HD**-0.5
        out_ref[pl.ds(place(i), BLOCK), 0:LANES] = unrotate(grad_query, rows).astype(jnp.bfloat16)
    for b in range(blocks):
        rows = pl.ds(b * BLOCK, BLOCK)
        there = pl.ds(place(b), BLOCK)
        out_ref[there, LANES : 2 * LANES] = unrotate(key_sum[rows, :], rows).astype(jnp.bfloat16)
        value_grad = value_sum[rows, :]
        if mixed:
            value_grad = 0.5 * value_grad
            passed_ref[rows, :] = value_grad
        else:
            value_grad = value_grad + extra_ref[rows, :]
        out_ref[there, 2 * LANES :] = value_grad.astype(jnp.bfloat16)


def bias_rows(blocks):
    return sum(i + 1 - window(i) for i in range(blocks)) * BLOCK


def whole(shape):
    return pl.BlockSpec(shape, lambda h, s: (0,) * len(shape))


def attend_ahead(tokens, weight, first_kept, tables, half):
    cosine, sine, column, row = tables
    length, width = 2 * tokens[0].shape[0], weight.shape[1]
    pairs, blocks = width // (3 * LANES), length // BLOCK
    mixed = first_kept is not None
    wide = pl.BlockSpec((length, 3 * LANES), lambda h, s: (0, h))
    slim = pl.BlockSpec((length, LANES), lambda h, s: (0, h))
    return pl.pallas_call(
        functools.partial(ahead_kernel, blocks, mixed),
        out_shape=(
            jax.ShapeDtypeStruct((length, width), jnp.bfloat16),
            jax.ShapeDtypeStruct((length, pairs * LANES), jnp.bfloat16),
            jax.ShapeDtypeStruct((pairs, LANES // HD, length), jnp.float32),
        ),
        grid_spec=pltpu.PrefetchScalarGridSpec(
            num_scalar_prefetch=1,
            grid=(pairs,),
            in_specs=[whole(tokens[0].shape)] * 2
            + [pl.BlockSpec((weight.shape[0], 3 * LANES), lambda h, s: (0, h))]
            + ([wide] if mixed else [])
            + [whole(cosine.shape), whole(sine.shape), whole(column.shape), whole(row.shape)],
            out_specs=(wide, slim, pl.BlockSpec((1, LANES // HD, length), lambda h, s: (h, 0, 0))),
            scratch_shapes=[pltpu.VMEM((bias_rows(blocks), BLOCK), jnp.float32)],
        ),
        compiler_params=pltpu.CompilerParams(dimension_semantics=("arbitrary",), vmem_limit_bytes=48 << 20),
        cost_estimate=pl.CostEstimate(flops=0, transcendentals=0, bytes_accessed=0),
        name="attend_ahead",
    )(half, *tokens, weight, *((first_kept,) if mixed else ()), cosine, sine, column, row)


def attend_back(kept, grad, lse, extra, tables, half):
    cosine, sine, column, row = tables
    length, width = kept.shape
    pairs, blocks = width // (3 * LANES), length // BLOCK
    mixed = extra is None
    wide = pl.BlockSpec((length, 3 * LANES), lambda h, s: (0, h))
    slim = pl.BlockSpec((length, LANES), lambda h, s: (0, h))
    outs = [jax.ShapeDtypeStruct((length, width), jnp.bfloat16)]
    out_specs = [wide]
    if mixed:
        outs.append(jax.ShapeDtypeStruct((length, pairs * LANES), jnp.float32))
        out_specs.append(slim)
    result = pl.pallas_call(
        functools.partial(back_kernel, blocks, mixed),
        out_shape=tuple(outs),
        grid_spec=pltpu.PrefetchScalarGridSpec(
            num_scalar_prefetch=1,
            grid=(pairs,),
            in_specs=[wide]
            + [pl.BlockSpec((length // 2, LANES), lambda h, s: (0, h))] * 2
            + [pl.BlockSpec((1, LANES // HD, length), lambda h, s: (h, 0, 0))]
            + ([] if mixed else [slim])
            + [whole(cosine.shape), whole(sine.shape), whole(column.shape), whole(row.shape)],
            out_specs=tuple(out_specs),
            scratch_shapes=[
                pltpu.VMEM((bias_rows(blocks), BLOCK), jnp.float32),
                pltpu.VMEM((length, LANES), jnp.float32),
                pltpu.VMEM((length, LANES), jnp.float32),
            ],
        ),
        compiler_params=pltpu.CompilerParams(dimension_semantics=("arbitrary",), vmem_limit_bytes=48 << 20),
        cost_estimate=pl.CostEstimate(flops=0, transcendentals=0, bytes_accessed=0),
        name="attend_back",
    )(half, kept, *grad, lse, *(() if mixed else (extra,)), cosine, sine, column, row)
    return result if mixed else (result[0], None)


def swap_cores(x):
    return lax.ppermute(x, "seq", [(0, 1), (1, 0)])


def exchange(x, mask):
    count = lax.axis_size("rep")
    return lax.ppermute(x, "rep", [(i, i ^ mask) for i in range(count)])


def unflat(read, rows, columns, write):
    at = 0
    for i in range(columns // FLAT):
        write(0, i * FLAT, read(at, rows, 0, FLAT))
        at += rows
    left = columns % FLAT
    if left:
        step = rows * left // FLAT
        for i in range(FLAT // left):
            write(i * step, columns - left, read(at, step, i * left, left))
        at += step
    return at


def join_kernel(masks, parts, cores, slot_ref, *refs):
    pieces, outs = refs[: len(masks)], refs[-sum(len(w) if k == "columns" else 1 for k, _, w in parts) :]
    for mask, piece in zip(masks, pieces):
        slot = lax.bitwise_xor(slot_ref[0], mask)
        base, at = 0, 0
        for kind, rows, widths in parts:
            columns = sum(widths)

            def read(row, count, column, width, base=base):
                return piece[0, base + row : base + row + count, column : column + width]

            def write(row, column, values, kind=kind, rows=rows, widths=widths, at=at):
                if kind == "columns":
                    one = rows // cores
                    left, which = column, 0
                    while left >= widths[which]:
                        left, which = left - widths[which], which + 1
                    took, offset = 0, column
                    while took < values.shape[1]:
                        size = min(widths[which] - left, values.shape[1] - took)
                        count = values.shape[0]
                        for done in range(0, count, min(one, count)):
                            core, inside = divmod(row + done, one)
                            size_rows = min(one, count)
                            outs[at + which][0, core, slot, inside : inside + size_rows, left : left + size] = (
                                values[done : done + size_rows, took : took + size]
                            )
                        took, left, which = took + size, 0, which + 1
                else:
                    there = pl.ds(pl.multiple_of(slot * columns, columns) + column, values.shape[1])
                    outs[at][0, row : row + values.shape[0], there] = values

            base += unflat(read, rows, columns, write)
            at += len(widths) if kind == "columns" else 1


def join(pieces, masks, slot, sizes, parts, start=None, after=()):
    groups, cores = sizes
    count, rows = len(masks), pieces[0].shape[0] // groups
    read = rows if start is None else sum(h * sum(w) for _, h, w in parts) // FLAT
    at = 0 if start is None else start // read
    shapes = []
    for kind, height, widths in parts:
        if kind == "columns":
            shapes += [(groups, cores, count, height // cores, w) for w in widths]
        else:
            shapes.append((groups, height, count * widths[0]))
    outs = pl.pallas_call(
        functools.partial(join_kernel, masks, parts, cores),
        out_shape=[jax.ShapeDtypeStruct(s, jnp.bfloat16) for s in shapes],
        grid_spec=pltpu.PrefetchScalarGridSpec(
            num_scalar_prefetch=1,
            grid=(groups,),
            in_specs=[pl.BlockSpec((1, read, FLAT), lambda g, s: (g, at, 0))] * count
            + [pl.BlockSpec(memory_space=pl.ANY)] * len(after),
            out_specs=[
                pl.BlockSpec((1, *s[1:]), lambda g, t, n=len(s): (g,) + (0,) * (n - 1)) for s in shapes
            ],
        ),
        cost_estimate=pl.CostEstimate(flops=0, transcendentals=0, bytes_accessed=0),
        name="join",
    )(slot, *[p.reshape(groups, rows, FLAT) for p in pieces], *after)
    return [o.reshape(-1, o.shape[-1]) for o in outs]


def core_columns(rows, sizes, core):
    shards, cores = sizes
    width = rows.shape[1] // (shards * cores)
    even, odd = (
        jnp.concatenate(
            [rows[:, (s * cores + c) * width : (s * cores + c + 1) * width] for s in range(shards)],
            axis=1,
        )
        for c in range(cores)
    )
    return jnp.where(core == 0, even, odd), jnp.where(core == 0, odd, even)


def head_major(parts):
    pairs = parts[0].shape[1] // LANES
    return jnp.concatenate(
        [p[:, i * LANES : (i + 1) * LANES] for i in range(pairs) for p in parts], axis=1
    )


def head_minor(joined):
    pairs = joined.shape[1] // (3 * LANES)
    return [
        jnp.concatenate(
            [
                joined[:, (3 * i + j) * LANES : (3 * i + j + 1) * LANES]
                for i in range(pairs)
            ],
            axis=1,
        )
        for j in range(3)
    ]


def chip_rows(rows_of, sizes, core):
    mine, theirs = rows_of
    other = swap_cores(theirs)
    return jnp.concatenate(
        [jnp.where(core == 0, mine, other), jnp.where(core == 0, other, mine)], axis=0
    )


def gather_shard(x):
    return lax.all_gather(x, "shard", axis=0, tiled=True)


def column_parts(weights, sizes, core, interleave):
    mine, theirs = zip(*[core_columns(w.astype(jnp.bfloat16), sizes, core) for w in weights])
    if interleave:
        return head_major(mine), head_major(theirs)
    return jnp.concatenate(mine, axis=1), jnp.concatenate(theirs, axis=1)


def gather_plain(masters, sizes, core):
    _, w_query, w_key, w_value, w_proj, _, w_gate, w_upward, w_down = masters
    w_qkv = gather_shard(chip_rows(column_parts((w_query, w_key, w_value), sizes, core, True), sizes, core))
    w_wide = gather_shard(chip_rows(column_parts((w_gate, w_upward), sizes, core, False), sizes, core))
    w_proj, w_down = (gather_shard(w.astype(jnp.bfloat16)) for w in (w_proj, w_down))
    return w_qkv, w_proj, w_wide, w_down


def call(kernel, outs, grid, in_specs, out_specs, name, scratch=(), scalars=1):
    return pl.pallas_call(
        kernel,
        out_shape=outs,
        grid_spec=pltpu.PrefetchScalarGridSpec(
            num_scalar_prefetch=scalars,
            grid=grid,
            in_specs=in_specs,
            out_specs=out_specs,
            scratch_shapes=scratch,
        ),
        compiler_params=pltpu.CompilerParams(
            dimension_semantics=("arbitrary",) * len(grid), vmem_limit_bytes=56 << 20
        ),
        cost_estimate=pl.CostEstimate(flops=0, transcendentals=0, bytes_accessed=0),
        name=name,
    )


def fixed(shape):
    return pl.BlockSpec(shape, lambda *ids: (0,) * len(shape))


def low(values):
    return values.astype(jnp.bfloat16)


def near_split_kernel(shards, place_ref, *refs):
    weights, gains, (mine, theirs) = refs[:3], refs[3:-2], refs[-2:]
    core = place_ref[1]
    for out, which in ((mine, core), (theirs, 1 - core)):
        for s in range(shards):
            there = pl.ds(pl.multiple_of((2 * s + which) * LANES, LANES), LANES)
            for j, weight in enumerate(weights):
                out[:, (3 * s + j) * LANES : (3 * s + j + 1) * LANES] = low(weight[:, there])
        if gains:
            rows = jnp.concatenate([g[...] for g in gains] + [jnp.zeros((16 - len(gains), LANES), jnp.float32)], axis=0)
            out[0:16, 3 * shards * LANES :] = low(rows)


def near_merge_kernel(place_ref, mine, theirs, proj, out):
    core = place_ref[1]
    rows = mine.shape[0]
    for j in range(3):
        for part, which in ((mine, core), (theirs, 1 - core)):
            there = pl.ds(pl.multiple_of((2 * j + which) * rows, rows), rows)
            out[there, :] = part[:, j * FLAT : (j + 1) * FLAT]
    half = proj.shape[0] // 2
    start = 6 * rows
    out[start : start + half, 0 : FLAT // 2] = low(proj[0:half, :])
    out[start : start + half, FLAT // 2 :] = low(proj[half:, :])
    if out.shape[0] > start + half:
        out[start + half :, :] = jnp.zeros((16, FLAT), jnp.bfloat16)
        for part, which in ((mine, core), (theirs, 1 - core)):
            there = pl.ds(pl.multiple_of(which * LANES, LANES), LANES)
            out[start + half :, there] = part[0:16, 3 * FLAT : 3 * FLAT + LANES]


def far_split_kernel(shards, place_ref, gate, upward, mine, theirs):
    core = place_ref[1]
    width = gate.shape[1] // (2 * shards)
    for at, weight in enumerate((gate, upward)):
        even, odd = (
            low(jnp.concatenate([weight[:, (2 * s + c) * width : (2 * s + c + 1) * width] for s in range(shards)], axis=1))
            for c in range(2)
        )
        there = slice(at * shards * width, (at + 1) * shards * width)
        mine[:, there] = jnp.where(core == 0, even, odd)
        theirs[:, there] = jnp.where(core == 0, odd, even)


def far_merge_kernel(place_ref, mine, theirs, down, out):
    core = place_ref[1]
    rows, columns = mine.shape
    blocks = columns // FLAT
    for part, which in ((mine, core), (theirs, 1 - core)):
        for j in range(blocks):
            there = pl.ds(pl.multiple_of((2 * j + which) * rows, rows), rows)
            out[there, :] = part[:, j * FLAT : (j + 1) * FLAT]
        there = pl.ds(pl.multiple_of(which * (FLAT // 2), FLAT // 2), FLAT // 2)
        out[2 * blocks * rows : (2 * blocks + 1) * rows, there] = part[:, blocks * FLAT :]
    half, start = down.shape[0] // 2, (2 * blocks + 1) * rows
    out[start:, 0 : FLAT // 2] = low(down[0:half, :])
    out[start:, FLAT // 2 :] = low(down[half:, :])


def shape_of(*shape, dtype=jnp.bfloat16):
    return jax.ShapeDtypeStruct(shape, dtype)


def quarter_of_rows(weight):
    return pl.BlockSpec((weight.shape[0] // 4, weight.shape[1]), lambda i, s: (s[0], 0))


def quarter_of_columns(weight):
    return pl.BlockSpec((weight.shape[0], weight.shape[1] // 4), lambda i, s: (0, s[0]))


def gather_near(weights, proj, gains, shards, place):
    rows = weights[0].shape[0] // 4
    width = 3 * shards * LANES + (LANES if gains else 0)
    gains = [g.reshape(1, LANES) for g in gains]
    mine, theirs = call(
        functools.partial(near_split_kernel, shards),
        [shape_of(rows, width)] * 2,
        (1,),
        [quarter_of_rows(w) for w in weights] + [fixed((1, LANES))] * len(gains),
        [fixed((rows, width))] * 2,
        "near_split",
    )(place, *weights, *gains)
    total = 6 * rows + proj.shape[0] // 2 + (16 if gains else 0)
    merged = call(
        near_merge_kernel,
        shape_of(total, FLAT),
        (1,),
        [fixed((rows, width))] * 2 + [quarter_of_columns(proj)],
        fixed((total, FLAT)),
        "near_merge",
    )(place, mine, swap_cores(theirs), proj)
    return merged


def gather_far(weights, down, shards, place):
    rows, width = weights[0].shape[0] // 4, weights[0].shape[1]
    mine, theirs = call(
        functools.partial(far_split_kernel, shards),
        [shape_of(rows, width)] * 2,
        (1,),
        [quarter_of_rows(w) for w in weights],
        [fixed((rows, width))] * 2,
        "far_split",
    )(place, *weights)
    total = rows * width // (FLAT // 2) + down.shape[0] // 2
    merged = call(
        far_merge_kernel,
        shape_of(total, FLAT),
        (1,),
        [fixed((rows, width))] * 2 + [quarter_of_columns(down)],
        fixed((total, FLAT)),
        "far_merge",
    )(place, mine, swap_cores(theirs), down)
    return merged


def dot_nn(a, b):
    return jnp.dot(a, b, preferred_element_type=jnp.float32)


def halves_of_rows(tile, per_half):
    return [
        lambda i, s: (jnp.minimum(i, per_half - 1), 0),
        lambda i, s: (jnp.maximum(i - per_half, 0), 0),
    ]


def gated_kernel(per_half, none_ref, mine, other, weight, gate_out, upward_out, inner_out):
    tokens = jnp.where(pl.program_id(0) < per_half, mine[...], other[...])
    width = gate_out.shape[1]
    one, two = dot_nn(tokens, weight[:, :width]), dot_nn(tokens, weight[:, width:])
    inner_out[...] = low(one * jax.nn.sigmoid(one) * two)
    gate_out[...] = low(one)
    upward_out[...] = low(two)


def gated(tokens, weight, place):
    length, width, tile = 2 * tokens[0].shape[0], weight.shape[1] // 2, 512
    rows = pl.BlockSpec((tile, width), lambda i, s: (i, 0))
    maps = halves_of_rows(tile, length // tile // 2)
    return call(
        functools.partial(gated_kernel, length // tile // 2),
        [shape_of(length, width)] * 3,
        (length // tile,),
        [pl.BlockSpec((tile, tokens[0].shape[1]), m) for m in maps] + [fixed(weight.shape)],
        [rows] * 3,
        "gated",
    )(place, *tokens, weight)


def gated_back_kernel(per_half, none_ref, mine, other, weight, gate, upward, out):
    grad = jnp.where(pl.program_id(0) < per_half, mine[...], other[...])
    width = gate.shape[1]
    inner = lax.dot_general(grad, weight[...], (((1,), (1,)), ((), ())), preferred_element_type=jnp.float32)
    one, two = gate[...].astype(jnp.float32), upward[...].astype(jnp.float32)
    part = jax.nn.sigmoid(one)
    out[:, :width] = low(inner * two * part * (1.0 + one * (1.0 - part)))
    out[:, width:] = low(inner * one * part)


def gated_back(grad, weight, gate, upward, place):
    (length, width), tile = gate.shape, 512
    rows = pl.BlockSpec((tile, width), lambda i, s: (i, 0))
    maps = halves_of_rows(tile, length // tile // 2)
    return call(
        functools.partial(gated_back_kernel, length // tile // 2),
        shape_of(length, 2 * width),
        (length // tile,),
        [pl.BlockSpec((tile, grad[0].shape[1]), m) for m in maps] + [fixed(weight.shape), rows, rows],
        pl.BlockSpec((tile, 2 * width), lambda i, s: (i, 0)),
        "gated_back",
    )(place, *grad, weight, gate, upward)


def turned(a, b):
    return lax.dot_general(a, b, (((0,), (0,)), ((), ())), preferred_element_type=jnp.float32)


def grad_rows_kernel(bits_ref, mine, other, right, *outs):
    half, parts = mine.shape[0], len(outs) // 2
    product = turned(mine[...], right[0:half, :]) + turned(other[...], right[half:, :])
    groups, rows, width = outs[0].shape
    for part in range(parts):
        sent, kept = outs[2 * part : 2 * part + 2]
        upper, columns = bits_ref[part] == 0, slice(part * width, (part + 1) * width)
        for g in range(groups):
            one, two = (low(product[(2 * g + h) * rows : (2 * g + h + 1) * rows, columns]) for h in range(2))
            kept[g] = jnp.where(upper, one, two)
            sent[g] = jnp.where(upper, two, one)


def grad_rows(left, right, groups, bits, parts=1, tile=512):
    half, features = left[0].shape
    length, width = right.shape
    per, rows = groups * tile // features, features // groups // 2
    out = pl.BlockSpec((per, rows, width // parts), lambda i, s: (i, 0, 0))
    return call(
        grad_rows_kernel,
        [shape_of(groups, rows, width // parts)] * (2 * parts),
        (features // tile,),
        [pl.BlockSpec((half, tile), lambda i, s: (0, i))] * 2 + [fixed((length, width))],
        [out] * (2 * parts),
        "grad_rows",
    )(bits, *left, right)


def grad_whole_kernel(none_ref, left, mine, other, out):
    half = mine.shape[0]
    out[...] = low(turned(left[0:half, :], mine[...]) + turned(left[half:, :], other[...]))


def grad_whole(left, right, place, steps=2):
    length, rows = left.shape
    half, width = right[0].shape
    side = pl.BlockSpec((half, width // steps), lambda i, s: (0, i))
    return call(
        grad_whole_kernel,
        shape_of(rows, width),
        (steps,),
        [fixed((length, rows)), side, side],
        pl.BlockSpec((rows, width // steps), lambda i, s: (0, i)),
        "grad_whole",
    )(place, left, *right)


def grad_columns_kernel(bits_ref, left, mine, other, sent, kept):
    half = mine.shape[0]
    product = low(turned(left[0:half, :], mine[...]) + turned(left[half:, :], other[...]))

    @pl.when(pl.program_id(0) == 0)
    def _():
        sent[...] = product

    @pl.when(pl.program_id(0) == 1)
    def _():
        kept[...] = product


def grad_columns(left, right, bits):
    length, rows = left.shape
    half, width = right[0].shape
    side = pl.BlockSpec((half, width // 2), lambda i, s: (0, jnp.where(i == 0, 1 - s[0], s[0])))
    return call(
        grad_columns_kernel,
        [shape_of(rows, width // 2)] * 2,
        (2,),
        [fixed((length, rows)), side, side],
        [fixed((rows, width // 2))] * 2,
        "grad_columns",
    )(bits, left, *right)


def add(a, b):
    return a + b


def halve_kernel(parts, bits_ref, *refs):
    ins, outs = refs[: 2 * parts], refs[2 * parts :]
    for part in range(parts):
        kept, got = ins[2 * part : 2 * part + 2]
        sent_out, kept_out = outs[2 * part : 2 * part + 2]
        total = add(kept[...], got[...])
        upper = bits_ref[1 - part] == 0
        middle = kept.shape[1] // 2
        one, two = total[:, :middle], total[:, middle:]
        kept_out[...] = jnp.where(upper, one, two)
        sent_out[...] = jnp.where(upper, two, one)


def halve(ins, bits, steps):
    shape, parts = ins[0].shape, len(ins) // 2
    block = (shape[0] // steps, *shape[1:])
    small = (*shape[:1], shape[1] // 2, *shape[2:])
    index = lambda i, s: (i,) + (0,) * (len(shape) - 1)
    return call(
        functools.partial(halve_kernel, parts),
        [shape_of(*small)] * (2 * parts),
        (steps,),
        [pl.BlockSpec(block, index)] * (2 * parts),
        [pl.BlockSpec((block[0], *small[1:]), index)] * (2 * parts),
        "halve",
    )(bits, *ins)


def flatten_kernel(parts, none_ref, *refs):
    bodies, tails, out = refs[: 2 * parts], refs[2 * parts : -1], refs[-1]
    sums = [add(bodies[2 * p][...], bodies[2 * p + 1][...]) for p in range(parts)]
    total = jnp.concatenate(sums, axis=2) if parts > 1 else sums[0]
    cores, rows, columns = total.shape
    blocks, left = columns // FLAT, columns % FLAT
    for j in range(blocks):
        for c in range(cores):
            there = slice((j * cores + c) * rows, (j * cores + c + 1) * rows)
            out[0, there, :] = total[c, :, j * FLAT : (j + 1) * FLAT]
    at = blocks * cores * rows
    if left:
        for c in range(cores):
            out[0, at : at + rows, c * left : (c + 1) * left] = total[c, :, columns - left :]
        at += rows
    if tails:
        tail = add(tails[0][...], tails[1][...])
        half = tail.shape[0] // 2
        out[0, at:, 0 : FLAT // 2] = tail[:half]
        out[0, at:, FLAT // 2 :] = tail[half:]


def flatten(bodies, tails, shards, bits):
    groups, rows, columns = bodies[0].shape
    height, width = tails[0].shape if tails else (0, 0)
    cores, parts = groups // shards, len(bodies) // 2
    total = (parts * cores * rows * columns + height // shards * width) // FLAT
    return call(
        functools.partial(flatten_kernel, parts),
        shape_of(shards, total, FLAT),
        (shards,),
        [pl.BlockSpec((cores, rows, columns), lambda i, s: (i, 0, 0))] * len(bodies)
        + [pl.BlockSpec((height // shards, width), lambda i, s: (i, 0))] * len(tails),
        pl.BlockSpec((1, total, FLAT), lambda i, s: (i, 0, 0)),
        "flatten",
    )(bits, *bodies, *tails).reshape(-1, FLAT)


def append_kernel(none_ref, *refs):
    bodies, (kept, got, out) = refs[:-3], refs[-3:]
    at = 0
    for body in bodies:
        out[at : at + body.shape[0], :] = body[...]
        at += body.shape[0]
    tail, half = add(kept[...], got[...]), kept.shape[0] // 2
    out[at:, 0 : FLAT // 2] = tail[:half]
    out[at:, FLAT // 2 :] = tail[half:]


def append(bodies, kept, got, bits):
    rows = sum(b.shape[0] for b in bodies) + kept.shape[0] // 2
    return call(
        append_kernel,
        shape_of(rows, FLAT),
        (1,),
        [fixed(x.shape) for x in (*bodies, kept, got)],
        fixed((rows, FLAT)),
        "append",
    )(bits, *bodies, kept, got)


def from_row(pieces, start):
    return [p.at[pl.ds(start, p.shape[0] - start)] for p in pieces] if start else pieces


def pick_kernel(blocks, rows, left, start, count, place_ref, *refs):
    pieces, out = from_row(refs[:count], start), refs[-1]
    which = 1 - place_ref[1]
    for k, piece in enumerate(pieces):
        for j in range(blocks):
            there = pl.ds(pl.multiple_of((2 * j + which) * rows, rows), rows)
            out[k, j * rows : (j + 1) * rows, :] = piece[there, :]
        if left:
            there = pl.ds(pl.multiple_of(which * left, left), left)
            out[k, blocks * rows :, 0:left] = piece[2 * blocks * rows : (2 * blocks + 1) * rows, there]
            out[k, blocks * rows :, left:] = jnp.zeros((rows, FLAT - left), jnp.bfloat16)


def pick(pieces, rows, columns, place, start, after):
    blocks, left = columns // FLAT, columns % FLAT
    total = (blocks + (left > 0)) * rows
    return call(
        functools.partial(pick_kernel, blocks, rows, left, start, len(pieces)),
        shape_of(len(pieces), total, FLAT),
        (1,),
        [fixed(pieces[0].shape)] * len(pieces) + [pl.BlockSpec(memory_space=pl.ANY)] * len(after),
        fixed((len(pieces), total, FLAT)),
        "pick",
    )(place, *pieces, *after)


def slots_of(bits_ref):
    places = []
    for one, two in ((0, 0), (1, 0), (0, 1), (1, 1)):
        first, second = lax.bitwise_xor(bits_ref[0], one), lax.bitwise_xor(bits_ref[1], two)
        places.append((2 * first + second, 2 * second + first))
    return places


def tail_out(piece, start, out, slot):
    half, columns = out.shape[0] // 2, FLAT // 2
    there = pl.ds(pl.multiple_of(slot * columns, columns), columns)
    out[0:half, there] = piece[start : start + half, 0:columns].astype(jnp.float32)
    out[half:, there] = piece[start : start + half, columns:].astype(jnp.float32)


def finish_near_kernel(shards, rows, start, bits_ref, place_ref, *refs):
    pieces, other, outs, tail = from_row(refs[:4], start), refs[4], refs[5:8], refs[8]
    core = place_ref[1]
    for k, slots in enumerate(slots_of(bits_ref)):
        for s in range(shards):
            there = pl.ds(pl.multiple_of(slots[2 * s // shards] * rows, rows), rows)
            for j, out in enumerate(outs):
                block, lane = divmod((3 * s + j) * LANES, FLAT)
                mine_rows = pl.ds(pl.multiple_of((2 * block + core) * rows, rows), rows)
                mine = pieces[k][mine_rows, lane : lane + LANES]
                theirs = other[k, block * rows : (block + 1) * rows, lane : lane + LANES]
                for part, which in ((mine, core), (theirs, 1 - core)):
                    lanes = pl.ds(pl.multiple_of((2 * s + which) * LANES, LANES), LANES)
                    out[there, lanes] = part.astype(jnp.float32)
        tail_out(pieces[k], 6 * rows, tail, slots[0])


def finish_far_kernel(shards, rows, start, bits_ref, place_ref, *refs):
    pieces, other, outs, tail = from_row(refs[:4], start), refs[4], refs[5:7], refs[7]
    core = place_ref[1]
    width = outs[0].shape[1] // (2 * shards)
    columns = 2 * shards * width
    blocks, left = columns // FLAT, columns % FLAT
    for k, slots in enumerate(slots_of(bits_ref)):
        mine = [
            pieces[k][pl.ds(pl.multiple_of((2 * j + core) * rows, rows), rows), :] for j in range(blocks)
        ]
        lanes = pl.ds(pl.multiple_of(core * left, left), left)
        mine.append(pieces[k][2 * blocks * rows : (2 * blocks + 1) * rows, lanes])
        theirs = [other[k, j * rows : (j + 1) * rows, :] for j in range(blocks)]
        theirs.append(other[k, blocks * rows :, 0:left])
        mine, theirs = (jnp.concatenate(p, axis=1).astype(jnp.float32) for p in (mine, theirs))
        even, odd = jnp.where(core == 0, mine, theirs), jnp.where(core == 0, theirs, mine)
        for at, out in enumerate(outs):
            there = pl.ds(pl.multiple_of(slots[at] * rows, rows), rows)
            parts = [
                p[:, (at * shards + s) * width : (at * shards + s + 1) * width]
                for s in range(shards)
                for p in (even, odd)
            ]
            out[there, :] = jnp.concatenate(parts, axis=1)
        tail_out(pieces[k], (2 * blocks + 1) * rows, tail, slots[0])


class Way:
    def __init__(self, halves, plan, bits):
        self.sent, self.kept = halves[::2], halves[1::2]
        self.plan, self.bits = plan, bits
        self.got = [exchange(x, plan[p]) for p, x in enumerate(self.sent)]

    def last(self, value):
        return [x for pair in zip(self.kept, self.got) for x in (tie(pair[0], value), pair[1])]

    def half(self, value, steps=2):
        outs = halve(self.last(value), self.bits, steps)
        self.sent, self.kept = outs[::2], outs[1::2]
        self.got = [exchange(x, self.plan[1 - p]) for p, x in enumerate(self.sent)]
        return tuple(self.sent)


class TunedSender:
    def __init__(self, sizes, place, near, far):
        self.sizes, self.place, self.near_plan, self.far_plan = sizes, place, near, far
        self.near_bits, self.far_bits = (
            jnp.stack([bit_of(place[0], m) for m in plan]).astype(jnp.int32) for plan in (near, far)
        )
        self.groups = sizes[0] * sizes[1]

    def down(self, left, right):
        grad = grad_whole(left, right, self.place)
        self.down_sum = scatter_shard(grad)
        return grad

    def down_way(self, value):
        reduced, bit = tie(self.down_sum, value), self.far_bits[0]
        width = reduced.shape[1] // 2
        halves = [lax.dynamic_slice_in_dim(reduced, b * width, width, 1) for b in (1 - bit, bit)]
        self.way_down = Way(halves, self.far_plan, self.far_bits)
        return halves[0]

    def wide(self, left, right):
        self.way_wide = Way(grad_rows(left, right, self.groups, self.far_bits, 2), self.far_plan, self.far_bits)
        return self.way_wide.sent[0]

    def proj(self, left, right):
        self.proj_halves = grad_columns(left, right, self.near_bits)
        return self.proj_halves[0]

    def proj_way(self, value):
        sent, kept = self.proj_halves
        self.way_proj = Way([tie(sent, value), kept], self.near_plan, self.near_bits)
        return ()

    def qkv(self, left, right):
        self.way_qkv = Way(grad_rows(left, right, self.groups, self.near_bits, 2), self.near_plan, self.near_bits)
        return self.way_qkv.sent[0]

    def half(self, name, steps=2):
        return lambda value: getattr(self, name).half(value, steps)

    def got(self, name):
        return lambda value: tuple(getattr(self, name).got)

    def scatter_wide(self, value):
        self.wide_shape = self.way_wide.kept[0].shape
        flat = flatten(self.way_wide.last(value), (), self.sizes[0], self.far_bits)
        self.wide_sum = scatter_shard(flat)
        return flat

    def scatter_near(self, value):
        self.near_shape, self.proj_height = self.way_qkv.kept[0].shape, self.way_proj.kept[0].shape[0] // self.sizes[0]
        flat = flatten(self.way_qkv.last(value), self.way_proj.last(value), self.sizes[0], self.near_bits)
        self.near_sum = scatter_shard(flat)
        return flat

    def shared(self, piece, plan):
        return [piece] + [exchange(piece, m) for m in (*plan, plan[0] ^ plan[1])]

    def share_near(self, value):
        self.near_at, self.near_pieces = 0, self.shared(tie(self.near_sum, value), self.near_plan)
        return self.near_pieces[0]

    def share_far(self, value):
        piece = append([tie(self.wide_sum, value)], self.way_down.kept[0], self.way_down.got[0], self.far_bits)
        self.far_at, self.far_pieces = 0, self.shared(piece, self.far_plan)
        return piece

    def share_all(self, value):
        bodies = [tie(self.near_sum, value), self.wide_sum]
        piece = append(bodies, self.way_down.kept[0], self.way_down.got[0], self.far_bits)
        self.near_at, self.far_at = 0, self.near_sum.shape[0]
        own, one, two, both = self.near_pieces = self.shared(piece, self.near_plan)
        self.far_pieces = [own, one, two, both] if self.near_plan == self.far_plan else [own, two, one, both]
        return piece

    def far_got(self, value):
        return tuple(self.far_pieces[1:])

    def near_got(self, value):
        return tuple(self.near_pieces[1:])

    def pick_near(self, value, *after):
        _, rows, columns = self.near_shape
        pieces = [tie(self.near_pieces[0], value), *self.near_pieces[1:]]
        picked = pick(pieces, rows, 2 * columns, self.place, self.near_at, after)
        self.near_other = swap_cores(picked)
        return picked

    def pick_far(self, value, *after):
        _, rows, columns = self.wide_shape
        pieces = [tie(self.far_pieces[0], value), *self.far_pieces[1:]]
        picked = pick(pieces, rows, 2 * columns, self.place, self.far_at, after)
        self.far_other = swap_cores(picked)
        return picked

    def finish_near(self, value):
        rows, features = self.near_shape[1], self.groups * LANES
        self.near = self.finish(
            functools.partial(finish_near_kernel, self.sizes[0], rows, self.near_at),
            [(4 * rows, features)] * 3 + [(self.proj_height, 2 * FLAT)],
            (self.near_bits, tie(self.place, value), *self.near_pieces, self.near_other),
            "finish_near",
        )
        return self.near[0]

    def finish_far(self, value):
        _, rows, columns = self.wide_shape
        self.far = self.finish(
            functools.partial(finish_far_kernel, self.sizes[0], rows, self.far_at),
            [(4 * rows, 2 * columns)] * 2 + [(self.way_down.kept[0].shape[0], 2 * FLAT)],
            (self.far_bits, tie(self.place, value), *self.far_pieces, self.far_other),
            "finish_far",
        )
        return self.far[0]

    def finish(self, kernel, shapes, operands, name):
        return call(
            kernel,
            [shape_of(*s, dtype=jnp.float32) for s in shapes],
            (1,),
            [fixed(x.shape) for x in operands[2:]],
            [fixed(s) for s in shapes],
            name,
            scalars=2,
        )(*operands)


class PlainSender:
    def __init__(self, sizes, core):
        self.sizes, self.core = sizes, core

    def total(self, grad):
        return lax.psum(scatter_shard(low(grad)), "rep")

    def down(self, left, right):
        self.down_sum = self.total(dot_tn(left, jnp.concatenate(right, axis=0)))

    def proj(self, left, right):
        self.proj_sum = self.total(dot_tn(left, jnp.concatenate(right, axis=0)))

    def wide(self, left, right):
        self.wide_sum = self.total(dot_tn(jnp.concatenate(left, axis=0), right))

    def qkv(self, left, right):
        self.qkv_sum = self.total(dot_tn(jnp.concatenate(left, axis=0), right))

    def columns(self, reduced):
        shaped = reduced.reshape(2, -1, reduced.shape[1])
        mine = lax.dynamic_index_in_dim(shaped, self.core, 0, keepdims=False)
        other = swap_cores(lax.dynamic_index_in_dim(shaped, 1 - self.core, 0, keepdims=False))
        even, odd = jnp.where(self.core == 0, mine, other), jnp.where(self.core == 0, other, mine)
        return even.astype(jnp.float32), odd.astype(jnp.float32)

    def near(self):
        even, odd = self.columns(self.qkv_sum)
        parts = [spread_columns(e, o, self.sizes) for e, o in zip(head_minor(even), head_minor(odd))]
        return (*parts, self.proj_sum.astype(jnp.float32))

    def far(self):
        even, odd = self.columns(self.wide_sum)
        width = even.shape[1] // 2
        parts = [spread_columns(even[:, at], odd[:, at], self.sizes) for at in (slice(0, width), slice(width, None))]
        return (*parts, self.down_sum.astype(jnp.float32))


def bit_of(rep, mask):
    return (rep // mask) % 2


def scatter_shard(x):
    return lax.psum_scatter(x, "shard", scatter_dimension=0, tiled=True)


def spread_columns(even, odd, sizes):
    shards, cores = sizes
    width = even.shape[1] // shards
    return jnp.concatenate(
        [p[:, s * width : (s + 1) * width] for s in range(shards) for p in (even, odd)], axis=1
    )


def norm_ahead(values, gain_row):
    factor = lax.rsqrt(jnp.mean(values * values, axis=-1, keepdims=True) + eps_norm)
    return ((values * factor * gain_row).astype(jnp.bfloat16), factor)


def norm_back(values, factor, gain_row, upstream):
    scaled = upstream * gain_row
    gain_grad = jnp.sum(upstream * values * factor, axis=0)
    inner_mean = jnp.mean(scaled * values, axis=-1, keepdims=True)
    return (factor * scaled - values * (factor * factor * factor) * inner_mean, gain_grad)


def both_halves(mine):
    return mine, swap_cores(mine)


def dot(a, b):
    return jnp.dot(a, b, preferred_element_type=jnp.float32)


def dot_nt(a, b):
    return lax.dot_general(a, b, (((1,), (1,)), ((), ())), preferred_element_type=jnp.float32)


def dot_tn(a, b):
    return lax.dot_general(a, b, (((0,), (0,)), ((), ())), preferred_element_type=jnp.float32)


def sum_halves(product, rows, hook=lambda value: value):
    theirs = hook(swap_cores(product(slice(rows, 2 * rows)).astype(jnp.bfloat16)))
    return product(slice(0, rows)) + theirs.astype(jnp.float32)


def tie(value, *others):
    return lax.optimization_barrier((value, *others))[0]


def layer_ahead(flat, gains, weights, first_kept, tables, place):
    gain_attn, gain_ffn = gains
    rows = flat.shape[0]
    normed, factor_attn = norm_ahead(flat, gain_attn)
    normed = both_halves(normed)
    w_qkv, w_proj = weights.near()
    kept, attended, lse = attend_ahead(normed, w_qkv, first_kept, tables, place[1:])
    attended = weights.after_attention(attended)
    theirs = low(dot(attended[rows:], w_proj))
    middle = flat + dot(attended[:rows], w_proj) + swap_cores(theirs).astype(jnp.float32)
    normed_ffn, factor_ffn = norm_ahead(middle, gain_ffn)
    normed_ffn = both_halves(normed_ffn)
    (w_wide,) = weights.wide()
    normed_ffn = (weights.before_wide(normed_ffn[0]), normed_ffn[1])
    gate_pre, upward_pre, inner = gated(normed_ffn, w_wide, place)
    inner = weights.after_wide(inner)
    (w_down,) = weights.down(inner)
    theirs = low(dot(inner[rows:], w_down))
    result = middle + dot(inner[:rows], w_down) + swap_cores(theirs).astype(jnp.float32)
    result = weights.at_end(result)
    saved = (
        flat,
        factor_attn,
        normed,
        kept,
        lse,
        attended,
        middle,
        factor_ffn,
        normed_ffn,
        gate_pre,
        upward_pre,
        inner,
    )
    return result, kept, saved, (w_qkv, w_proj, w_wide, w_down)


class Plain:
    def __init__(self, weights):
        self.weights = weights

    def near(self):
        return self.weights[:2]

    def wide(self):
        return self.weights[2:3]

    def down(self, inner):
        return self.weights[3:]

    def same(self, value):
        return value

    after_attention = before_wide = after_wide = at_end = same


class Quarters:
    def __init__(self, place, piece, first, second, before_first=(), before_second=()):
        self.slot, self.starts = place[:1], {}
        self.masks = (0, first, second, first ^ second)
        self.one = exchange(tie(piece, *before_first), first)
        self.two = exchange(tie(piece, *before_second), second)
        self.three = exchange(tie(self.one, *before_second), second)
        self.pieces = [piece, self.one, self.two, self.three]


class Tuned(Plain):
    def __init__(self, shapes, sizes, place):
        (qkv_rows, qkv_width), proj_rows, (wide_rows, wide_width), down_rows = shapes
        self.cut, self.shards = wide_rows * wide_width // FLAT, sizes[0]
        self.near_parts = (("columns", qkv_rows, (qkv_width,)), ("rows", proj_rows, (FLAT // 2,)))
        self.wide_parts = (("columns", wide_rows, (wide_width,)),)
        self.down_parts = (("rows", down_rows, (FLAT // 2,)),)
        self.join = lambda q, parts, after=(): join(
            q.pieces, q.masks, q.slot, sizes, parts, q.starts.get(parts[0][0]), after
        )

    def split(self, far):
        far = far.reshape(self.shards, -1, FLAT)
        return (f.reshape(-1, FLAT) for f in (far[:, : self.cut], far[:, self.cut :]))

    def near(self):
        return self.join(self.near_way, self.near_parts)

    def wide(self):
        return self.join(self.wide_way, self.wide_parts)

    def down(self, inner):
        return self.join(self.down_way, self.down_parts, (inner,))


class Halves:
    def __init__(self, place, pieces, before):
        self.slot, self.starts = 2 * half_of(place[:1]), {}
        self.masks = (0, 1, 2, 3)
        self.one, self.two = exchange(tie(pieces[0], *before), 1), exchange(pieces[1], 2)
        self.pieces = [*pieces, self.one, self.two]


def half_of(rep):
    return lax.bitwise_xor(rep, rep // 2) % 2


def first_ways(layer, near, far, place):
    near = Quarters(place, near, 1, 2)
    wide, down = layer.split(tie(far, near.one, near.two, near.three))
    return near, Quarters(place, wide, 2, 1), Quarters(place, down, 1, 2)


def second_ways(layer, near, far, wide_one, down_one, place):
    near = Quarters(place, near, 2, 1, (down_one.two,), (wide_one.one,))
    wide, down = zip(*[layer.split(f) for f in far])
    wide = Halves(place, wide, (near.two, near.three))
    return near, wide, Halves(place, down, (near.two, near.three))


def layer_back(upstream, gains, weights, saved, extra, tables, place, send, hooks):
    gain_attn, gain_ffn = gains
    w_qkv, w_proj, w_wide, w_down = weights
    (
        flat,
        factor_attn,
        normed,
        kept,
        lse,
        attended,
        middle,
        factor_ffn,
        normed_ffn,
        gate_pre,
        upward_pre,
        inner,
    ) = saved
    rows = flat.shape[0]
    mine, other = both_halves(low(upstream))
    grad_down = hooks.start(mine), other
    grad_down = hooks.after_down(hooks.after(grad_down[0], send.down(inner, grad_down))), grad_down[1]
    grad_wide = hooks.before_wide(gated_back(grad_down, w_down, gate_pre, upward_pre, place))
    grad_wide = hooks.after_wide(hooks.after(grad_wide, send.wide(normed_ffn, grad_wide)))
    grad_normed_ffn = sum_halves(lambda part: dot_nt(grad_wide[part], w_wide), rows)
    grad_part_ffn, grad_gain_ffn = norm_back(middle, factor_ffn, gain_ffn, grad_normed_ffn)
    grad_middle = upstream + grad_part_ffn
    mine, other = both_halves(low(grad_middle))
    grad_branch = hooks.before_branch(mine), other
    mine, other = (low(dot_nt(g, w_proj)) for g in grad_branch)
    mine = hooks.before_attention(hooks.after(mine, send.proj(attended, grad_branch)))
    grad_qkv, passed = attend_back(kept, (mine, other), lse, extra, tables, place[1:])
    grad_qkv = hooks.before_qkv(grad_qkv)
    grad_qkv = hooks.after_qkv(hooks.after(grad_qkv, send.qkv(normed, grad_qkv)))
    grad_normed = sum_halves(lambda part: dot_nt(grad_qkv[part], w_qkv), rows, hooks.before_norm)
    grad_part_attn, grad_gain_attn = norm_back(flat, factor_attn, gain_attn, grad_normed)
    grad_flat = hooks.at_end(grad_middle + grad_part_attn)
    return grad_flat, (grad_gain_attn, grad_gain_ffn), passed


class Hooks:
    def same(self, value):
        return value

    start = before_norm = before_branch = after_down = before_wide = after_wide = before_attention = before_qkv = after_qkv = at_end = same

    def after(self, value, other):
        return value if other is None else tie(value, other)


def sum_over(x, axes):
    for axis in axes:
        count, mask = lax.axis_size(axis), 1
        while mask < count:
            x = x + lax.ppermute(x, axis, [(i, i ^ mask) for i in range(count)])
            mask *= 2
    return x


def shards(inputs, documents, *rest):
    masters_one, masters_two, cotangent = rest[:9], rest[9:18], rest[18]
    batch, rows, features = inputs.shape
    reps, sizes = lax.axis_size("rep"), (lax.axis_size("shard"), lax.axis_size("seq"))
    assert batch == 1 and sizes[1] == 2
    core, rep = lax.axis_index("seq"), lax.axis_index("rep")
    rows_owned = masters_one[1].shape[0]
    tuned = reps == 4 and rows_owned == LANES
    length = sizes[1] * rows
    frequencies = rope_base ** (-(jnp.arange(HD // 2, dtype=jnp.float32) * 2.0 / HD))
    angles = jnp.arange(length, dtype=jnp.float32)[:, None] * frequencies[None, :]
    cosine, sine = jnp.cos(angles), jnp.sin(angles)
    tables = (
        jnp.tile(cosine, (1, LANES * 2 // HD)),
        jnp.tile(jnp.concatenate([-sine, sine], axis=1), (1, LANES // HD)),
        documents.reshape(length, 1),
        documents.reshape(1, length),
    )
    gain_rows = jnp.stack([masters_one[0], masters_one[5], masters_two[0], masters_two[5]]).astype(
        jnp.bfloat16
    )
    flat = inputs.reshape(rows, features).astype(jnp.float32)
    place = jnp.stack([rep, core]).astype(jnp.int32)
    if tuned:
        gain_list = [masters_one[0], masters_one[5], masters_two[0], masters_two[5]]
        near_one = gather_near(masters_one[1:4], masters_one[4], gain_list, sizes[0], place)
        far_one = gather_far(masters_one[6:8], masters_one[8], sizes[0], place)
        near_two = gather_near(masters_two[1:4], masters_two[4], [], sizes[0], place)
        quarter_of = 2 * half_of(rep)
        far_two = [
            gather_far(
                masters_two[6:8], masters_two[8], sizes[0], jnp.stack([quarter_of + u, core]).astype(jnp.int32)
            )
            for u in range(2)
        ]
        ready = (far_one, near_two, *far_two)
        near_one, far_one, near_two = gather_shard(near_one), gather_shard(far_one), gather_shard(near_two)
        far_two = [gather_shard(f) for f in far_two]
        near_one = tie(near_one, *ready)
        gains = near_one.reshape(sizes[0], -1, FLAT)[:, -16:-12, : 2 * LANES]
        gains = gains.transpose(1, 0, 2).reshape(4, features).astype(jnp.float32)
        quarter, columns = rows_owned // 4 * 2, sizes[0] * LANES
        shapes = (
            (quarter, 3 * columns),
            rows_owned,
            (quarter, 2 * sizes[0] * masters_one[8].shape[0]),
            masters_one[8].shape[0],
        )
        first, second = Tuned(shapes, sizes, place), Tuned(shapes, sizes, place)
        near, wide, down = ways_one = first_ways(first, near_one, far_one, place)
        first.near_way, first.wide_way, first.down_way = ways_one
        ways = second_ways(second, near_two, far_two, wide, down, place)
        second.near_way, second.wide_way, second.down_way = ways
        first.after_attention = lambda value: tie(value, near_two, wide.one, wide.two, down.one, down.two)
        first.before_wide = lambda value: tie(value, far_two[0])
        first.after_wide = lambda value: tie(value, far_two[1], ways[0].one, ways[0].two)
        first.at_end = lambda value: tie(value, ways[0].three)
        second.after_attention = lambda value: tie(value, ways[1].one, ways[1].two)
    else:
        gains = lax.all_gather(gain_rows, ("shard", "seq"), axis=1, tiled=True).astype(jnp.float32)
        first, second = (Plain(gather_plain(m, sizes, core)) for m in (masters_one, masters_two))
    middle_one, first_kept, saved_one, weights_one = layer_ahead(
        flat, (gains[0:1], gains[1:2]), first, None, tables, place
    )
    final, _, saved_two, weights_two = layer_ahead(
        middle_one, (gains[2:3], gains[3:4]), second, first_kept, tables, place
    )
    outputs = final.astype(jnp.bfloat16).reshape(batch, rows, features)
    upstream = cotangent.reshape(rows, features).astype(jnp.float32)
    hooks_two, hooks_one = Hooks(), Hooks()
    if tuned:
        two, one = TunedSender(sizes, place, (1, 2), (2, 1)), TunedSender(sizes, place, (1, 2), (2, 1))

        def at(*steps):
            def hook(value):
                for step in steps:
                    done = step(value)
                    value = tie(value, *(done if isinstance(done, tuple) else (done,)))
                return value

            return hook

        hooks_two.before_attention = at(two.proj_way)
        hooks_two.before_qkv = at(two.half("way_wide"), two.half("way_proj", 1))
        hooks_one.start = at(two.down_way)
        hooks_one.after_down = at(two.scatter_wide)
        hooks_one.before_wide = at(two.half("way_qkv"))
        hooks_one.after_wide = at(
            lambda value: two.wide_sum, two.half("way_down", 1), two.scatter_near, two.got("way_down")
        )
        hooks_one.before_attention = at(one.proj_way, one.half("way_wide"), one.down_way)
        hooks_one.before_qkv = at(
            lambda value: two.near_sum,
            two.share_far,
            one.half("way_proj", 1),
            one.scatter_wide,
            one.half("way_down", 1),
        )
        hooks_one.after_qkv = at(two.far_got, one.got("way_down"))
        hooks_one.before_norm = at(one.half("way_qkv"))
    else:
        two, one = PlainSender(sizes, core), PlainSender(sizes, core)
    grad_middle, gains_two, extra = layer_back(
        upstream, (gains[2:3], gains[3:4]), weights_two, saved_two, None, tables, place, two, hooks_two
    )
    grad_flat, gains_one, _ = layer_back(
        grad_middle, (gains[0:1], gains[1:2]), weights_one, saved_one, extra, tables, place, one, hooks_one
    )
    gain_grads = jnp.stack([*gains_one, *gains_two])
    if tuned:
        gain_total = sum_over(gain_grads, ("shard", "seq", "rep"))
        value = at(one.got("way_qkv"), one.got("way_proj"), one.share_far, one.scatter_near)(tie(grad_flat, outputs))
        at(two.pick_far, two.finish_far, two.share_near)(value)
        one.pick_far(value, two.far[0])
        two.pick_near(value, two.far[0])
        at(one.finish_far, two.finish_near, one.share_near)(value)
        one.pick_near(value, two.near[0], one.far[0], gain_total)
        one.finish_near(value)
        near_two, far_two, near_one, far_one = two.near, two.far, one.near, one.far
    else:
        gain_total = sum_over(gain_grads, ("shard", "seq", "rep"))
        near_two, far_two, near_one, far_one = two.near(), two.far(), one.near(), one.far()
    grad_input = grad_flat.reshape(batch, rows, features)
    block = features // (sizes[0] * sizes[1])
    mine = lax.axis_index("shard") * sizes[1] + core
    own = lax.dynamic_slice_in_dim(gain_total, mine * block, block, 1)

    def ordered(gain_attn, gain_ffn, near, far):
        (query, key, value, proj), (gate, upward, down) = near, far
        return (gain_attn, query, key, value, proj, gain_ffn, gate, upward, down)

    return (
        (outputs, grad_input)
        + ordered(own[0], own[1], near_one, far_one)
        + ordered(own[2], own[3], near_two, far_two)
    )


def solution(mesh):
    tokens = P(("rep", "shard"), "seq", None)
    vector, matrix = P(("shard", "seq")), P(("shard", "seq"), None)
    layer = (vector, matrix, matrix, matrix, matrix, vector, matrix, matrix, matrix)
    return jax.shard_map(
        shards,
        mesh=mesh,
        in_specs=(tokens, P(("rep", "shard"), None), *layer, *layer, tokens),
        out_specs=(tokens, tokens, *layer, *layer),
        check_vma=False,
    )
```
